256 devices in a mesh: az: 32 (over z, y_hi, core), dr: 8 (over x, y_lo).
Axes of the slice: x: 4, y: 4 (y_hi: 2, y_lo: 2; y = y_hi * 2 + y_lo), z: 8, core: 2. Of those that a mesh axis runs over, the one named last changes fastest.
Arguments:
- stack: bfloat16 [2, 32, 768, 4096], P(None, 'dr', 'az'), may hold values from -6 to 6
- range_filter: float32 [32, 4096], P('dr'), may hold values from 0.2 to 1.5
- scatter_mask: int32 [768, 4096], P('az'), may hold values 0 or 1
Outputs:
- phase_vector: float32 [2, 32, 192, 1024], P(None, None, 'az', 'dr')
The draws below stay inside these ranges and needn't reach their ends.
All inputs are finite; a program needn't handle non-finite values. No bound on the sum of `scatter_mask` on one device may be relied on, other than what follows from the above.
Results may differ from the reference program's by a relative error of at most 0.0037.
Values may be sent and summed in bfloat16 or wider, within the bound.
No kernel may reach another device: no remote copies, remote signals or barrier semaphores. Data moves between devices by JAX's collectives and lax.ppermute only.
A program may use at most 64 MiB of HBM per device.

```python
import jax
import jax.numpy as jnp
from jax import lax

DATES = 32
RG = 4096
ITERS = 4
AZ = 768


def set_ends(drawn, rng, smallest, top_value):
    longest = drawn.shape.index(max(drawn.shape))
    spots = []
    for shift in (0, 1):
        where = [jax.random.randint(jax.random.fold_in(rng, axis), (), 0, length) for axis, length in enumerate(drawn.shape)]
        where[longest] = (where[longest] + shift) % drawn.shape[longest]
        spots.append(tuple(where))
    return drawn.at[spots[0]].set(smallest).at[spots[1]].set(top_value)


def level_of(own_key, dims, pieces, least, top_value):
    level, own = 1.0, jax.random.fold_in(own_key, 6)
    for dim, shards_of in pieces:
        draws = jnp.exp(jax.random.uniform(jax.random.fold_in(own, dim), (shards_of,), jnp.float32, least / len(pieces), top_value / len(pieces)))
        level = level * jnp.repeat(draws, dims[dim] // shards_of).reshape([-1 if axis == dim else 1 for axis in range(len(dims))])
    return level


def centred(own_key, extent, deviation, limit, cuts=(), held_as=jnp.bfloat16):
    array = jax.random.normal(own_key, extent, jnp.float32) * deviation
    if len(cuts) > 0:
        array = level_of(own_key, extent, cuts, -0.22, 0.18) * array
    return jnp.clip(array, min=-limit, max=limit).astype(held_as)


def setup_inputs(seed: int = 0) -> dict:
    key_list = jax.random.split(jax.random.key(seed), 4)
    return {
        "stack": centred(key_list[0], (2, DATES, AZ, RG), 1.0, 6.0, ((1, 8), (2, 32))),
        "range_filter": jnp.clip(0.2 + 1.3 * jax.random.uniform(key_list[1], (DATES, RG), jnp.float32) ** level_of(key_list[1], (DATES, RG), ((0, 8),), -0.2, 0.2), 0.2, 1.5),
        "scatter_mask": set_ends((jax.random.randint(key_list[2], (AZ, RG), 0, 4) < 3).astype(jnp.int32), jax.random.fold_in(key_list[2], 1), 0, 1),
    }


BETA_LOAD = 1.0
PROJ_LOAD = 1.0

def link_phases(cov_real, cov_imag):
    diagonal = jnp.moveaxis(jnp.diagonal(cov_real, axis1=0, axis2=1), -1, 0)
    scales = jnp.sqrt(diagonal + BETA_LOAD)
    product = scales[:, None] * scales[None, :]
    coh_real = cov_real / product
    coh_imag = cov_imag / product
    vec_real = jnp.ones(diagonal.shape, jnp.float32)
    vec_imag = jnp.zeros(diagonal.shape, jnp.float32)
    for repeat in range(ITERS):
        new_real = lax.optimization_barrier(jnp.sum(coh_real * vec_real[None] - coh_imag * vec_imag[None], axis=1))
        new_imag = lax.optimization_barrier(jnp.sum(coh_real * vec_imag[None] + coh_imag * vec_real[None], axis=1))
        length = jnp.sqrt(new_real * new_real + new_imag * new_imag + PROJ_LOAD)
        vec_real = new_real / length
        vec_imag = new_imag / length
    return jnp.stack([vec_real, vec_imag])

def reference(stack, range_filter, scatter_mask):

    def filter_date(position):
        date_stack = lax.dynamic_index_in_dim(stack, position, 1, keepdims=False)
        gains = lax.dynamic_index_in_dim(range_filter, position, 0, keepdims=False)
        field = date_stack[0].astype(jnp.float32) + 1j * date_stack[1].astype(jnp.float32)
        spectrum = jnp.fft.fft(field, axis=-1) * gains[None, :]
        result = jnp.fft.ifft(spectrum, axis=-1)
        return jnp.stack([jnp.real(result).astype(jnp.bfloat16), jnp.imag(result).astype(jnp.bfloat16)])
    filtered = lax.map(filter_date, jnp.arange(DATES, dtype=jnp.int32))
    filtered = jnp.moveaxis(filtered, 0, 1).reshape(2 * DATES, AZ, RG)
    padded = jnp.pad(filtered, ((0, 0), (6, 6), (6, 6)))
    weight = jnp.pad(scatter_mask, 6).astype(jnp.bfloat16)
    masked = padded * weight[None]
    block_cols = RG // 4 + 3
    windows = RG // 4

    def advance(previous, row_index):
        start = row_index * 4
        plain_rows = lax.dynamic_slice_in_dim(padded, start, 4, 1).astype(jnp.float32).reshape(2 * DATES, 4, block_cols, 4)
        masked_rows = lax.dynamic_slice_in_dim(masked, start, 4, 1).astype(jnp.float32).reshape(2 * DATES, 4, block_cols, 4)
        gram_matrix = jnp.einsum('ajbk,cjbk->acb', masked_rows, plain_rows, precision=lax.Precision.HIGHEST)
        current = jnp.stack([gram_matrix[:DATES, :DATES] + gram_matrix[DATES:, DATES:], gram_matrix[DATES:, :DATES] - gram_matrix[:DATES, DATES:]])
        row_sum = previous[0] + previous[1] + previous[2] + current
        window_sum = row_sum[..., 0:windows] + row_sum[..., 1:windows + 1] + row_sum[..., 2:windows + 2] + row_sum[..., 3:windows + 3]
        phases = link_phases(window_sum[0], window_sum[1])
        return (jnp.concatenate([previous[1:], current[None]], axis=0), phases)
    initial = jnp.zeros((3, 2, DATES, DATES, block_cols), jnp.float32)
    unused, outputs = lax.scan(advance, initial, jnp.arange(AZ // 4 + 3, dtype=jnp.int32))
    return jnp.transpose(outputs[3:], (1, 2, 0, 3))
```

```python
import math

import jax
import jax.numpy as jnp
import numpy as np
from jax import lax
from jax.experimental import pallas as pl
from jax.experimental.pallas import tpu as pltpu
from jax.sharding import PartitionSpec as P

ITERS = 4
BETA_LOAD = 1.0
PROJ_LOAD = 1.0

DATES = 32
LINES = 24
RG = 4096
TILES = 8
HALO = 6
PLANES = 32
HERE = 4
ROWS = HERE * LINES
SLOTS = LINES + 1
TAIL_SLOT = 18
COMBOS = 80
OFFSETS = (0, 32, 56, 72)


def slot_of(line):
    if line < 6:
        return 12 + line
    return line - 6 if line < 18 else line + 1


def split_np(table):
    high = table.astype(jnp.bfloat16)
    low = (table - high.astype(np.float64)).astype(jnp.bfloat16)
    return np.stack([high, low])


def tables():
    turn = 2.0 * np.pi / 128 * (np.outer(np.arange(128), np.arange(128)) % 128)
    cos, sin = np.cos(turn), np.sin(turn)
    forward = split_np(np.block([[cos, -sin], [sin, cos]]))
    inverse = split_np(np.block([[cos, sin], [-sin, cos]]) / RG)
    angle = 2.0 * np.pi / RG * np.outer(np.arange(PLANES), np.arange(128))
    twist = np.stack([np.cos(angle), np.sin(angle)]).astype(np.float32)
    place = np.zeros((640, 512), np.float32)
    for phase in range(4):
        for block in range(128):
            place[122 + 4 * block + phase, phase * 128 + block] = 1.0
    return forward, inverse, twist, place.astype(jnp.bfloat16)


def tail_band():
    band = np.zeros((6, 128, 128), np.float32)
    for row in range(6):
        for line in range(4 * row, 4 * row + 16):
            for block in range(3):
                band[row, line * 3 + block, 125 + block :] = 1.0
    return band.astype(jnp.bfloat16)


def cmul(value, cos, sin):
    re, im = value
    if abs(sin) < 1e-12:
        return (re, im) if cos > 0 else (-re, -im)
    if abs(cos) < 1e-12:
        return (-im, re) if sin > 0 else (im, -re)
    if abs(abs(cos) - abs(sin)) < 1e-12:
        size = abs(cos)
        if cos > 0 and sin > 0:
            return ((re - im) * size, (re + im) * size)
        if cos > 0:
            return ((re + im) * size, (im - re) * size)
        if sin > 0:
            return ((-re - im) * size, (re - im) * size)
        return ((im - re) * size, (-re - im) * size)
    return (re * cos - im * sin, im * cos + re * sin)


def small_dft(values, sign):
    count = len(values)
    if count == 1:
        return values
    even = small_dft(values[0::2], sign)
    odd = small_dft(values[1::2], sign)
    half = count // 2
    low, high = [], []
    for k in range(half):
        angle = sign * 2.0 * math.pi * k / count
        re, im = cmul(odd[k], math.cos(angle), math.sin(angle))
        low.append((even[k][0] + re, even[k][1] + im))
        high.append((even[k][0] - re, even[k][1] - im))
    return low + high


def dft_planes(load, hold, store, sign):
    for m in range(8):
        parts = small_dft([load(8 * i + m) for i in range(4)], sign)
        for s in range(4):
            angle = sign * 2.0 * math.pi * m * s / 32
            re, im = cmul(parts[s], math.cos(angle), math.sin(angle))
            hold[0, s * 8 + m] = re
            hold[1, s * 8 + m] = im
    for s in range(4):
        parts = small_dft([(hold[0, s * 8 + m], hold[1, s * 8 + m]) for m in range(8)], sign)
        for u in range(8):
            store(s + 4 * u, *parts[u])


def split(values):
    high = values.astype(jnp.bfloat16)
    return high, (values - high.astype(jnp.float32)).astype(jnp.bfloat16)


def dot3(values, table):
    high, low = split(values)
    dot = lambda left, right: jnp.dot(left, right, preferred_element_type=jnp.float32)
    return dot(high, table[0]) + (dot(high, table[1]) + dot(low, table[0]))


def filter_kernel(
    stack, gain, mask, forward, inverse, twist, place, out, first, spec, hold, lines_out
):
    for c in range(2):
        for d in range(HERE):
            for n in range(PLANES):
                first[c, n, d * LINES : (d + 1) * LINES] = stack[
                    c, d, :, n * 128 : (n + 1) * 128
                ].astype(jnp.float32)

    def ahead(block, carry):
        rows = pl.ds(pl.multiple_of(block * 8, 8), 8)

        def store(q, re, im):
            spec[0, q, rows] = re
            spec[1, q, rows] = im

        dft_planes(lambda n: (first[0, n, rows], first[1, n, rows]), hold, store, -1)
        return carry

    lax.fori_loop(0, ROWS // 8, ahead, 0)

    def middle(step, carry):
        group = 4
        parts, turns = [], []
        for i in range(group):
            q = step * group + i
            tc = twist[0, pl.ds(q, 1), :]
            ts = twist[1, pl.ds(q, 1), :]
            turns.append((tc, ts))
            re, im = spec[0, q], spec[1, q]
            parts.append(jnp.concatenate([re * tc + im * ts, im * tc - re * ts], axis=1))
        found = dot3(jnp.concatenate(parts, axis=0), forward)
        scaled = []
        for i in range(group):
            q = step * group + i
            for d in range(HERE):
                row = gain[q, pl.ds(d, 1), :]
                begin = i * ROWS + d * LINES
                scaled.append(
                    found[begin : begin + LINES] * jnp.concatenate([row, row], axis=1)
                )
        back = dot3(jnp.concatenate(scaled, axis=0), inverse)
        for i in range(group):
            q = step * group + i
            tc, ts = turns[i]
            re = back[i * ROWS : (i + 1) * ROWS, :128]
            im = back[i * ROWS : (i + 1) * ROWS, 128:]
            spec[0, q] = re * tc - im * ts
            spec[1, q] = im * tc + re * ts
        return carry

    lax.fori_loop(0, PLANES // 4, middle, 0)

    def behind(block, carry):
        rows = pl.ds(pl.multiple_of(block * 8, 8), 8)
        to_re = pl.ds(pl.multiple_of(block * 8, 8), 8)
        to_im = pl.ds(pl.multiple_of(block * 8 + ROWS, 8), 8)
        lines = pl.ds(pl.multiple_of(lax.rem(block, 3) * 8, 8), 8)

        def store(n, re, im):
            weight = mask[lines, n * 128 : (n + 1) * 128].astype(jnp.float32)
            lines_out[n + 1, to_re] = re * weight
            lines_out[n + 1, to_im] = im * weight

        dft_planes(lambda q: (spec[0, q, rows], spec[1, q, rows]), hold, store, 1)
        return carry

    lax.fori_loop(0, ROWS // 8, behind, 0)
    blank = jnp.zeros((2 * ROWS, 128), jnp.float32)
    for n in (0, 33, 34, 35, 36):
        lines_out[n] = blank
    lanes = lax.broadcasted_iota(jnp.int32, (8, 128), 1)

    def tile(t, carry):
        left = jnp.concatenate(
            [
                jnp.concatenate(
                    [lines_out[4 * t + v, pl.ds(line, 8, stride=LINES), :] for line in range(LINES)],
                    axis=0,
                )
                for v in range(5)
            ],
            axis=1,
        ).astype(jnp.bfloat16)
        found = jnp.dot(left, place[...], preferred_element_type=jnp.float32)

        @pl.when(t < TILES)
        def _():
            for line in range(LINES):
                out[t, slot_of(line)] = jnp.concatenate(
                    [found[line * 8 : line * 8 + 8, p * 128 : p * 128 + 128] for p in range(4)],
                    axis=0,
                ).astype(jnp.bfloat16)

        @pl.when(t > 0)
        def _():
            tails = []
            for p in range(4):
                tail = jnp.zeros((8, 128), jnp.float32)
                for line in range(LINES):
                    part = found[line * 8 : line * 8 + 8, p * 128 : p * 128 + 128]
                    if line:
                        part = pltpu.roll(part, 3 * line, 1)
                    keep = (lanes >= 3 * line) & (lanes < 3 * line + 3)
                    tail = jnp.where(keep, part, tail)
                tails.append(tail)
            out[t - 1, TAIL_SLOT] = jnp.concatenate(tails, axis=0).astype(jnp.bfloat16)

        return carry

    lax.fori_loop(0, TILES + 1, tile, 0)


def filter_lines(stack, gains, mask):
    forward, inverse, twist, place = tables()
    gain = jnp.transpose(gains.reshape(HERE, 128, PLANES), (2, 0, 1))
    return pl.pallas_call(
        filter_kernel,
        out_shape=jax.ShapeDtypeStruct((TILES, SLOTS, 32, 128), jnp.bfloat16),
        scratch_shapes=[
            pltpu.VMEM((2, PLANES, ROWS, 128), jnp.float32),
            pltpu.VMEM((2, PLANES, ROWS, 128), jnp.float32),
            pltpu.VMEM((2, PLANES, 8, 128), jnp.float32),
            pltpu.VMEM((37, 2 * ROWS, 128), jnp.float32),
        ],
        name="filter_lines",
    )(stack, gain, mask, forward, inverse, twist, place)


def combo_of(date, group):
    own = date // 8
    return OFFSETS[own] + (date % 8) * (4 - own) + group - own


def fold_rows(parts, low, pair, even):
    half = [
        jnp.where(low, parts[d], parts[d + 4])
        + pltpu.roll(jnp.where(low, parts[d + 4], parts[d]), 4, 0)
        for d in range(4)
    ]
    quarter = [
        jnp.where(
            pair,
            half[d] + pltpu.roll(half[d], 6, 0),
            half[d + 2] + pltpu.roll(half[d + 2], 2, 0),
        )
        for d in range(2)
    ]
    return jnp.where(
        even,
        quarter[0] + pltpu.roll(quarter[0], 7, 0),
        quarter[1] + pltpu.roll(quarter[1], 1, 0),
    )


def link_kernel(own, above, below, band, out, z_re, z_im, z_sum, z_dif, sums, tails, cov, vec):
    rows = lax.broadcasted_iota(jnp.int32, (8, 128), 0)
    lanes = lax.broadcasted_iota(jnp.int32, (8, 128), 1)
    low = rows < 4

    def put(plane, group, first, second):
        re = jnp.where(low, first, pltpu.roll(second, 4, 0))
        im = jnp.where(low, pltpu.roll(first, 4, 0), second)
        z_re[plane, group] = re
        z_im[plane, group] = im
        z_sum[plane, group] = re + im
        z_dif[plane, group] = im - re

    def unpack(ref, slot, line):
        for group in range(4):
            first = ref[2 * group, slot].astype(jnp.float32)
            second = ref[2 * group + 1, slot].astype(jnp.float32)
            for p in range(4):
                put(line * 4 + p, group, first[8 * p : 8 * p + 8], second[8 * p : 8 * p + 8])

    def unpack_run(ref, slot, line, count):
        def step(i, carry):
            unpack(ref, slot + i, line + i)
            return carry

        lax.fori_loop(0, count, step, 0)

    unpack_run(above, 1, 0, 6)
    unpack_run(own, 12, 6, 6)
    unpack_run(own, 0, 12, 12)
    unpack_run(own, 19, 24, 6)
    unpack_run(below, 0, 30, 6)
    for group in range(4):
        pieces = []
        for source in (2 * group, 2 * group + 1):
            mid = own[source, TAIL_SLOT].astype(jnp.float32)
            up = above[source, 0].astype(jnp.float32)
            down = below[source, 6].astype(jnp.float32)
            piece = []
            for p in range(4):
                cut = slice(8 * p, 8 * p + 8)
                value = pltpu.roll(mid[cut], 18, 1)
                value = jnp.where(lanes < 18, pltpu.roll(up[cut], 128 - 54, 1), value)
                value = jnp.where(
                    (lanes >= 90) & (lanes < 108), pltpu.roll(down[cut], 90, 1), value
                )
                piece.append(value)
            pieces.append(piece)
        for p in range(4):
            put(144 + p, group, pieces[0][p], pieces[1][p])

    def gram(base, count, own_group, first_row, groups):
        width = len(groups)
        totals = [[None] * 3 for _ in range(4 * width)]
        for step in range(count):
            plane = base + step
            others = [(z_re[plane, g], z_sum[plane, g], z_dif[plane, g]) for g in groups]
            for i in range(4):
                row = pl.ds(first_row + i, 8, stride=0)
                mine = (
                    z_sum[plane, own_group, row, :],
                    z_re[plane, own_group, row, :],
                    z_im[plane, own_group, row, :],
                )
                for j in range(width):
                    total = totals[i * width + j]
                    for k in range(3):
                        term = others[j][k] * mine[k]
                        total[k] = term if total[k] is None else total[k] + term
        return [(one + three, one - two) for one, two, three in totals]

    for own_group in range(4):
        left = list(range(own_group, 4))
        while left:
            groups, left = left[:2], left[2:]
            width = len(groups)

            def half(h, carry, own_group=own_group, groups=groups, width=width):
                first_row = h * 4

                def one_row(r, carry):
                    found = gram(r * 16, 16, own_group, first_row, groups)
                    for i in range(4 * width):
                        sums[r, i, 0] = found[i][0]
                        sums[r, i, 1] = found[i][1]
                    return carry

                lax.fori_loop(0, 9, one_row, 0)
                found = gram(144, 4, own_group, first_row, groups)
                for i in range(4):
                    for j in range(width):
                        combo = (
                            OFFSETS[own_group]
                            + (first_row + i) * (4 - own_group)
                            + groups[j]
                            - own_group
                        )
                        spot = pl.ds(pl.multiple_of(combo * 8, 8), 8)
                        for c in range(2):
                            tails[c, spot] = found[i * width + j][c]
                            rowsum = [sums[r, i * width + j, c] for r in range(9)]
                            pairs = [rowsum[r] + rowsum[r + 1] for r in range(8)]
                            for a in range(6):
                                value = pairs[a] + pairs[a + 2]
                                value = value + jnp.where(
                                    lanes < 127, pltpu.roll(value, 127, 1), 0.0
                                )
                                value = value + jnp.where(
                                    lanes < 126, pltpu.roll(value, 126, 1), 0.0
                                )
                                cov[a, c, spot] = value
                return carry

            lax.fori_loop(0, 2, half, 0)

    pair = lax.rem(rows, 4) < 2
    even = lax.rem(rows, 2) == 0

    def window_row(a, carry):
        for c in range(2):
            high, lo = split(tails[c])
            cov[a, c] += jnp.dot(
                high, band[a], preferred_element_type=jnp.float32
            ) + jnp.dot(lo, band[a], preferred_element_type=jnp.float32)
        inverse = []
        for g in range(4):
            power = jnp.zeros((8, 128), jnp.float32)
            for i in range(8):
                combo = combo_of(8 * g + i, g)
                power = jnp.where(rows == i, cov[a, 0, combo * 8 : combo * 8 + 8], power)
            inverse.append(1.0 / jnp.sqrt(power + BETA_LOAD))
        for g in range(4):
            vec[0, g] = inverse[g]
            vec[1, g] = jnp.zeros((8, 128), jnp.float32)
            vec[2, g] = inverse[g]

        def iterate(step, carry):
            have_re = [vec[0, g] for g in range(4)]
            have_im = [vec[1, g] for g in range(4)]
            new_re = [jnp.zeros((8, 128), jnp.float32)] * 4
            new_im = [jnp.zeros((8, 128), jnp.float32)] * 4
            for own_group in range(4):
                parts_re, parts_im = [], []
                for i in range(8):
                    row = pl.ds(i, 8, stride=0)
                    mine_re = vec[0, own_group, row, :]
                    mine_im = vec[1, own_group, row, :]
                    part_re = part_im = None
                    for g in range(own_group, 4):
                        combo = combo_of(8 * own_group + i, g)
                        cov_re = cov[a, 0, combo * 8 : combo * 8 + 8]
                        cov_im = cov[a, 1, combo * 8 : combo * 8 + 8]
                        new_re[g] = new_re[g] + (cov_re * mine_re + cov_im * mine_im)
                        new_im[g] = new_im[g] + (cov_re * mine_im - cov_im * mine_re)
                        if g > own_group:
                            term_re = cov_re * have_re[g] - cov_im * have_im[g]
                            term_im = cov_re * have_im[g] + cov_im * have_re[g]
                            part_re = term_re if part_re is None else part_re + term_re
                            part_im = term_im if part_im is None else part_im + term_im
                    parts_re.append(part_re)
                    parts_im.append(part_im)
                if own_group < 3:
                    new_re[own_group] = new_re[own_group] + fold_rows(parts_re, low, pair, even)
                    new_im[own_group] = new_im[own_group] + fold_rows(parts_im, low, pair, even)
            for g in range(4):
                weight = vec[2, g]
                u_re = new_re[g] * weight
                u_im = new_im[g] * weight
                length = 1.0 / jnp.sqrt(u_re * u_re + u_im * u_im + PROJ_LOAD)
                x_re = u_re * length
                x_im = u_im * length
                vec[3, g] = x_re
                vec[4, g] = x_im
                vec[0, g] = x_re * weight
                vec[1, g] = x_im * weight
            return carry

        lax.fori_loop(0, ITERS, iterate, 0)
        for g in range(4):
            for i in range(8):
                for c in range(2):
                    out[c, 8 * g + i, pl.ds(a, 1), :] = vec[3 + c, g, i : i + 1, :]
        return carry

    lax.fori_loop(0, 6, window_row, 0)


def link_windows(own, above, below):
    field = pltpu.VMEM((148, 4, 8, 128), jnp.float32)
    return pl.pallas_call(
        link_kernel,
        out_shape=jax.ShapeDtypeStruct((2, DATES, 6, 128), jnp.float32),
        scratch_shapes=[
            field,
            field,
            field,
            field,
            pltpu.VMEM((9, 8, 2, 8, 128), jnp.float32),
            pltpu.VMEM((2, COMBOS * 8, 128), jnp.float32),
            pltpu.VMEM((6, 2, COMBOS * 8, 128), jnp.float32),
            pltpu.VMEM((5, 4, 8, 128), jnp.float32),
        ],
        name="link_windows",
    )(own, above, below, tail_band())


def on_device(stack, range_filter, scatter_mask):
    tiles = filter_lines(stack, range_filter, scatter_mask)
    own = lax.all_to_all(tiles, "dr", split_axis=0, concat_axis=0, tiled=True)
    count = lax.axis_size("az")
    down = [(i, i + 1) for i in range(count - 1)]
    up = [(i + 1, i) for i in range(count - 1)]
    above = lax.ppermute(own[:, 18:25], "az", down)
    below = lax.ppermute(own[:, 12:19], "az", up)
    return link_windows(own, above, below)


def solution(mesh):
    in_specs = (P(None, "dr", "az", None), P("dr", None), P("az", None))
    out_specs = P(None, None, "az", "dr")
    return jax.shard_map(
        on_device, mesh=mesh, in_specs=in_specs, out_specs=out_specs, check_vma=False
    )
```

```python
import math

import jax
import jax.numpy as jnp
import numpy as np
from jax import lax
from jax.experimental import pallas as pl
from jax.experimental.pallas import tpu as pltpu
from jax.sharding import PartitionSpec as P

ITERS = 4
BETA_LOAD = 1.0
PROJ_LOAD = 1.0

DATES = 32
LINES = 24
RG = 4096
TILES = 8
HALO = 6
PLANES = 32
HERE = 4
ROWS = HERE * LINES
SLOTS = LINES + 1
TAIL_SLOT = 18
SHIFTS = 17
PAIRS = SHIFTS * DATES
WRAP = 48


def slot_of(line):
    if line < 6:
        return 12 + line
    return line - 6 if line < 18 else line + 1


def split_np(table):
    high = table.astype(jnp.bfloat16)
    low = (table - high.astype(np.float64)).astype(jnp.bfloat16)
    return np.concatenate([high, high, low], axis=0)


def tables():
    lane = np.arange(128)
    freq = 4 * (lane % 32) + lane // 32
    turn = 2.0 * np.pi / 128 * (np.outer(lane, freq) % 128)
    forward = split_np(np.block([[np.cos(turn), -np.sin(turn)], [np.sin(turn), np.cos(turn)]]))
    turn = 2.0 * np.pi / 128 * (np.outer(freq, lane - HALO) % 128)
    inverse = split_np(
        np.block([[np.cos(turn), np.sin(turn)], [-np.sin(turn), np.cos(turn)]]) / RG
    )
    plane = np.arange(PLANES)
    angle = 2.0 * np.pi / RG * np.outer(plane, lane)
    back = 2.0 * np.pi / RG * np.outer(plane, lane - HALO)
    twist = np.stack([np.cos(angle), np.sin(angle), np.cos(back), np.sin(back)])
    place = np.zeros((512, 512), np.float32)
    for phase in range(4):
        for block in range(128):
            place[4 * block + phase, phase * 128 + block] = 1.0
    return forward, inverse, twist.astype(np.float32), place.astype(jnp.bfloat16)


def tail_band():
    band = np.zeros((6, 128, 128), np.float32)
    for row in range(6):
        for line in range(4 * row, 4 * row + 16):
            for block in range(3):
                band[row, line * 3 + block, 125 + block :] = 1.0
    return band.astype(jnp.bfloat16)


def cmul(value, cos, sin):
    re, im = value
    if abs(sin) < 1e-12:
        return (re, im) if cos > 0 else (-re, -im)
    if abs(cos) < 1e-12:
        return (-im, re) if sin > 0 else (im, -re)
    if abs(abs(cos) - abs(sin)) < 1e-12:
        size = abs(cos)
        if cos > 0 and sin > 0:
            return ((re - im) * size, (re + im) * size)
        if cos > 0:
            return ((re + im) * size, (im - re) * size)
        if sin > 0:
            return ((-re - im) * size, (re - im) * size)
        return ((im - re) * size, (-re - im) * size)
    return (re * cos - im * sin, im * cos + re * sin)


def small_dft(values, sign):
    count = len(values)
    if count == 1:
        return values
    even = small_dft(values[0::2], sign)
    odd = small_dft(values[1::2], sign)
    half = count // 2
    low, high = [], []
    for k in range(half):
        angle = sign * 2.0 * math.pi * k / count
        re, im = cmul(odd[k], math.cos(angle), math.sin(angle))
        low.append((even[k][0] + re, even[k][1] + im))
        high.append((even[k][0] - re, even[k][1] - im))
    return low + high


def dft_planes(load, hold, store, sign):
    for m in range(8):
        parts = small_dft([load(8 * i + m) for i in range(4)], sign)
        for s in range(4):
            angle = sign * 2.0 * math.pi * m * s / 32
            re, im = cmul(parts[s], math.cos(angle), math.sin(angle))
            hold[0, s * 8 + m] = re
            hold[1, s * 8 + m] = im
    for s in range(4):
        parts = small_dft([(hold[0, s * 8 + m], hold[1, s * 8 + m]) for m in range(8)], sign)
        for u in range(8):
            store(s + 4 * u, *parts[u])


def split(values):
    high = values.astype(jnp.bfloat16)
    return high, (values - high.astype(jnp.float32)).astype(jnp.bfloat16)


def dot3(values, table):
    high, low = split(values)
    return jnp.dot(
        jnp.concatenate([high, low, high], axis=1), table, preferred_element_type=jnp.float32
    )


GROUP = 4


def filter_kernel(
    stack, gains, mask, forward, inverse, twist, place, out,
    first, spec, hold, held, gain, weights, lines_out,
):
    lanes = lax.broadcasted_iota(jnp.int32, (8, 128), 1)
    for c in range(2):
        for d in range(HERE):
            for n in range(PLANES):
                first[c, n, d * LINES : (d + 1) * LINES] = stack[
                    c, d, :, n * 128 : (n + 1) * 128
                ].astype(jnp.float32)
    for n in range(PLANES):
        four = gains[:, n * 128 : (n + 1) * 128]
        for d in range(HERE):
            gain[d, n : n + 1] = four[d : d + 1]
    for d in range(HERE):
        turned = jnp.transpose(gain[d])
        gain[d] = jnp.concatenate([turned[32 * w : 32 * w + 32] for w in range(4)], axis=1)
    for block in range(LINES // 8):
        rows = slice(8 * block, 8 * block + 8)
        before = pltpu.roll(mask[rows, RG - 128 :].astype(jnp.float32), HALO, 1)
        for n in range(PLANES):
            now = pltpu.roll(mask[rows, n * 128 : (n + 1) * 128].astype(jnp.float32), HALO, 1)
            joined = jnp.where(lanes < HALO, before, now)
            if n == 0:
                weights[PLANES, rows] = jnp.where(lanes < HALO, joined, 0.0)
                joined = jnp.where(lanes < HALO, 0.0, joined)
            weights[n, rows] = joined
            before = now

    def ahead(block, carry):
        rows = pl.ds(pl.multiple_of(block * 8, 8), 8)

        def store(q, re, im):
            spec[0, q, rows] = re
            spec[1, q, rows] = im

        dft_planes(lambda n: (first[0, n, rows], first[1, n, rows]), hold, store, -1)
        return carry

    lax.fori_loop(0, ROWS // 8, ahead, 0)
    steps = PLANES // GROUP

    def middle(step, carry):
        now = jnp.minimum(step, steps - 1) * GROUP
        past = jnp.maximum(step - 1, 0) * GROUP
        parts = []
        for i in range(GROUP):
            tc = twist[0, pl.ds(now + i, 1), :]
            ts = twist[1, pl.ds(now + i, 1), :]
            re, im = spec[0, now + i], spec[1, now + i]
            parts.append(jnp.concatenate([re * tc + im * ts, im * tc - re * ts], axis=1))
        back = dot3(held[lax.rem(step + 1, 2)], inverse[...])
        found = dot3(jnp.concatenate(parts, axis=0), forward[...])
        for i in range(GROUP):
            for d in range(HERE):
                row = gain[d, pl.ds(now + i, 1), :]
                begin = i * ROWS + d * LINES
                held[lax.rem(step, 2), begin : begin + LINES] = found[
                    begin : begin + LINES
                ] * jnp.concatenate([row, row], axis=1)
        for i in range(GROUP):
            tc = twist[2, pl.ds(past + i, 1), :]
            ts = twist[3, pl.ds(past + i, 1), :]
            re = back[i * ROWS : (i + 1) * ROWS, :128]
            im = back[i * ROWS : (i + 1) * ROWS, 128:]
            first[0, past + i] = re * tc - im * ts
            first[1, past + i] = im * tc + re * ts
        return carry

    lax.fori_loop(0, steps + 1, middle, 0)

    def behind(block, carry):
        rows = pl.ds(pl.multiple_of(block * 8, 8), 8)
        to_im = pl.ds(pl.multiple_of(block * 8 + ROWS, 8), 8)
        lines = pl.ds(pl.multiple_of(lax.rem(block, 3) * 8, 8), 8)

        def store(n, re, im):
            weight = weights[n, lines]
            lines_out[n, rows] = re * weight
            lines_out[n, to_im] = im * weight
            if n == 0:
                weight = weights[PLANES, lines]
                lines_out[PLANES, rows] = re * weight
                lines_out[PLANES, to_im] = im * weight

        dft_planes(lambda q: (first[0, q, rows], first[1, q, rows]), hold, store, 1)
        return carry

    lax.fori_loop(0, ROWS // 8, behind, 0)

    def gather(plane):
        return jnp.concatenate(
            [lines_out[plane, pl.ds(line, 8, stride=LINES), :] for line in range(LINES)], axis=0
        )

    def put_tail(slot, found):
        tails = []
        for p in range(4):
            tail = jnp.zeros((8, 128), jnp.float32)
            for line in range(LINES):
                part = found[line * 8 : line * 8 + 8, p * 128 : p * 128 + 128]
                if line:
                    part = pltpu.roll(part, 3 * line, 1)
                tail = jnp.where(lanes >= 3 * line, part, tail)
            tails.append(jnp.where(lanes < 3 * LINES, tail, 0.0))
        out[slot, TAIL_SLOT] = jnp.concatenate(tails, axis=0).astype(jnp.bfloat16)

    def tile(t, carry):
        left = jnp.concatenate([gather(4 * t + v) for v in range(4)], axis=1).astype(jnp.bfloat16)
        found = jnp.dot(left, place[...], preferred_element_type=jnp.float32)
        for line in range(LINES):
            out[t, slot_of(line)] = jnp.concatenate(
                [found[line * 8 : line * 8 + 8, p * 128 : p * 128 + 128] for p in range(4)],
                axis=0,
            ).astype(jnp.bfloat16)
        put_tail(lax.rem(t + TILES - 1, TILES), found)
        return carry

    lax.fori_loop(0, TILES, tile, 0)
    found = jnp.dot(
        gather(PLANES).astype(jnp.bfloat16), place[:128], preferred_element_type=jnp.float32
    )
    put_tail(TILES - 1, found)


def filter_lines(stack, gains, mask):
    forward, inverse, twist, place = tables()
    return pl.pallas_call(
        filter_kernel,
        out_shape=jax.ShapeDtypeStruct((TILES, SLOTS, 32, 128), jnp.bfloat16),
        scratch_shapes=[
            pltpu.VMEM((2, PLANES, ROWS, 128), jnp.float32),
            pltpu.VMEM((2, PLANES, ROWS, 128), jnp.float32),
            pltpu.VMEM((2, PLANES, 8, 128), jnp.float32),
            pltpu.VMEM((2, GROUP * ROWS, 256), jnp.float32),
            pltpu.VMEM((HERE, PLANES, 128), jnp.float32),
            pltpu.VMEM((PLANES + 1, LINES, 128), jnp.float32),
            pltpu.VMEM((PLANES + 1, 2 * ROWS, 128), jnp.float32),
        ],
        compiler_params=pltpu.CompilerParams(vmem_limit_bytes=24 << 20),
        cost_estimate=pl.CostEstimate(
            flops=4_000_000_000, bytes_accessed=4_000_000, transcendentals=0
        ),
        name="filter_lines",
    )(stack, gains, mask, forward, inverse, twist, place)


def unpacker(fields):
    z_re, z_im, z_sum, z_dif = fields
    rows = lax.broadcasted_iota(jnp.int32, (8, 128), 0)
    low = rows < 4

    def put(plane, group, first, second):
        re = jnp.where(low, first, pltpu.roll(second, 4, 0))
        im = jnp.where(low, pltpu.roll(first, 4, 0), second)
        total, change = re + im, im - re
        z_im[plane, 8 * group : 8 * group + 8] = im
        for begin in [8 * group] + ([32 + 8 * group] if group < 2 else []):
            z_re[plane, begin : begin + 8] = re
            z_sum[plane, begin : begin + 8] = total
            z_dif[plane, begin : begin + 8] = change

    def run(ref, slot, line, count):
        def step(i, carry):
            for group in range(4):
                first = ref[2 * group, slot + i].astype(jnp.float32)
                second = ref[2 * group + 1, slot + i].astype(jnp.float32)
                for p in range(4):
                    cut = slice(8 * p, 8 * p + 8)
                    put((line + i) * 4 + p, group, first[cut], second[cut])
            return carry

        lax.fori_loop(0, count, step, 0)

    return put, run


WIDTH = 8


def gram(fields, base, count, store):
    z_re, z_im, z_sum, z_dif = fields

    def block(index, carry):
        group = index // 2
        own = pl.ds(pl.multiple_of(group * 8, 8), 8)
        begin = pl.multiple_of(group * 8 + lax.rem(index, 2) * 8, 8)
        totals = [[None] * 3 for _ in range(WIDTH)]
        for step in range(count):
            plane = base + step
            mine = (z_sum[plane, own], z_re[plane, own], z_im[plane, own])
            for i in range(WIDTH):
                other = pl.ds(begin + 1 + i, 8)
                others = (z_re[plane, other], z_sum[plane, other], z_dif[plane, other])
                for k in range(3):
                    term = others[k] * mine[k]
                    totals[i][k] = term if step == 0 else totals[i][k] + term
        for i in range(WIDTH):
            one, two, three = totals[i]
            spot = (lax.rem(index, 2) * 8 + 1 + i) * DATES + group * 8
            spot = pl.ds(pl.multiple_of(spot, 8), 8)
            store(0, spot, one + three)
            store(1, spot, one - two)
        return carry

    lax.fori_loop(0, 8, block, 0)
    for group in range(4):
        own = slice(8 * group, 8 * group + 8)
        total = None
        for step in range(count):
            re, im = z_re[base + step, own], z_im[base + step, own]
            term = re * re + im * im
            total = term if total is None else total + term
        store(0, own, total)


def gram_rows(fields, sums, count, first_plane, first_row):
    def one_row(r, carry):
        def store(c, spot, value):
            sums[first_row + r, c, spot] = value

        gram(fields, first_plane + r * 16, 16, store)
        return carry

    lax.fori_loop(0, count, one_row, 0)


def inner_kernel(own, sums, z_re, z_im, z_sum, z_dif):
    fields = (z_re, z_im, z_sum, z_dif)
    put, run = unpacker(fields)
    run(own, 14, 0, 4)
    run(own, 0, 4, 12)
    run(own, 19, 16, 4)
    gram_rows(fields, sums, 5, 0, 0)


def inner_rows(own):
    field = pltpu.VMEM((80, WRAP, 128), jnp.float32)
    return pl.pallas_call(
        inner_kernel,
        out_shape=jax.ShapeDtypeStruct((5, 2, PAIRS, 128), jnp.float32),
        scratch_shapes=[field] * 4,
        compiler_params=pltpu.CompilerParams(vmem_limit_bytes=24 << 20),
        cost_estimate=pl.CostEstimate(
            flops=20_000_000_000, bytes_accessed=4_000_000, transcendentals=0
        ),
        name="inner_rows",
    )(own)


def link_kernel(
    own, above, below, inner, band, out, z_re, z_im, z_sum, z_dif, sums, tails, extra, cov, vec
):
    fields = (z_re, z_im, z_sum, z_dif)
    lanes = lax.broadcasted_iota(jnp.int32, (8, 128), 1)
    put, run = unpacker(fields)
    run(above, 1, 0, 6)
    run(own, 12, 6, 2)
    run(own, 23, 8, 2)
    run(below, 0, 10, 6)
    for group in range(4):
        pieces = []
        for source in (2 * group, 2 * group + 1):
            mid = own[source, TAIL_SLOT].astype(jnp.float32)
            up = above[source, 0].astype(jnp.float32)
            down = below[source, 6].astype(jnp.float32)
            piece = []
            for p in range(4):
                cut = slice(8 * p, 8 * p + 8)
                value = pltpu.roll(mid[cut], 18, 1)
                value = jnp.where(lanes < 18, pltpu.roll(up[cut], 128 - 54, 1), value)
                value = jnp.where(
                    (lanes >= 90) & (lanes < 108), pltpu.roll(down[cut], 90, 1), value
                )
                piece.append(value)
            pieces.append(piece)
        for p in range(4):
            put(64 + p, group, pieces[0][p], pieces[1][p])

    def store_tail(c, spot, value):
        tails[c, spot] = value

    gram(fields, 64, 4, store_tail)
    tails[1, 0:DATES] = jnp.zeros((DATES, 128), jnp.float32)
    gram_rows(fields, sums, 4, 0, 0)

    def add_tail(a, carry):
        for c in range(2):
            high, low = split(tails[c])
            extra[a, c] = jnp.dot(
                jnp.concatenate([high, low], axis=1),
                jnp.concatenate([band[a], band[a]], axis=0),
                preferred_element_type=jnp.float32,
            )
        return carry

    lax.fori_loop(0, 6, add_tail, 0)

    def windows(c, s, group):
        spot = s * DATES + group * 8
        spot = spot if isinstance(spot, int) else pl.multiple_of(spot, 8)
        where = pl.ds(spot, 8)
        rowsum = [sums[r, c, where] for r in (0, 1)]
        rowsum += [inner[r, c, where] for r in range(5)]
        rowsum += [sums[r, c, where] for r in (2, 3)]
        pairs = [rowsum[r] + rowsum[r + 1] for r in range(8)]
        twice = s * 2 * DATES + group * 8
        twice = twice if isinstance(twice, int) else pl.multiple_of(twice, 8)
        for a in range(6):
            value = pairs[a] + pairs[a + 2]
            value = value + jnp.where(lanes < 127, pltpu.roll(value, 127, 1), 0.0)
            value = value + jnp.where(lanes < 126, pltpu.roll(value, 126, 1), 0.0)
            value = value + extra[a, c, where]
            cov[a, c, pl.ds(twice, 8)] = value
            cov[a, c, pl.ds(twice + DATES, 8)] = value

    for group in range(4):
        windows(0, 0, group)

    def shift_windows(s, carry):
        for group in range(4):
            windows(0, s, group)
            windows(1, s, group)
        return carry

    lax.fori_loop(1, SHIFTS, shift_windows, 0)

    def put_vec(c, group, value):
        for copy in range(3):
            vec[c, copy * DATES + group * 8 : copy * DATES + group * 8 + 8] = value

    def window_row(a, carry):
        weights = []
        for group in range(4):
            power = cov[a, 0, 8 * group : 8 * group + 8]
            weights.append(1.0 / jnp.sqrt(power + BETA_LOAD))
            put_vec(0, group, weights[group])

        def iterate(real, last):
            found = []
            for group in range(4):
                row = 8 * group
                re_parts, im_parts = [], []
                for s in range(SHIFTS):
                    terms = [(2 * s * DATES + row, DATES + row + s, 1)]
                    if 0 < s < SHIFTS - 1:
                        terms.append((2 * s * DATES + DATES + row - s, DATES + row - s, -1))
                    for place, other, sign in terms:
                        cov_re = cov[a, 0, place : place + 8]
                        x_re = vec[0, other : other + 8]
                        x_im = None if real else vec[1, other : other + 8]
                        if s == 0:
                            re = cov_re * x_re
                            im = None if real else cov_re * x_im
                        else:
                            cov_im = cov[a, 1, place : place + 8]
                            re = cov_re * x_re
                            im = cov_im * x_re
                            if sign < 0:
                                im = -im if real else cov_re * x_im - im
                                re = re if real else re + cov_im * x_im
                            elif not real:
                                re = re - cov_im * x_im
                                im = im + cov_re * x_im
                        re_parts.append(re)
                        if im is not None:
                            im_parts.append(im)
                found.append((sum_two(re_parts), sum_two(im_parts)))
            for group in range(4):
                u_re = found[group][0] * weights[group]
                u_im = found[group][1] * weights[group]
                length = 1.0 / jnp.sqrt(u_re * u_re + u_im * u_im + PROJ_LOAD)
                x_re, x_im = u_re * length, u_im * length
                if last:
                    out[0, a, 8 * group : 8 * group + 8] = x_re
                    out[1, a, 8 * group : 8 * group + 8] = x_im
                else:
                    put_vec(0, group, x_re * weights[group])
                    put_vec(1, group, x_im * weights[group])

        iterate(True, False)
        lax.fori_loop(0, ITERS - 2, lambda i, carry: (iterate(False, False), carry)[1], 0)
        iterate(False, True)
        return carry

    lax.fori_loop(0, 6, window_row, 0)


def sum_two(parts):
    sums = parts[:2]
    for i, part in enumerate(parts[2:]):
        sums[i % 2] = sums[i % 2] + part
    return sums[0] + sums[1]


def link_windows(own, above, below, inner):
    field = pltpu.VMEM((68, WRAP, 128), jnp.float32)
    found = pl.pallas_call(
        link_kernel,
        out_shape=jax.ShapeDtypeStruct((2, 6, DATES, 128), jnp.float32),
        scratch_shapes=[field] * 4
        + [
            pltpu.VMEM((4, 2, PAIRS, 128), jnp.float32),
            pltpu.VMEM((2, PAIRS, 128), jnp.float32),
            pltpu.VMEM((6, 2, PAIRS, 128), jnp.float32),
            pltpu.VMEM((6, 2, 2 * PAIRS, 128), jnp.float32),
            pltpu.VMEM((2, 3 * DATES, 128), jnp.float32),
        ],
        compiler_params=pltpu.CompilerParams(vmem_limit_bytes=40 << 20),
        cost_estimate=pl.CostEstimate(
            flops=20_000_000_000, bytes_accessed=8_000_000, transcendentals=0
        ),
        name="link_windows",
    )(own, above, below, inner, tail_band())
    return jnp.transpose(found, (0, 2, 1, 3))


def on_device(stack, range_filter, scatter_mask):
    tiles = filter_lines(stack, range_filter, scatter_mask)
    own = lax.all_to_all(tiles, "dr", split_axis=0, concat_axis=0, tiled=True)
    count = lax.axis_size("az")
    down = [(i, i + 1) for i in range(count - 1)]
    up = [(i + 1, i) for i in range(count - 1)]
    above = lax.ppermute(own[:, 18:25], "az", down)
    below = lax.ppermute(own[:, 12:19], "az", up)
    inner = inner_rows(own)
    return link_windows(own, above, below, inner)


def solution(mesh):
    in_specs = (P(None, "dr", "az", None), P("dr", None), P("az", None))
    out_specs = P(None, None, "az", "dr")
    return jax.shard_map(
        on_device, mesh=mesh, in_specs=in_specs, out_specs=out_specs, check_vma=False
    )
```

```python
import functools
import math

import jax
import jax.numpy as jnp
import numpy as np
from jax import lax
from jax.experimental import pallas as pl
from jax.experimental.pallas import tpu as pltpu
from jax.sharding import PartitionSpec as P


ITERS = 4
BETA_LOAD = 1.0
PROJ_LOAD = 1.0

DATES = 32
RG = 4096
TILES = 8
HALO = 6
PLANES = 32
HERE = 4
FIRST, SECOND = (0, 16), (8,)
SHIFTS = 17
PAIRS = (SHIFTS + 1) * DATES
WRAP = 48


def slots_of(blocks):
    if blocks == FIRST:
        order = [6, 7, 16, 17, 0, 1, 2, 3, 4, 5, None, 18, 19, 20, 21, 22, 23]
    else:
        order = list(range(8, 16)) + [None]
    lines = [block + i for block in blocks for i in range(8)]
    return [order.index(line) for line in lines], order.index(None)


def split_np(table):
    high = table.astype(jnp.bfloat16)
    low = (table - high.astype(np.float64)).astype(jnp.bfloat16)
    return np.concatenate([high, high, low], axis=0)


def tables():
    lane = np.arange(128)
    freq = 4 * (lane % 32) + lane // 32
    turn = 2.0 * np.pi / 128 * (np.outer(lane, freq) % 128)
    forward = split_np(np.block([[np.cos(turn), -np.sin(turn)], [np.sin(turn), np.cos(turn)]]))
    turn = 2.0 * np.pi / 128 * (np.outer(freq, lane - HALO) % 128)
    inverse = split_np(
        np.block([[np.cos(turn), np.sin(turn)], [-np.sin(turn), np.cos(turn)]]) / RG
    )
    plane = np.arange(PLANES)
    angle = 2.0 * np.pi / RG * np.outer(plane, lane)
    back = 2.0 * np.pi / RG * np.outer(plane, lane - HALO)
    twist = np.stack([np.cos(angle), np.sin(angle), np.cos(back), np.sin(back)])
    place = np.zeros((512, 512), np.float32)
    for phase in range(4):
        for block in range(128):
            place[4 * block + phase, phase * 128 + block] = 1.0
    return forward, inverse, twist.astype(np.float32), place.astype(jnp.bfloat16)


def tail_band():
    near = np.zeros((128, 128), np.float32)
    for block in range(128):
        near[block, max(block - 3, 0) : block + 1] = 1.0
    band = np.zeros((6, 128, 128), np.float32)
    for row in range(6):
        for line in range(4 * row, 4 * row + 16):
            for block in range(3):
                band[row, line * 3 + block, 125 + block :] = 1.0
    both = np.concatenate(list(band), axis=1)
    both = np.concatenate([both, both], axis=0).astype(jnp.bfloat16)
    return np.concatenate([near, near], axis=0).astype(jnp.bfloat16), both


def cmul(value, cos, sin):
    re, im = value
    if abs(sin) < 1e-12:
        return (re, im) if cos > 0 else (-re, -im)
    if abs(cos) < 1e-12:
        return (-im, re) if sin > 0 else (im, -re)
    if abs(abs(cos) - abs(sin)) < 1e-12:
        size = abs(cos)
        if cos > 0 and sin > 0:
            return ((re - im) * size, (re + im) * size)
        if cos > 0:
            return ((re + im) * size, (im - re) * size)
        if sin > 0:
            return ((-re - im) * size, (re - im) * size)
        return ((im - re) * size, (-re - im) * size)
    return (re * cos - im * sin, im * cos + re * sin)


def small_dft(values, sign):
    count = len(values)
    if count == 1:
        return values
    even = small_dft(values[0::2], sign)
    odd = small_dft(values[1::2], sign)
    half = count // 2
    low, high = [], []
    for k in range(half):
        angle = sign * 2.0 * math.pi * k / count
        re, im = cmul(odd[k], math.cos(angle), math.sin(angle))
        low.append((even[k][0] + re, even[k][1] + im))
        high.append((even[k][0] - re, even[k][1] - im))
    return low + high


def dft_planes(load, hold, store, sign):
    for m in range(8):
        parts = small_dft([load(8 * i + m) for i in range(4)], sign)
        for s in range(4):
            angle = sign * 2.0 * math.pi * m * s / 32
            re, im = cmul(parts[s], math.cos(angle), math.sin(angle))
            hold[0, s * 8 + m] = re
            hold[1, s * 8 + m] = im
    for s in range(4):
        parts = small_dft([(hold[0, s * 8 + m], hold[1, s * 8 + m]) for m in range(8)], sign)
        for u in range(8):
            store(s + 4 * u, *parts[u])


def split(values):
    high = values.astype(jnp.bfloat16)
    return high, (values - high.astype(jnp.float32)).astype(jnp.bfloat16)


def dot3(values, table):
    high, low = split(values)
    return jnp.dot(
        jnp.concatenate([high, low, high], axis=1), table, preferred_element_type=jnp.float32
    )


def filter_kernel(
    blocks, group, stack, gains, mask, forward, inverse, twist, place, out,
    raw, gains_in, mask_in, forward_in, inverse_in, twist_in, place_in, sem,
    first, spec, hold, held, gain, weights, lines_out,
):
    count = len(blocks)
    lines_here = 8 * count
    rows_here = HERE * lines_here
    line_slots, tail_slot = slots_of(blocks)
    copies = {}
    for i, block in enumerate(blocks):
        for c in range(2):
            for d in range(HERE):
                index = (c * HERE + d) * count + i
                copies[c, d, i] = pltpu.make_async_copy(
                    stack.at[c, d, pl.ds(block, 8)], raw.at[c, d * count + i], sem.at[index]
                )
        copies["mask", i] = pltpu.make_async_copy(
            mask.at[pl.ds(block, 8)], mask_in.at[pl.ds(8 * i, 8)], sem.at[8 * count + i]
        )
    others = (
        ("gains", gains, gains_in),
        ("twist", twist, twist_in),
        ("forward", forward, forward_in),
        ("inverse", inverse, inverse_in),
        ("place", place, place_in),
    )
    for i, (name, source, target) in enumerate(others):
        copies[name] = pltpu.make_async_copy(source, target, sem.at[9 * count + i])
    for copy in copies.values():
        copy.start()
    lanes = lax.broadcasted_iota(jnp.int32, (8, 128), 1)
    copies["gains"].wait()
    for n in range(PLANES):
        four = gains_in[:, n * 128 : (n + 1) * 128]
        for d in range(HERE):
            gain[d, n : n + 1] = four[d : d + 1]
    for d in range(HERE):
        turned = jnp.transpose(gain[d])
        gain[d] = jnp.concatenate([turned[32 * w : 32 * w + 32] for w in range(4)], axis=1)
    for i in range(count):
        copies["mask", i].wait()
        rows = slice(8 * i, 8 * i + 8)
        before = pltpu.roll(mask_in[rows, RG - 128 :].astype(jnp.float32), HALO, 1)
        for n in range(PLANES):
            now = pltpu.roll(mask_in[rows, n * 128 : (n + 1) * 128].astype(jnp.float32), HALO, 1)
            joined = jnp.where(lanes < HALO, before, now)
            if n == 0:
                weights[PLANES, rows] = jnp.where(lanes < HALO, joined, 0.0)
                joined = jnp.where(lanes < HALO, 0.0, joined)
            weights[n, rows] = joined
            before = now

    def ahead(block, carry):
        rows = pl.ds(pl.multiple_of(block * 8, 8), 8)

        def store(q, re, im):
            spec[0, q, rows] = re
            spec[1, q, rows] = im

        for c in range(2):
            pltpu.make_async_copy(
                stack.at[0, 0, pl.ds(0, 8)], raw.at[c, block], sem.at[c * HERE * count + block]
            ).wait()

        def load(n):
            lanes = slice(n * 128, (n + 1) * 128)
            return (
                raw[0, block, :, lanes].astype(jnp.float32),
                raw[1, block, :, lanes].astype(jnp.float32),
            )

        dft_planes(load, hold, store, -1)
        return carry

    lax.fori_loop(0, rows_here // 8, ahead, 0)
    steps = PLANES // group
    for name in ("twist", "forward", "inverse"):
        copies[name].wait()

    def middle(step, carry):
        now = jnp.minimum(step, steps - 1) * group
        past = jnp.maximum(step - 1, 0) * group
        parts = []
        for i in range(group):
            tc = twist_in[0, pl.ds(now + i, 1), :]
            ts = twist_in[1, pl.ds(now + i, 1), :]
            re, im = spec[0, now + i], spec[1, now + i]
            parts.append(jnp.concatenate([re * tc + im * ts, im * tc - re * ts], axis=1))
        back = dot3(held[lax.rem(step + 1, 2)], inverse_in[...])
        found = dot3(jnp.concatenate(parts, axis=0), forward_in[...])
        for i in range(group):
            for d in range(HERE):
                row = gain[d, pl.ds(now + i, 1), :]
                begin = i * rows_here + d * lines_here
                held[lax.rem(step, 2), begin : begin + lines_here] = found[
                    begin : begin + lines_here
                ] * jnp.concatenate([row, row], axis=1)
        for i in range(group):
            tc = twist_in[2, pl.ds(past + i, 1), :]
            ts = twist_in[3, pl.ds(past + i, 1), :]
            re = back[i * rows_here : (i + 1) * rows_here, :128]
            im = back[i * rows_here : (i + 1) * rows_here, 128:]
            first[0, past + i] = re * tc - im * ts
            first[1, past + i] = im * tc + re * ts
        return carry

    lax.fori_loop(0, steps + 1, middle, 0)

    def behind(block, carry):
        rows = pl.ds(pl.multiple_of(block * 8, 8), 8)
        to_im = pl.ds(pl.multiple_of(block * 8 + rows_here, 8), 8)
        lines = pl.ds(pl.multiple_of(lax.rem(block, count) * 8, 8), 8)

        def store(n, re, im):
            weight = weights[n, lines]
            lines_out[n, rows] = re * weight
            lines_out[n, to_im] = im * weight
            if n == 0:
                weight = weights[PLANES, lines]
                lines_out[PLANES, rows] = re * weight
                lines_out[PLANES, to_im] = im * weight

        dft_planes(lambda q: (first[0, q, rows], first[1, q, rows]), hold, store, 1)
        return carry

    lax.fori_loop(0, rows_here // 8, behind, 0)
    copies["place"].wait()

    def gather(plane):
        return jnp.concatenate(
            [lines_out[plane, pl.ds(line, 8, stride=lines_here), :] for line in range(lines_here)],
            axis=0,
        )

    def put_tail(slot, found):
        tails = []
        for p in range(4):
            tail = jnp.zeros((8, 128), jnp.float32)
            for line in range(lines_here):
                part = found[line * 8 : line * 8 + 8, p * 128 : p * 128 + 128]
                if line:
                    part = pltpu.roll(part, 3 * line, 1)
                tail = jnp.where(lanes >= 3 * line, part, tail)
            tails.append(jnp.where(lanes < 3 * lines_here, tail, 0.0))
        out[slot, tail_slot] = jnp.concatenate(tails, axis=0).astype(jnp.bfloat16)

    def tile(t, carry):
        left = jnp.concatenate([gather(4 * t + v) for v in range(4)], axis=1).astype(jnp.bfloat16)
        found = jnp.dot(left, place_in[...], preferred_element_type=jnp.float32)
        for line in range(lines_here):
            out[t, line_slots[line]] = jnp.concatenate(
                [found[line * 8 : line * 8 + 8, p * 128 : p * 128 + 128] for p in range(4)],
                axis=0,
            ).astype(jnp.bfloat16)
        put_tail(lax.rem(t + TILES - 1, TILES), found)
        return carry

    lax.fori_loop(0, TILES, tile, 0)
    found = jnp.dot(
        gather(PLANES).astype(jnp.bfloat16), place_in[:128], preferred_element_type=jnp.float32
    )
    put_tail(TILES - 1, found)


def filter_lines(stack, gains, mask, blocks, group):
    forward, inverse, twist, place = tables()
    count = len(blocks)
    rows = HERE * 8 * count
    return pl.pallas_call(
        functools.partial(filter_kernel, blocks, group),
        out_shape=jax.ShapeDtypeStruct((TILES, 8 * count + 1, 32, 128), jnp.bfloat16),
        in_specs=[pl.BlockSpec(memory_space=pltpu.MemorySpace.HBM)] * 7,
        scratch_shapes=[
            pltpu.VMEM((2, HERE * count, 8, RG), jnp.bfloat16),
            pltpu.VMEM((HERE, RG), jnp.float32),
            pltpu.VMEM((8 * count, RG), jnp.int32),
            pltpu.VMEM((768, 256), jnp.bfloat16),
            pltpu.VMEM((768, 256), jnp.bfloat16),
            pltpu.VMEM((4, PLANES, 128), jnp.float32),
            pltpu.VMEM((512, 512), jnp.bfloat16),
            pltpu.SemaphoreType.DMA((9 * count + 5,)),
            pltpu.VMEM((2, PLANES, rows, 128), jnp.float32),
            pltpu.VMEM((2, PLANES, rows, 128), jnp.float32),
            pltpu.VMEM((2, PLANES, 8, 128), jnp.float32),
            pltpu.VMEM((2, group * rows, 256), jnp.float32),
            pltpu.VMEM((HERE, PLANES, 128), jnp.float32),
            pltpu.VMEM((PLANES + 1, 8 * count, 128), jnp.float32),
            pltpu.VMEM((PLANES + 1, 2 * rows, 128), jnp.float32),
        ],
        compiler_params=pltpu.CompilerParams(
            vmem_limit_bytes=(60 if blocks == FIRST else 24) << 20
        ),
        cost_estimate=pl.CostEstimate(
            flops=2_000_000_000 * count, bytes_accessed=2_000_000, transcendentals=0
        ),
    )(stack, gains, mask, forward, inverse, twist, place)


def unpacker(fields):
    z_re, z_im, z_sum, z_dif = fields
    rows = lax.broadcasted_iota(jnp.int32, (8, 128), 0)
    low = rows < 4

    def put(plane, group, first, second):
        re = jnp.where(low, first, pltpu.roll(second, 4, 0))
        im = jnp.where(low, pltpu.roll(first, 4, 0), second)
        total, change = re + im, im - re
        z_im[plane, 8 * group : 8 * group + 8] = im
        for begin in [8 * group] + ([32 + 8 * group] if group < 2 else []):
            z_re[plane, begin : begin + 8] = re
            z_sum[plane, begin : begin + 8] = total
            z_dif[plane, begin : begin + 8] = change

    def run(ref, slot, line, count):
        def step(i, carry):
            for group in range(4):
                first = ref[2 * group, slot + i].astype(jnp.float32)
                second = ref[2 * group + 1, slot + i].astype(jnp.float32)
                for p in range(4):
                    cut = slice(8 * p, 8 * p + 8)
                    put((line + i) * 4 + p, group, first[cut], second[cut])
            return carry

        lax.fori_loop(0, count, step, 0)

    return put, run


WIDTH = 8


def gram(fields, base, count, store):
    z_re, z_im, z_sum, z_dif = fields

    def block(index, carry):
        group = index // 2
        own = pl.ds(pl.multiple_of(group * 8, 8), 8)
        begin = pl.multiple_of(group * 8 + lax.rem(index, 2) * 8, 8)
        unit = min(8, count)

        def some(chunk, totals):
            totals = [list(totals[3 * i : 3 * i + 3]) for i in range(WIDTH)]
            for step in range(unit):
                plane = base + chunk * unit + step
                mine = (z_sum[plane, own], z_re[plane, own], z_im[plane, own])
                for i in range(WIDTH):
                    other = pl.ds(begin + 1 + i, 8)
                    others = (z_re[plane, other], z_sum[plane, other], z_dif[plane, other])
                    for k in range(3):
                        totals[i][k] = totals[i][k] + others[k] * mine[k]
            return tuple(t for total in totals for t in total)

        zero = jnp.zeros((8, 128), jnp.float32)
        totals = lax.fori_loop(0, count // unit, some, (zero,) * (3 * WIDTH))
        totals = [totals[3 * i : 3 * i + 3] for i in range(WIDTH)]
        for i in range(WIDTH):
            one, two, three = totals[i]
            spot = (lax.rem(index, 2) * 8 + 1 + i) * DATES + group * 8
            spot = pl.ds(pl.multiple_of(spot, 8), 8)
            store(0, spot, one + three)
            store(1, spot, one - two)
        return carry

    lax.fori_loop(0, 8, block, 0)
    for group in range(4):
        own = slice(8 * group, 8 * group + 8)
        total = None
        for step in range(count):
            re, im = z_re[base + step, own], z_im[base + step, own]
            term = re * re + im * im
            total = term if total is None else total + term
        store(0, own, total)


def gram_rows(fields, sums, count, first_plane, first_row):
    def one_row(r, carry):
        def store(c, spot, value):
            sums[first_row + r, c, spot] = value

        gram(fields, first_plane + r * 16, 16, store)
        return carry

    lax.fori_loop(0, count, one_row, 0)


def early_kernel(own, sums, *fields):
    _, run = unpacker(fields)
    run(own, 6, 0, 4)
    run(own, 11, 4, 4)
    gram_rows(fields, sums, 2, 0, 0)


def inner_kernel(own, rest, sums, *fields):
    _, run = unpacker(fields)
    run(own, 0, 0, 2)
    run(rest, 0, 2, 8)
    run(own, 2, 10, 2)
    gram_rows(fields, sums, 3, 0, 0)


def own_rows(kernel, count, *chunks):
    field = pltpu.VMEM((count * 16, WRAP, 128), jnp.float32)
    return pl.pallas_call(
        kernel,
        out_shape=jax.ShapeDtypeStruct((count, 2, PAIRS, 128), jnp.float32),
        scratch_shapes=[field] * 4,
        compiler_params=pltpu.CompilerParams(vmem_limit_bytes=16 << 20),
        cost_estimate=pl.CostEstimate(
            flops=3_000_000_000 * count, bytes_accessed=2_000_000, transcendentals=0
        ),
    )(*chunks)


def link_kernel(
    own, rest, above, below, early, inner, near, band, out,
    z_re, z_im, z_sum, z_dif, sums, tails, extra, cov, vec,
):
    fields = (z_re, z_im, z_sum, z_dif)
    lanes = lax.broadcasted_iota(jnp.int32, (8, 128), 1)
    put, run = unpacker(fields)
    run(above, 1, 0, 6)
    run(own, 4, 6, 2)
    run(own, 15, 8, 2)
    run(below, 0, 10, 6)
    for group in range(4):
        pieces = []
        for source in (2 * group, 2 * group + 1):
            mine = own[source, 10].astype(jnp.float32)
            others = rest[source, 8].astype(jnp.float32)
            up = above[source, 0].astype(jnp.float32)
            down = below[source, 6].astype(jnp.float32)
            piece = []
            for p in range(4):
                cut = slice(8 * p, 8 * p + 8)
                value = jnp.zeros((8, 128), jnp.float32)
                for part, turn, begin in (
                    (up, 128 - 30, 0),
                    (mine, 18, 18),
                    (others, 42, 42),
                    (mine, 42, 66),
                    (down, 90, 90),
                ):
                    value = jnp.where(lanes >= begin, pltpu.roll(part[cut], turn, 1), value)
                piece.append(jnp.where(lanes < 108, value, 0.0))
            pieces.append(piece)
        for p in range(4):
            put(64 + p, group, pieces[0][p], pieces[1][p])

    def store_tail(c, spot, value):
        tails[c, spot] = value

    gram(fields, 64, 4, store_tail)
    tails[1, 0:DATES] = jnp.zeros((DATES, 128), jnp.float32)
    gram_rows(fields, sums, 4, 0, 0)
    for c in range(2):
        high, low = split(tails[c])
        extra[c] = jnp.dot(
            jnp.concatenate([high, low], axis=1), band[...], preferred_element_type=jnp.float32
        )

    def windows(step, carry):
        size = 2 * DATES
        begin = pl.multiple_of(step * size, size)
        spot = pl.ds(begin, size)
        twice = pl.multiple_of(step * 2 * size, 2 * size)
        for c in range(2):
            rowsum = [sums[r, c, spot] for r in (0, 1)]
            rowsum += [early[0, c, spot]] + [inner[r, c, spot] for r in range(3)]
            rowsum += [early[1, c, spot]]
            rowsum += [sums[r, c, spot] for r in (2, 3)]
            pairs = [rowsum[r] + rowsum[r + 1] for r in range(8)]
            value = jnp.concatenate([pairs[a] + pairs[a + 2] for a in range(6)], axis=0)
            high, low = split(value)
            found = jnp.dot(
                jnp.concatenate([high, low], axis=1), near[...], preferred_element_type=jnp.float32
            )
            for a in range(6):
                full = found[a * size : (a + 1) * size] + extra[c, spot, a * 128 : a * 128 + 128]
                for i in range(2):
                    half = full[i * DATES : (i + 1) * DATES]
                    cov[a, c, pl.ds(twice + 2 * i * DATES, DATES)] = half
                    cov[a, c, pl.ds(twice + (2 * i + 1) * DATES, DATES)] = half
        return carry

    lax.fori_loop(0, (SHIFTS + 1) // 2, windows, 0)

    def put_vec(c, group, value):
        for copy in range(3):
            vec[c, copy * DATES + group * 8 : copy * DATES + group * 8 + 8] = value

    def window_row(a, carry):
        weights = []
        for group in range(4):
            power = cov[a, 0, 8 * group : 8 * group + 8]
            weights.append(1.0 / jnp.sqrt(power + BETA_LOAD))
            put_vec(0, group, weights[group])

        def iterate(real, last):
            found = []
            for group in range(4):
                row = 8 * group
                re_parts, im_parts = [], []
                for s in range(SHIFTS):
                    terms = [(2 * s * DATES + row, DATES + row + s, 1)]
                    if 0 < s < SHIFTS - 1:
                        terms.append((2 * s * DATES + DATES + row - s, DATES + row - s, -1))
                    for place, other, sign in terms:
                        cov_re = cov[a, 0, place : place + 8]
                        x_re = vec[0, other : other + 8]
                        x_im = None if real else vec[1, other : other + 8]
                        if s == 0:
                            re = cov_re * x_re
                            im = None if real else cov_re * x_im
                        else:
                            cov_im = cov[a, 1, place : place + 8]
                            re = cov_re * x_re
                            im = cov_im * x_re
                            if sign < 0:
                                im = -im if real else cov_re * x_im - im
                                re = re if real else re + cov_im * x_im
                            elif not real:
                                re = re - cov_im * x_im
                                im = im + cov_re * x_im
                        re_parts.append(re)
                        if im is not None:
                            im_parts.append(im)
                found.append((sum_two(re_parts), sum_two(im_parts)))
            for group in range(4):
                u_re = found[group][0] * weights[group]
                u_im = found[group][1] * weights[group]
                length = 1.0 / jnp.sqrt(u_re * u_re + u_im * u_im + PROJ_LOAD)
                x_re, x_im = u_re * length, u_im * length
                if last:
                    out[0, a, 8 * group : 8 * group + 8] = x_re
                    out[1, a, 8 * group : 8 * group + 8] = x_im
                else:
                    put_vec(0, group, x_re * weights[group])
                    put_vec(1, group, x_im * weights[group])

        iterate(True, False)
        lax.fori_loop(0, ITERS - 2, lambda i, carry: (iterate(False, False), carry)[1], 0)
        iterate(False, True)
        return carry

    lax.fori_loop(0, 6, window_row, 0)


def sum_two(parts):
    sums = parts[:2]
    for i, part in enumerate(parts[2:]):
        sums[i % 2] = sums[i % 2] + part
    return sums[0] + sums[1]


def link_windows(own, rest, above, below, early, inner):
    field = pltpu.VMEM((68, WRAP, 128), jnp.float32)
    found = pl.pallas_call(
        link_kernel,
        out_shape=jax.ShapeDtypeStruct((2, 6, DATES, 128), jnp.float32),
        scratch_shapes=[field] * 4
        + [
            pltpu.VMEM((4, 2, PAIRS, 128), jnp.float32),
            pltpu.VMEM((2, PAIRS, 128), jnp.float32),
            pltpu.VMEM((2, PAIRS, 6 * 128), jnp.float32),
            pltpu.VMEM((6, 2, 2 * PAIRS, 128), jnp.float32),
            pltpu.VMEM((2, 3 * DATES, 128), jnp.float32),
        ],
        compiler_params=pltpu.CompilerParams(vmem_limit_bytes=40 << 20),
        cost_estimate=pl.CostEstimate(
            flops=20_000_000_000, bytes_accessed=8_000_000, transcendentals=0
        ),
        name="link_windows",
    )(own, rest, above, below, early, inner, *tail_band())
    return jnp.transpose(found, (0, 2, 1, 3))


def on_device(stack, range_filter, scatter_mask):
    def move(tiles):
        return lax.all_to_all(tiles, "dr", split_axis=0, concat_axis=0, tiled=True)

    own = move(filter_lines(stack, range_filter, scatter_mask, FIRST, 4))
    tiles = filter_lines(stack, range_filter, scatter_mask, SECOND, 8)
    rest = move(tiles)
    count = lax.axis_size("az")
    down = [(i, i + 1) for i in range(count - 1)]
    up = [(i + 1, i) for i in range(count - 1)]
    above = lax.ppermute(own[:, 10:17], "az", down)
    below = lax.ppermute(own[:, 4:11], "az", up)
    early = own_rows(early_kernel, 2, own)
    inner = own_rows(inner_kernel, 3, own, rest)
    return link_windows(own, rest, above, below, early, inner)


def solution(mesh):
    in_specs = (P(None, "dr", "az", None), P("dr", None), P("az", None))
    out_specs = P(None, None, "az", "dr")
    return jax.shard_map(
        on_device, mesh=mesh, in_specs=in_specs, out_specs=out_specs, check_vma=False
    )
```

```python
import functools
import math

import jax
import jax.numpy as jnp
import numpy as np
from jax import lax
from jax.experimental import pallas as pl
from jax.experimental.pallas import tpu as pltpu
from jax.sharding import PartitionSpec as P


ITERS = 4
BETA_LOAD = 1.0
PROJ_LOAD = 1.0

DATES = 32
RG = 4096
TILES = 8
HALO = 6
PLANES = 32
HERE = 4
FIRST, SECOND = (0, 16), (8,)
SHIFTS = 17
PAIRS = (SHIFTS + 1) * DATES
WRAP = 48


def slots_of(blocks):
    if blocks == FIRST:
        order = [6, 7, 16, 17, 0, 1, 2, 3, 4, 5, None, 18, 19, 20, 21, 22, 23]
    else:
        order = list(range(8, 16)) + [None]
    lines = [block + i for block in blocks for i in range(8)]
    return [order.index(line) for line in lines], order.index(None)


def tables():
    lane = np.arange(128)
    freq = 4 * (lane % 32) + lane // 32
    turn = 2.0 * np.pi / 128 * (np.outer(lane, freq) % 128)
    forward = np.block([[np.cos(turn), -np.sin(turn)], [np.sin(turn), np.cos(turn)]])
    turn = 2.0 * np.pi / 128 * (np.outer(freq, lane - HALO) % 128)
    inverse = np.block([[np.cos(turn), np.sin(turn)], [-np.sin(turn), np.cos(turn)]]) / RG
    plane = np.arange(PLANES)
    angle = 2.0 * np.pi / RG * np.outer(plane, lane)
    back = 2.0 * np.pi / RG * np.outer(plane, lane - HALO)
    parts = [forward[:, :128], forward[:, 128:], inverse[:, :128], inverse[:, 128:]]
    parts += [np.cos(angle), np.sin(angle), np.cos(back), np.sin(back)]
    return np.concatenate(parts, axis=0).astype(np.float32)


def cmul(value, cos, sin):
    re, im = value
    if abs(sin) < 1e-12:
        return (re, im) if cos > 0 else (-re, -im)
    if abs(cos) < 1e-12:
        return (-im, re) if sin > 0 else (im, -re)
    if abs(abs(cos) - abs(sin)) < 1e-12:
        size = abs(cos)
        if cos > 0 and sin > 0:
            return ((re - im) * size, (re + im) * size)
        if cos > 0:
            return ((re + im) * size, (im - re) * size)
        if sin > 0:
            return ((-re - im) * size, (re - im) * size)
        return ((im - re) * size, (-re - im) * size)
    return (re * cos - im * sin, im * cos + re * sin)


def small_dft(values, sign):
    count = len(values)
    if count == 1:
        return values
    even = small_dft(values[0::2], sign)
    odd = small_dft(values[1::2], sign)
    half = count // 2
    low, high = [], []
    for k in range(half):
        angle = sign * 2.0 * math.pi * k / count
        re, im = cmul(odd[k], math.cos(angle), math.sin(angle))
        low.append((even[k][0] + re, even[k][1] + im))
        high.append((even[k][0] - re, even[k][1] - im))
    return low + high


def dft_planes(load, hold, store, sign):
    for m in range(8):
        parts = small_dft([load(8 * i + m) for i in range(4)], sign)
        for s in range(4):
            angle = sign * 2.0 * math.pi * m * s / 32
            re, im = cmul(parts[s], math.cos(angle), math.sin(angle))
            hold[0, s * 8 + m] = re
            hold[1, s * 8 + m] = im
    for s in range(4):
        parts = small_dft([(hold[0, s * 8 + m], hold[1, s * 8 + m]) for m in range(8)], sign)
        for u in range(8):
            store(s + 4 * u, *parts[u])


def split(values):
    high = values.astype(jnp.bfloat16)
    return high, (values - high.astype(jnp.float32)).astype(jnp.bfloat16)


def dot3(values, table):
    high, low = split(values)
    return jnp.dot(
        jnp.concatenate([high, low, high], axis=1), table, preferred_element_type=jnp.float32
    )


def filter_kernel(
    blocks, group, stack, gains, mask, table, out,
    raw, gains_in, mask_in, table_in, sem,
    spec, first, hold, held, gain, weights, lines_out, forward, inverse, place,
):
    count = len(blocks)
    lines_here = 8 * count
    rows_here = HERE * lines_here
    line_slots, tail_slot = slots_of(blocks)
    stack_copies = []
    for d in range(HERE):
        for i, block in enumerate(blocks):
            for c in range(2):
                stack_copies.append(
                    pltpu.make_async_copy(
                        stack.at[c, d, pl.ds(block, 8)],
                        raw.at[c, d * count + i],
                        sem.at[c * HERE * count + d * count + i],
                    )
                )
    copies = {}
    for i, (name, source, target) in enumerate(
        (("table", table, table_in), ("gains", gains, gains_in))
    ):
        copies[name] = pltpu.make_async_copy(source, target, sem.at[9 * count + i])
    for i, block in enumerate(blocks):
        copies["mask", i] = pltpu.make_async_copy(
            mask.at[pl.ds(block, 8)], mask_in.at[pl.ds(8 * i, 8)], sem.at[8 * count + i]
        )
    for copy in stack_copies + list(copies.values()):
        copy.start()
    lanes = lax.broadcasted_iota(jnp.int32, (8, 128), 1)

    def ahead(block, carry):
        rows = pl.ds(pl.multiple_of(block * 8, 8), 8)

        def store(q, re, im):
            spec[0, q, rows] = re
            spec[1, q, rows] = im

        for c in range(2):
            pltpu.make_async_copy(
                stack.at[0, 0, pl.ds(0, 8)], raw.at[c, block], sem.at[c * HERE * count + block]
            ).wait()

        def load(n):
            lanes = slice(n * 128, (n + 1) * 128)
            return (
                raw[0, block, :, lanes].astype(jnp.float32),
                raw[1, block, :, lanes].astype(jnp.float32),
            )

        dft_planes(load, hold, store, -1)
        return carry

    lax.fori_loop(0, rows_here // 8, ahead, 0)
    copies["gains"].wait()
    for n in range(PLANES):
        four = gains_in[:, n * 128 : (n + 1) * 128]
        for d in range(HERE):
            gain[d, n : n + 1] = four[d : d + 1]
    for d in range(HERE):
        turned = jnp.transpose(gain[d])
        gain[d] = jnp.concatenate([turned[32 * w : 32 * w + 32] for w in range(4)], axis=1)
    steps = PLANES // group
    copies["table"].wait()
    for i, target in enumerate((forward, inverse)):
        for half in range(2):
            begin = 256 * (2 * i + half)
            high, low = split(table_in[begin : begin + 256])
            for j, part in enumerate((high, high, low)):
                target[256 * j : 256 * j + 256, 128 * half : 128 * half + 128] = part
    row = lax.broadcasted_iota(jnp.int32, (512, 128), 0)
    column = lax.broadcasted_iota(jnp.int32, (512, 128), 1)
    for p in range(4):
        place[:, 128 * p : 128 * p + 128] = jnp.where(row == 4 * column + p, 1.0, 0.0).astype(
            jnp.bfloat16
        )

    def middle(step, carry):
        now = jnp.minimum(step, steps - 1) * group
        past = jnp.maximum(step - 1, 0) * group
        parts = []
        for i in range(group):
            tc = table_in[pl.ds(1024 + now + i, 1), :]
            ts = table_in[pl.ds(1056 + now + i, 1), :]
            re, im = spec[0, now + i], spec[1, now + i]
            parts.append(jnp.concatenate([re * tc + im * ts, im * tc - re * ts], axis=1))
        back = dot3(held[lax.rem(step + 1, 2)], inverse[...])
        found = dot3(jnp.concatenate(parts, axis=0), forward[...])
        for i in range(group):
            for d in range(HERE):
                row = gain[d, pl.ds(now + i, 1), :]
                begin = i * rows_here + d * lines_here
                held[lax.rem(step, 2), begin : begin + lines_here] = found[
                    begin : begin + lines_here
                ] * jnp.concatenate([row, row], axis=1)
        for i in range(group):
            tc = table_in[pl.ds(1088 + past + i, 1), :]
            ts = table_in[pl.ds(1120 + past + i, 1), :]
            re = back[i * rows_here : (i + 1) * rows_here, :128]
            im = back[i * rows_here : (i + 1) * rows_here, 128:]
            first[0, past + i] = re * tc - im * ts
            first[1, past + i] = im * tc + re * ts
        return carry

    lax.fori_loop(0, steps + 1, middle, 0)

    for i in range(count):
        copies["mask", i].wait()
        rows = slice(8 * i, 8 * i + 8)
        before = pltpu.roll(mask_in[rows, RG - 128 :].astype(jnp.float32), HALO, 1)
        for n in range(PLANES):
            now = pltpu.roll(mask_in[rows, n * 128 : (n + 1) * 128].astype(jnp.float32), HALO, 1)
            joined = jnp.where(lanes < HALO, before, now)
            if n == 0:
                weights[PLANES, rows] = jnp.where(lanes < HALO, joined, 0.0)
                joined = jnp.where(lanes < HALO, 0.0, joined)
            weights[n, rows] = joined
            before = now

    def behind(block, carry):
        rows = pl.ds(pl.multiple_of(block * 8, 8), 8)
        to_im = pl.ds(pl.multiple_of(block * 8 + rows_here, 8), 8)
        lines = pl.ds(pl.multiple_of(lax.rem(block, count) * 8, 8), 8)

        def store(n, re, im):
            weight = weights[n, lines]
            lines_out[n, rows] = re * weight
            lines_out[n, to_im] = im * weight
            if n == 0:
                weight = weights[PLANES, lines]
                lines_out[PLANES, rows] = re * weight
                lines_out[PLANES, to_im] = im * weight

        dft_planes(lambda q: (first[0, q, rows], first[1, q, rows]), hold, store, 1)
        return carry

    lax.fori_loop(0, rows_here // 8, behind, 0)

    def gather(plane):
        return jnp.concatenate(
            [lines_out[plane, pl.ds(line, 8, stride=lines_here), :] for line in range(lines_here)],
            axis=0,
        )

    def put_tail(slot, found):
        tails = []
        for p in range(4):
            tail = jnp.zeros((8, 128), jnp.float32)
            for line in range(lines_here):
                part = found[line * 8 : line * 8 + 8, p * 128 : p * 128 + 128]
                if line:
                    part = pltpu.roll(part, 3 * line, 1)
                tail = jnp.where(lanes >= 3 * line, part, tail)
            tails.append(jnp.where(lanes < 3 * lines_here, tail, 0.0))
        out[slot, tail_slot] = jnp.concatenate(tails, axis=0).astype(jnp.bfloat16)

    def one_tile(t):
        left = jnp.concatenate([gather(4 * t + v) for v in range(4)], axis=1).astype(jnp.bfloat16)
        found = jnp.dot(left, place[...], preferred_element_type=jnp.float32)
        for line in range(lines_here):
            out[t, line_slots[line]] = jnp.concatenate(
                [found[line * 8 : line * 8 + 8, p * 128 : p * 128 + 128] for p in range(4)],
                axis=0,
            ).astype(jnp.bfloat16)
        put_tail(lax.rem(t + TILES - 1, TILES), found)

    def tile(step, carry):
        one_tile(2 * step)
        one_tile(2 * step + 1)
        return carry

    lax.fori_loop(0, TILES // 2, tile, 0)
    found = jnp.dot(
        gather(PLANES).astype(jnp.bfloat16), place[:128], preferred_element_type=jnp.float32
    )
    put_tail(TILES - 1, found)


def filter_lines(stack, gains, mask, blocks, group):
    count = len(blocks)
    rows = HERE * 8 * count
    return pl.pallas_call(
        functools.partial(filter_kernel, blocks, group),
        out_shape=jax.ShapeDtypeStruct((TILES, 8 * count + 1, 32, 128), jnp.bfloat16),
        in_specs=[pl.BlockSpec(memory_space=pltpu.MemorySpace.HBM)] * 4,
        scratch_shapes=[
            pltpu.VMEM((2, HERE * count, 8, RG), jnp.bfloat16),
            pltpu.VMEM((HERE, RG), jnp.float32),
            pltpu.VMEM((8 * count, RG), jnp.int32),
            pltpu.VMEM((1152, 128), jnp.float32),
            pltpu.SemaphoreType.DMA((9 * count + 2,)),
            pltpu.VMEM((2, PLANES, rows, 128), jnp.float32),
            pltpu.VMEM((2, PLANES, rows, 128), jnp.float32),
            pltpu.VMEM((2, PLANES, 8, 128), jnp.float32),
            pltpu.VMEM((2, group * rows, 256), jnp.float32),
            pltpu.VMEM((HERE, PLANES, 128), jnp.float32),
            pltpu.VMEM((PLANES + 1, 8 * count, 128), jnp.float32),
            pltpu.VMEM((PLANES + 1, 2 * rows, 128), jnp.float32),
            pltpu.VMEM((768, 256), jnp.bfloat16),
            pltpu.VMEM((768, 256), jnp.bfloat16),
            pltpu.VMEM((512, 512), jnp.bfloat16),
        ],
        compiler_params=pltpu.CompilerParams(vmem_limit_bytes=65_700_000),
        cost_estimate=pl.CostEstimate(
            flops=2_000_000_000 * count, bytes_accessed=2_000_000, transcendentals=0
        ),
    )(stack, gains, mask, tables())


def unpacker(fields):
    z_re, z_im, z_sum, z_dif = fields
    rows = lax.broadcasted_iota(jnp.int32, (8, 128), 0)
    low = rows < 4

    def put(plane, group, first, second):
        re = jnp.where(low, first, pltpu.roll(second, 4, 0))
        im = jnp.where(low, pltpu.roll(first, 4, 0), second)
        total, change = re + im, im - re
        z_im[plane, 8 * group : 8 * group + 8] = im
        for begin in [8 * group] + ([32 + 8 * group] if group < 2 else []):
            z_re[plane, begin : begin + 8] = re
            z_sum[plane, begin : begin + 8] = total
            z_dif[plane, begin : begin + 8] = change

    def run(ref, slot, line, count):
        def step(i, carry):
            for group in range(4):
                first = ref[2 * group, slot + i].astype(jnp.float32)
                second = ref[2 * group + 1, slot + i].astype(jnp.float32)
                for p in range(4):
                    cut = slice(8 * p, 8 * p + 8)
                    put((line + i) * 4 + p, group, first[cut], second[cut])
            return carry

        lax.fori_loop(0, count, step, 0)

    return put, run


WIDTH = 8


def gram(fields, base, count, store):
    z_re, z_im, z_sum, z_dif = fields

    def block(index, carry):
        group = index // 2
        own = pl.ds(pl.multiple_of(group * 8, 8), 8)
        begin = pl.multiple_of(group * 8 + lax.rem(index, 2) * 8, 8)
        unit = min(8, count)

        def some(chunk, totals):
            totals = [list(totals[3 * i : 3 * i + 3]) for i in range(WIDTH)]
            for step in range(unit):
                plane = base + chunk * unit + step
                mine = (z_sum[plane, own], z_re[plane, own], z_im[plane, own])
                for i in range(WIDTH):
                    other = pl.ds(begin + 1 + i, 8)
                    others = (z_re[plane, other], z_sum[plane, other], z_dif[plane, other])
                    for k in range(3):
                        totals[i][k] = totals[i][k] + others[k] * mine[k]
            return tuple(t for total in totals for t in total)

        zero = jnp.zeros((8, 128), jnp.float32)
        totals = lax.fori_loop(0, count // unit, some, (zero,) * (3 * WIDTH))
        totals = [totals[3 * i : 3 * i + 3] for i in range(WIDTH)]
        for i in range(WIDTH):
            one, two, three = totals[i]
            spot = (lax.rem(index, 2) * 8 + 1 + i) * DATES + group * 8
            spot = pl.ds(pl.multiple_of(spot, 8), 8)
            store(0, spot, one + three)
            store(1, spot, one - two)
        return carry

    lax.fori_loop(0, 8, block, 0)
    for group in range(4):
        own = slice(8 * group, 8 * group + 8)
        total = None
        for step in range(count):
            re, im = z_re[base + step, own], z_im[base + step, own]
            term = re * re + im * im
            total = term if total is None else total + term
        store(0, own, total)


def gram_rows(fields, sums, count, first_plane, first_row):
    def one_row(r, carry):
        def store(c, spot, value):
            sums[first_row + r, c, spot] = value

        gram(fields, first_plane + r * 16, 16, store)
        return carry

    lax.fori_loop(0, count, one_row, 0)


def early_kernel(own, sums, *fields):
    _, run = unpacker(fields)
    run(own, 6, 0, 4)
    run(own, 11, 4, 4)
    gram_rows(fields, sums, 2, 0, 0)


def inner_kernel(own, rest, sums, *fields):
    _, run = unpacker(fields)
    run(own, 0, 0, 2)
    run(rest, 0, 2, 8)
    run(own, 2, 10, 2)
    gram_rows(fields, sums, 3, 0, 0)


def own_rows(kernel, count, *chunks):
    field = pltpu.VMEM((count * 16, WRAP, 128), jnp.float32)
    return pl.pallas_call(
        kernel,
        out_shape=jax.ShapeDtypeStruct((count, 2, PAIRS, 128), jnp.float32),
        scratch_shapes=[field] * 4,
        compiler_params=pltpu.CompilerParams(vmem_limit_bytes=(4 + 3 * count) << 20),
        cost_estimate=pl.CostEstimate(
            flops=3_000_000_000 * count, bytes_accessed=2_000_000, transcendentals=0
        ),
    )(*chunks)


def link_kernel(
    own, rest, above, below, early, inner, near, band, out,
    z_re, z_im, z_sum, z_dif, sums, tails, extra, cov, vec,
):
    fields = (z_re, z_im, z_sum, z_dif)
    lanes = lax.broadcasted_iota(jnp.int32, (8, 128), 1)
    put, run = unpacker(fields)
    run(above, 1, 0, 6)
    run(own, 4, 6, 2)
    run(own, 15, 8, 2)
    run(below, 0, 10, 6)
    for group in range(4):
        pieces = []
        for source in (2 * group, 2 * group + 1):
            mine = own[source, 10].astype(jnp.float32)
            others = rest[source, 8].astype(jnp.float32)
            up = above[source, 0].astype(jnp.float32)
            down = below[source, 6].astype(jnp.float32)
            piece = []
            for p in range(4):
                cut = slice(8 * p, 8 * p + 8)
                value = jnp.zeros((8, 128), jnp.float32)
                for part, turn, begin in (
                    (up, 128 - 30, 0),
                    (mine, 18, 18),
                    (others, 42, 42),
                    (mine, 42, 66),
                    (down, 90, 90),
                ):
                    value = jnp.where(lanes >= begin, pltpu.roll(part[cut], turn, 1), value)
                piece.append(jnp.where(lanes < 108, value, 0.0))
            pieces.append(piece)
        for p in range(4):
            put(64 + p, group, pieces[0][p], pieces[1][p])

    def store_tail(c, spot, value):
        tails[c, spot] = value

    gram(fields, 64, 4, store_tail)
    tails[1, 0:DATES] = jnp.zeros((DATES, 128), jnp.float32)
    gram_rows(fields, sums, 4, 0, 0)
    for c in range(2):
        high, low = split(tails[c])
        extra[c] = jnp.dot(
            jnp.concatenate([high, low], axis=1), band[...], preferred_element_type=jnp.float32
        )

    def windows(step, carry):
        size = 2 * DATES
        begin = pl.multiple_of(step * size, size)
        spot = pl.ds(begin, size)
        twice = pl.multiple_of(step * 2 * size, 2 * size)
        for c in range(2):
            rowsum = [sums[r, c, spot] for r in (0, 1)]
            rowsum += [early[0, c, spot]] + [inner[r, c, spot] for r in range(3)]
            rowsum += [early[1, c, spot]]
            rowsum += [sums[r, c, spot] for r in (2, 3)]
            pairs = [rowsum[r] + rowsum[r + 1] for r in range(8)]
            value = jnp.concatenate([pairs[a] + pairs[a + 2] for a in range(6)], axis=0)
            high, low = split(value)
            found = jnp.dot(
                jnp.concatenate([high, low], axis=1), near[...], preferred_element_type=jnp.float32
            )
            for a in range(6):
                full = found[a * size : (a + 1) * size] + extra[c, spot, a * 128 : a * 128 + 128]
                for i in range(2):
                    half = full[i * DATES : (i + 1) * DATES]
                    cov[a, c, pl.ds(twice + 2 * i * DATES, DATES)] = half
                    cov[a, c, pl.ds(twice + (2 * i + 1) * DATES, DATES)] = half
        return carry

    lax.fori_loop(0, (SHIFTS + 1) // 2, windows, 0)

    def put_vec(c, group, value):
        for copy in range(3):
            vec[c, copy * DATES + group * 8 : copy * DATES + group * 8 + 8] = value

    def window_row(a, carry):
        weights = []
        for group in range(4):
            power = cov[a, 0, 8 * group : 8 * group + 8]
            weights.append(1.0 / jnp.sqrt(power + BETA_LOAD))
            put_vec(0, group, weights[group])

        def iterate(real, last):
            found = []
            for group in range(4):
                row = 8 * group
                re_parts, im_parts = [], []
                for s in range(SHIFTS):
                    terms = [(2 * s * DATES + row, DATES + row + s, 1)]
                    if 0 < s < SHIFTS - 1:
                        terms.append((2 * s * DATES + DATES + row - s, DATES + row - s, -1))
                    for place, other, sign in terms:
                        cov_re = cov[a, 0, place : place + 8]
                        x_re = vec[0, other : other + 8]
                        x_im = None if real else vec[1, other : other + 8]
                        if s == 0:
                            re = cov_re * x_re
                            im = None if real else cov_re * x_im
                        else:
                            cov_im = cov[a, 1, place : place + 8]
                            re = cov_re * x_re
                            im = cov_im * x_re
                            if sign < 0:
                                im = -im if real else cov_re * x_im - im
                                re = re if real else re + cov_im * x_im
                            elif not real:
                                re = re - cov_im * x_im
                                im = im + cov_re * x_im
                        re_parts.append(re)
                        if im is not None:
                            im_parts.append(im)
                found.append((sum_two(re_parts), sum_two(im_parts)))
            for group in range(4):
                u_re = found[group][0] * weights[group]
                u_im = found[group][1] * weights[group]
                length = 1.0 / jnp.sqrt(u_re * u_re + u_im * u_im + PROJ_LOAD)
                x_re, x_im = u_re * length, u_im * length
                if last:
                    out[0, a, 8 * group : 8 * group + 8] = x_re
                    out[1, a, 8 * group : 8 * group + 8] = x_im
                else:
                    put_vec(0, group, x_re * weights[group])
                    put_vec(1, group, x_im * weights[group])

        iterate(True, False)
        lax.fori_loop(0, ITERS - 2, lambda i, carry: (iterate(False, False), carry)[1], 0)
        iterate(False, True)
        return carry

    lax.fori_loop(0, 6, window_row, 0)


def sum_two(parts):
    sums = parts[:2]
    for i, part in enumerate(parts[2:]):
        sums[i % 2] = sums[i % 2] + part
    return sums[0] + sums[1]


def tail_band():
    near = np.zeros((128, 128), np.float32)
    for block in range(128):
        near[block, max(block - 3, 0) : block + 1] = 1.0
    band = np.zeros((6, 128, 128), np.float32)
    for row in range(6):
        for line in range(4 * row, 4 * row + 16):
            for block in range(3):
                band[row, line * 3 + block, 125 + block :] = 1.0
    both = np.concatenate(list(band), axis=1)
    both = np.concatenate([both, both], axis=0).astype(jnp.bfloat16)
    return np.concatenate([near, near], axis=0).astype(jnp.bfloat16), both


def link_windows(own, rest, above, below, early, inner):
    field = pltpu.VMEM((68, WRAP, 128), jnp.float32)
    found = pl.pallas_call(
        link_kernel,
        out_shape=jax.ShapeDtypeStruct((2, 6, DATES, 128), jnp.float32),
        scratch_shapes=[field] * 4
        + [
            pltpu.VMEM((4, 2, PAIRS, 128), jnp.float32),
            pltpu.VMEM((2, PAIRS, 128), jnp.float32),
            pltpu.VMEM((2, PAIRS, 6 * 128), jnp.float32),
            pltpu.VMEM((6, 2, 2 * PAIRS, 128), jnp.float32),
            pltpu.VMEM((2, 3 * DATES, 128), jnp.float32),
        ],
        compiler_params=pltpu.CompilerParams(vmem_limit_bytes=28 << 20),
        cost_estimate=pl.CostEstimate(
            flops=20_000_000_000, bytes_accessed=8_000_000, transcendentals=0
        ),
        name="link_windows",
    )(own, rest, above, below, early, inner, *tail_band())
    return jnp.transpose(found, (0, 2, 1, 3))


def on_device(stack, range_filter, scatter_mask):
    def move(tiles):
        return lax.all_to_all(tiles, "dr", split_axis=0, concat_axis=0, tiled=True)

    tiles = filter_lines(stack, range_filter, scatter_mask, FIRST, 4)
    own = move(tiles)
    tiles = filter_lines(stack, range_filter, scatter_mask, SECOND, 8)
    rest = move(tiles)
    count = lax.axis_size("az")
    down = [(i, i + 1) for i in range(count - 1)]
    up = [(i + 1, i) for i in range(count - 1)]
    above = lax.ppermute(own[:, 10:17], "az", down)
    below = lax.ppermute(own[:, 4:11], "az", up)
    early = own_rows(early_kernel, 2, own)
    inner = own_rows(inner_kernel, 3, own, rest)
    return link_windows(own, rest, above, below, early, inner)


def solution(mesh):
    in_specs = (P(None, "dr", "az", None), P("dr", None), P("az", None))
    out_specs = P(None, None, "az", "dr")
    return jax.shard_map(
        on_device, mesh=mesh, in_specs=in_specs, out_specs=out_specs, check_vma=False
    )
```

```python
import math

import jax
import jax.numpy as jnp
import numpy as np
from jax import lax
from jax.experimental import pallas as pl
from jax.experimental.pallas import tpu as pltpu
from jax.sharding import PartitionSpec as P


ITERS = 4
BETA_LOAD = 1.0
PROJ_LOAD = 1.0

DATES = 32
RG = 4096
TILES = 8
HALO = 6
PLANES = 32
HERE = 4
FIRST, SECOND = (0, 16), (8,)
KEPT = (6, 7, 16, 17)
SHIFTS = 17
PAIRS = (SHIFTS + 1) * DATES
WRAP = 48


def slot_of(line):
    if 6 <= line < 18:
        return line - 6
    return line if line < 6 else line - 11


EARLY_TAIL, LATE_TAIL, SLOTS = 6, 12, 13


def tables():
    lane = np.arange(128)
    freq = 4 * (lane % 32) + lane // 32
    turn = 2.0 * np.pi / 128 * (np.outer(lane, freq) % 128)
    forward = np.block([[np.cos(turn), -np.sin(turn)], [np.sin(turn), np.cos(turn)]])
    turn = 2.0 * np.pi / 128 * (np.outer(freq, lane - HALO) % 128)
    inverse = np.block([[np.cos(turn), np.sin(turn)], [-np.sin(turn), np.cos(turn)]]) / RG
    plane = np.arange(PLANES)
    angle = 2.0 * np.pi / RG * np.outer(plane, lane)
    back = 2.0 * np.pi / RG * np.outer(plane, lane - HALO)
    parts = [forward[:, :128], forward[:, 128:], inverse[:, :128], inverse[:, 128:]]
    parts += [np.cos(angle), np.sin(angle), np.cos(back), np.sin(back)]
    return np.concatenate(parts, axis=0).astype(np.float32)


def cmul(value, cos, sin):
    re, im = value
    if abs(sin) < 1e-12:
        return (re, im) if cos > 0 else (-re, -im)
    if abs(cos) < 1e-12:
        return (-im, re) if sin > 0 else (im, -re)
    if abs(abs(cos) - abs(sin)) < 1e-12:
        size = abs(cos)
        if cos > 0 and sin > 0:
            return ((re - im) * size, (re + im) * size)
        if cos > 0:
            return ((re + im) * size, (im - re) * size)
        if sin > 0:
            return ((-re - im) * size, (re - im) * size)
        return ((im - re) * size, (-re - im) * size)
    return (re * cos - im * sin, im * cos + re * sin)


def small_dft(values, sign):
    count = len(values)
    if count == 1:
        return values
    even = small_dft(values[0::2], sign)
    odd = small_dft(values[1::2], sign)
    half = count // 2
    low, high = [], []
    for k in range(half):
        angle = sign * 2.0 * math.pi * k / count
        re, im = cmul(odd[k], math.cos(angle), math.sin(angle))
        low.append((even[k][0] + re, even[k][1] + im))
        high.append((even[k][0] - re, even[k][1] - im))
    return low + high


def dft_planes(load, hold, store, sign):
    for m in range(8):
        parts = small_dft([load(8 * i + m) for i in range(4)], sign)
        for s in range(4):
            angle = sign * 2.0 * math.pi * m * s / 32
            re, im = cmul(parts[s], math.cos(angle), math.sin(angle))
            hold[0, s * 8 + m] = re
            hold[1, s * 8 + m] = im
    for s in range(4):
        parts = small_dft([(hold[0, s * 8 + m], hold[1, s * 8 + m]) for m in range(8)], sign)
        for u in range(8):
            store(s + 4 * u, *parts[u])


def split(values):
    high = values.astype(jnp.bfloat16)
    return high, (values - high.astype(jnp.float32)).astype(jnp.bfloat16)


def dot3(values, table):
    high, low = split(values)
    return jnp.dot(
        jnp.concatenate([high, low, high], axis=1), table, preferred_element_type=jnp.float32
    )


def filter_kernel(
    blocks, group, stack, gains, mask, table, kept, out,
    raw, gains_in, mask_in, table_in, sem,
    spec, first, hold, held, gain, weights, lines_out, forward, inverse, place,
):
    count = len(blocks)
    lines_here = 8 * count
    rows_here = HERE * lines_here
    pitch = lines_here + 1
    early = blocks == FIRST
    stack_copies = []
    for d in range(HERE):
        for i, block in enumerate(blocks):
            for c in range(2):
                stack_copies.append(
                    pltpu.make_async_copy(
                        stack.at[c, d, pl.ds(block, 8)],
                        raw.at[c, d * count + i],
                        sem.at[c * HERE * count + d * count + i],
                    )
                )
    copies = {}
    for i, (name, source, target) in enumerate(
        (("table", table, table_in), ("gains", gains, gains_in))
    ):
        copies[name] = pltpu.make_async_copy(source, target, sem.at[9 * count + i])
    for i, block in enumerate(blocks):
        copies["mask", i] = pltpu.make_async_copy(
            mask.at[pl.ds(block, 8)], mask_in.at[pl.ds(8 * i, 8)], sem.at[8 * count + i]
        )
    for copy in stack_copies + list(copies.values()):
        copy.start()
    lanes = lax.broadcasted_iota(jnp.int32, (8, 128), 1)

    def ahead(block, carry):
        rows = pl.ds(pl.multiple_of(block * 8, 8), 8)

        def store(q, re, im):
            spec[0, q, rows] = re
            spec[1, q, rows] = im

        for c in range(2):
            pltpu.make_async_copy(
                stack.at[0, 0, pl.ds(0, 8)], raw.at[c, block], sem.at[c * HERE * count + block]
            ).wait()

        def load(n):
            lanes = slice(n * 128, (n + 1) * 128)
            return (
                raw[0, block, :, lanes].astype(jnp.float32),
                raw[1, block, :, lanes].astype(jnp.float32),
            )

        dft_planes(load, hold, store, -1)
        return carry

    lax.fori_loop(0, rows_here // 8, ahead, 0)
    copies["gains"].wait()
    for n in range(PLANES):
        four = gains_in[:, n * 128 : (n + 1) * 128]
        for d in range(HERE):
            gain[d, n : n + 1] = four[d : d + 1]
    for d in range(HERE):
        turned = jnp.transpose(gain[d])
        gain[d] = jnp.concatenate([turned[32 * w : 32 * w + 32] for w in range(4)], axis=1)
    steps = PLANES // group
    copies["table"].wait()
    for i, target in enumerate((forward, inverse)):
        for half in range(2):
            begin = 256 * (2 * i + half)
            high, low = split(table_in[begin : begin + 256])
            for j, part in enumerate((high, high, low)):
                target[256 * j : 256 * j + 256, 128 * half : 128 * half + 128] = part
    row = lax.broadcasted_iota(jnp.int32, (512, 128), 0)
    column = lax.broadcasted_iota(jnp.int32, (512, 128), 1)
    for p in range(4):
        place[:, 128 * p : 128 * p + 128] = jnp.where(row == 4 * column + p, 1.0, 0.0).astype(
            jnp.bfloat16
        )

    def middle(step, carry):
        now = jnp.minimum(step, steps - 1) * group
        past = jnp.maximum(step - 1, 0) * group
        parts = []
        for i in range(group):
            tc = table_in[pl.ds(1024 + now + i, 1), :]
            ts = table_in[pl.ds(1056 + now + i, 1), :]
            re, im = spec[0, now + i], spec[1, now + i]
            parts.append(jnp.concatenate([re * tc + im * ts, im * tc - re * ts], axis=1))
        back = dot3(held[lax.rem(step + 1, 2)], inverse[...])
        found = dot3(jnp.concatenate(parts, axis=0), forward[...])
        for i in range(group):
            for d in range(HERE):
                row = gain[d, pl.ds(now + i, 1), :]
                begin = i * rows_here + d * lines_here
                held[lax.rem(step, 2), begin : begin + lines_here] = found[
                    begin : begin + lines_here
                ] * jnp.concatenate([row, row], axis=1)
        for i in range(group):
            tc = table_in[pl.ds(1088 + past + i, 1), :]
            ts = table_in[pl.ds(1120 + past + i, 1), :]
            re = back[i * rows_here : (i + 1) * rows_here, :128]
            im = back[i * rows_here : (i + 1) * rows_here, 128:]
            first[0, past + i] = re * tc - im * ts
            first[1, past + i] = im * tc + re * ts
        return carry

    lax.fori_loop(0, steps + 1, middle, 0)

    for i in range(count):
        copies["mask", i].wait()
        rows = slice(8 * i, 8 * i + 8)
        before = pltpu.roll(mask_in[rows, RG - 128 :].astype(jnp.float32), HALO, 1)
        for n in range(PLANES):
            now = pltpu.roll(mask_in[rows, n * 128 : (n + 1) * 128].astype(jnp.float32), HALO, 1)
            joined = jnp.where(lanes < HALO, before, now)
            if n == 0:
                weights[PLANES, rows] = jnp.where(lanes < HALO, joined, 0.0)
                joined = jnp.where(lanes < HALO, 0.0, joined)
            weights[n, rows] = joined
            before = now

    def behind(block, carry):
        rows = pl.ds(pl.multiple_of(block * 8, 8), 8)
        begin = (block // count) * pitch + lax.rem(block, count) * 8
        to_re = pl.ds(begin, 8)
        to_im = pl.ds(begin + HERE * pitch, 8)
        lines = pl.ds(pl.multiple_of(lax.rem(block, count) * 8, 8), 8)

        def store(n, re, im):
            weight = weights[n, lines]
            lines_out[n, to_re] = re * weight
            lines_out[n, to_im] = im * weight
            if n == 0:
                weight = weights[PLANES, lines]
                lines_out[PLANES, to_re] = re * weight
                lines_out[PLANES, to_im] = im * weight

        dft_planes(lambda q: (first[0, q, rows], first[1, q, rows]), hold, store, 1)
        return carry

    lax.fori_loop(0, rows_here // 8, behind, 0)

    def gather(plane):
        return jnp.concatenate(
            [lines_out[plane, pl.ds(line, 8, stride=pitch), :] for line in range(lines_here)],
            axis=0,
        )

    def put_tail(slot, found):
        tails = []
        for p in range(4):
            tail = jnp.zeros((8, 128), jnp.float32)
            for line in range(lines_here):
                part = found[line * 8 : line * 8 + 8, p * 128 : p * 128 + 128]
                if line:
                    part = pltpu.roll(part, 3 * line, 1)
                tail = jnp.where(lanes >= 3 * line, part, tail)
            tails.append(jnp.where(lanes < 3 * lines_here, tail, 0.0))
        out[slot, EARLY_TAIL if early else LATE_TAIL] = jnp.concatenate(tails, axis=0).astype(
            jnp.bfloat16
        )

    def one_tile(t):
        left = jnp.concatenate([gather(4 * t + v) for v in range(4)], axis=1).astype(jnp.bfloat16)
        found = jnp.dot(left, place[...], preferred_element_type=jnp.float32)
        for index in range(lines_here):
            line = blocks[index // 8] + index % 8
            value = jnp.concatenate(
                [found[index * 8 : index * 8 + 8, p * 128 : p * 128 + 128] for p in range(4)],
                axis=0,
            ).astype(jnp.bfloat16)
            if early and line in KEPT:
                kept[t, KEPT.index(line)] = value
            else:
                out[t, slot_of(line)] = value
        if not early:
            for index, line in enumerate(KEPT):
                out[t, slot_of(line)] = kept[t, index]
        put_tail(lax.rem(t + TILES - 1, TILES), found)

    def tile(step, carry):
        one_tile(2 * step)
        one_tile(2 * step + 1)
        return carry

    lax.fori_loop(0, TILES // 2, tile, 0)
    found = jnp.dot(
        gather(PLANES).astype(jnp.bfloat16), place[:128], preferred_element_type=jnp.float32
    )
    put_tail(TILES - 1, found)


def filter_lines(stack, gains, mask, blocks, group, kept=None):
    count = len(blocks)
    tiles = jax.ShapeDtypeStruct((TILES, SLOTS, 32, 128), jnp.bfloat16)
    rest = jax.ShapeDtypeStruct((TILES, len(KEPT), 32, 128), jnp.bfloat16)
    hbm = pl.BlockSpec(memory_space=pltpu.MemorySpace.HBM)
    vmem = pl.BlockSpec(memory_space=pltpu.MemorySpace.VMEM)

    def kernel(*refs):
        if blocks == FIRST:
            refs = refs[:4] + (refs[5], refs[4]) + refs[6:]
        filter_kernel(blocks, group, *refs)

    rows = HERE * 8 * count
    return pl.pallas_call(
        kernel,
        out_shape=(tiles, rest) if blocks == FIRST else tiles,
        in_specs=[hbm] * 4 + ([] if blocks == FIRST else [vmem]),
        scratch_shapes=[
            pltpu.VMEM((2, HERE * count, 8, RG), jnp.bfloat16),
            pltpu.VMEM((HERE, RG), jnp.float32),
            pltpu.VMEM((8 * count, RG), jnp.int32),
            pltpu.VMEM((1152, 128), jnp.float32),
            pltpu.SemaphoreType.DMA((9 * count + 2,)),
            pltpu.VMEM((2, PLANES, rows, 128), jnp.float32),
            pltpu.VMEM((2, PLANES, rows, 128), jnp.float32),
            pltpu.VMEM((2, PLANES, 8, 128), jnp.float32),
            pltpu.VMEM((2, group * rows, 256), jnp.float32),
            pltpu.VMEM((HERE, PLANES, 128), jnp.float32),
            pltpu.VMEM((PLANES + 1, 8 * count, 128), jnp.float32),
            pltpu.VMEM((PLANES + 1, 2 * rows + 2 * HERE, 128), jnp.float32),
            pltpu.VMEM((768, 256), jnp.bfloat16),
            pltpu.VMEM((768, 256), jnp.bfloat16),
            pltpu.VMEM((512, 512), jnp.bfloat16),
        ],
        compiler_params=pltpu.CompilerParams(vmem_limit_bytes=65_700_000),
        cost_estimate=pl.CostEstimate(
            flops=2_000_000_000 * count, bytes_accessed=2_000_000, transcendentals=0
        ),
    )(stack, gains, mask, tables(), *(() if kept is None else (kept,)))


def unpacker(fields):
    z_re, z_im, z_sum, z_dif = fields
    rows = lax.broadcasted_iota(jnp.int32, (8, 128), 0)
    low = rows < 4

    def put(plane, group, first, second):
        re = jnp.where(low, first, pltpu.roll(second, 4, 0))
        im = jnp.where(low, pltpu.roll(first, 4, 0), second)
        total, change = re + im, im - re
        z_im[plane, 8 * group : 8 * group + 8] = im
        for begin in [8 * group] + ([32 + 8 * group] if group < 2 else []):
            z_re[plane, begin : begin + 8] = re
            z_sum[plane, begin : begin + 8] = total
            z_dif[plane, begin : begin + 8] = change

    def run(ref, slot, line, count):
        def step(i, carry):
            for group in range(4):
                first = ref[2 * group, slot + i].astype(jnp.float32)
                second = ref[2 * group + 1, slot + i].astype(jnp.float32)
                for p in range(4):
                    cut = slice(8 * p, 8 * p + 8)
                    put((line + i) * 4 + p, group, first[cut], second[cut])
            return carry

        lax.fori_loop(0, count, step, 0)

    return put, run


WIDTH = 8


def gram(fields, base, count, store):
    z_re, z_im, z_sum, z_dif = fields

    def block(index, carry):
        group = index // 2
        own = pl.ds(pl.multiple_of(group * 8, 8), 8)
        begin = pl.multiple_of(group * 8 + lax.rem(index, 2) * 8, 8)
        unit = min(8, count)

        def some(chunk, totals):
            totals = [list(totals[3 * i : 3 * i + 3]) for i in range(WIDTH)]
            for step in range(unit):
                plane = base + chunk * unit + step
                mine = (z_sum[plane, own], z_re[plane, own], z_im[plane, own])
                for i in range(WIDTH):
                    other = pl.ds(begin + 1 + i, 8)
                    others = (z_re[plane, other], z_sum[plane, other], z_dif[plane, other])
                    for k in range(3):
                        totals[i][k] = totals[i][k] + others[k] * mine[k]
            return tuple(t for total in totals for t in total)

        zero = jnp.zeros((8, 128), jnp.float32)
        totals = lax.fori_loop(0, count // unit, some, (zero,) * (3 * WIDTH))
        totals = [totals[3 * i : 3 * i + 3] for i in range(WIDTH)]
        for i in range(WIDTH):
            one, two, three = totals[i]
            spot = (lax.rem(index, 2) * 8 + 1 + i) * DATES + group * 8
            spot = pl.ds(pl.multiple_of(spot, 8), 8)
            store(0, spot, one + three)
            store(1, spot, one - two)
        return carry

    lax.fori_loop(0, 8, block, 0)
    for group in range(4):
        own = slice(8 * group, 8 * group + 8)
        total = None
        for step in range(count):
            re, im = z_re[base + step, own], z_im[base + step, own]
            term = re * re + im * im
            total = term if total is None else total + term
        store(0, own, total)


def gram_rows(fields, sums, count, first_plane, first_row):
    def one_row(r, carry):
        def store(c, spot, value):
            sums[first_row + r, c, spot] = value

        gram(fields, first_plane + r * 16, 16, store)
        return carry

    lax.fori_loop(0, count, one_row, 0)


def early_kernel(own, sums, *fields):
    _, run = unpacker(fields)
    run(own, 2, 0, 4)
    run(own, 7, 4, 4)
    gram_rows(fields, sums, 2, 0, 0)


def inner_kernel(rest, sums, *fields):
    _, run = unpacker(fields)
    run(rest, 0, 0, 12)
    gram_rows(fields, sums, 3, 0, 0)


def own_rows(kernel, count, *chunks):
    field = pltpu.VMEM((count * 16, WRAP, 128), jnp.float32)
    return pl.pallas_call(
        kernel,
        out_shape=jax.ShapeDtypeStruct((count, 2, PAIRS, 128), jnp.float32),
        scratch_shapes=[field] * 4,
        compiler_params=pltpu.CompilerParams(vmem_limit_bytes=(4 + 3 * count) << 20),
        cost_estimate=pl.CostEstimate(
            flops=3_000_000_000 * count, bytes_accessed=2_000_000, transcendentals=0
        ),
    )(*chunks)


def link_kernel(
    own, rest, above, below, early, inner, near, band, out,
    z_re, z_im, z_sum, z_dif, sums, tails, extra, cov, vec,
):
    fields = (z_re, z_im, z_sum, z_dif)
    lanes = lax.broadcasted_iota(jnp.int32, (8, 128), 1)
    put, run = unpacker(fields)
    run(above, 1, 0, 6)
    run(own, 0, 6, 2)
    run(own, 11, 8, 2)
    run(below, 0, 10, 6)
    for group in range(4):
        pieces = []
        for source in (2 * group, 2 * group + 1):
            mine = own[source, EARLY_TAIL].astype(jnp.float32)
            others = rest[source, LATE_TAIL].astype(jnp.float32)
            up = above[source, 0].astype(jnp.float32)
            down = below[source, 6].astype(jnp.float32)
            piece = []
            for p in range(4):
                cut = slice(8 * p, 8 * p + 8)
                value = jnp.zeros((8, 128), jnp.float32)
                for part, turn, begin in (
                    (up, 128 - 30, 0),
                    (mine, 18, 18),
                    (others, 42, 42),
                    (mine, 42, 66),
                    (down, 90, 90),
                ):
                    value = jnp.where(lanes >= begin, pltpu.roll(part[cut], turn, 1), value)
                piece.append(jnp.where(lanes < 108, value, 0.0))
            pieces.append(piece)
        for p in range(4):
            put(64 + p, group, pieces[0][p], pieces[1][p])

    def store_tail(c, spot, value):
        tails[c, spot] = value

    gram(fields, 64, 4, store_tail)
    tails[1, 0:DATES] = jnp.zeros((DATES, 128), jnp.float32)
    gram_rows(fields, sums, 4, 0, 0)
    for c in range(2):
        high, low = split(tails[c])
        extra[c] = jnp.dot(
            jnp.concatenate([high, low], axis=1), band[...], preferred_element_type=jnp.float32
        )

    def windows(step, carry):
        size = 2 * DATES
        begin = pl.multiple_of(step * size, size)
        spot = pl.ds(begin, size)
        twice = pl.multiple_of(step * 2 * size, 2 * size)
        for c in range(2):
            rowsum = [sums[r, c, spot] for r in (0, 1)]
            rowsum += [early[0, c, spot]] + [inner[r, c, spot] for r in range(3)]
            rowsum += [early[1, c, spot]]
            rowsum += [sums[r, c, spot] for r in (2, 3)]
            pairs = [rowsum[r] + rowsum[r + 1] for r in range(8)]
            value = jnp.concatenate([pairs[a] + pairs[a + 2] for a in range(6)], axis=0)
            high, low = split(value)
            found = jnp.dot(
                jnp.concatenate([high, low], axis=1), near[...], preferred_element_type=jnp.float32
            )
            for a in range(6):
                full = found[a * size : (a + 1) * size] + extra[c, spot, a * 128 : a * 128 + 128]
                for i in range(2):
                    half = full[i * DATES : (i + 1) * DATES]
                    cov[a, c, pl.ds(twice + 2 * i * DATES, DATES)] = half
                    cov[a, c, pl.ds(twice + (2 * i + 1) * DATES, DATES)] = half
        return carry

    lax.fori_loop(0, (SHIFTS + 1) // 2, windows, 0)

    def put_vec(c, group, value):
        for copy in range(3):
            vec[c, copy * DATES + group * 8 : copy * DATES + group * 8 + 8] = value

    def window_row(a, carry):
        weights = []
        for group in range(4):
            power = cov[a, 0, 8 * group : 8 * group + 8]
            weights.append(1.0 / jnp.sqrt(power + BETA_LOAD))
            put_vec(0, group, weights[group])

        def iterate(real, last):
            found = []
            for group in range(4):
                row = 8 * group
                re_parts, im_parts = [], []
                for s in range(SHIFTS):
                    terms = [(2 * s * DATES + row, DATES + row + s, 1)]
                    if 0 < s < SHIFTS - 1:
                        terms.append((2 * s * DATES + DATES + row - s, DATES + row - s, -1))
                    for place, other, sign in terms:
                        cov_re = cov[a, 0, place : place + 8]
                        x_re = vec[0, other : other + 8]
                        x_im = None if real else vec[1, other : other + 8]
                        if s == 0:
                            re = cov_re * x_re
                            im = None if real else cov_re * x_im
                        else:
                            cov_im = cov[a, 1, place : place + 8]
                            re = cov_re * x_re
                            im = cov_im * x_re
                            if sign < 0:
                                im = -im if real else cov_re * x_im - im
                                re = re if real else re + cov_im * x_im
                            elif not real:
                                re = re - cov_im * x_im
                                im = im + cov_re * x_im
                        re_parts.append(re)
                        if im is not None:
                            im_parts.append(im)
                found.append((sum_two(re_parts), sum_two(im_parts)))
            for group in range(4):
                u_re = found[group][0] * weights[group]
                u_im = found[group][1] * weights[group]
                length = 1.0 / jnp.sqrt(u_re * u_re + u_im * u_im + PROJ_LOAD)
                x_re, x_im = u_re * length, u_im * length
                if last:
                    out[0, a, 8 * group : 8 * group + 8] = x_re
                    out[1, a, 8 * group : 8 * group + 8] = x_im
                else:
                    put_vec(0, group, x_re * weights[group])
                    put_vec(1, group, x_im * weights[group])

        iterate(True, False)
        lax.fori_loop(0, ITERS - 2, lambda i, carry: (iterate(False, False), carry)[1], 0)
        iterate(False, True)
        return carry

    lax.fori_loop(0, 6, window_row, 0)


def sum_two(parts):
    sums = parts[:2]
    for i, part in enumerate(parts[2:]):
        sums[i % 2] = sums[i % 2] + part
    return sums[0] + sums[1]


def tail_band():
    near = np.zeros((128, 128), np.float32)
    for block in range(128):
        near[block, max(block - 3, 0) : block + 1] = 1.0
    band = np.zeros((6, 128, 128), np.float32)
    for row in range(6):
        for line in range(4 * row, 4 * row + 16):
            for block in range(3):
                band[row, line * 3 + block, 125 + block :] = 1.0
    both = np.concatenate(list(band), axis=1)
    both = np.concatenate([both, both], axis=0).astype(jnp.bfloat16)
    return np.concatenate([near, near], axis=0).astype(jnp.bfloat16), both


def link_windows(own, rest, above, below, early, inner):
    field = pltpu.VMEM((68, WRAP, 128), jnp.float32)
    found = pl.pallas_call(
        link_kernel,
        out_shape=jax.ShapeDtypeStruct((2, 6, DATES, 128), jnp.float32),
        scratch_shapes=[field] * 4
        + [
            pltpu.VMEM((4, 2, PAIRS, 128), jnp.float32),
            pltpu.VMEM((2, PAIRS, 128), jnp.float32),
            pltpu.VMEM((2, PAIRS, 6 * 128), jnp.float32),
            pltpu.VMEM((6, 2, 2 * PAIRS, 128), jnp.float32),
            pltpu.VMEM((2, 3 * DATES, 128), jnp.float32),
        ],
        compiler_params=pltpu.CompilerParams(vmem_limit_bytes=28 << 20),
        cost_estimate=pl.CostEstimate(
            flops=20_000_000_000, bytes_accessed=8_000_000, transcendentals=0
        ),
        name="link_windows",
    )(own, rest, above, below, early, inner, *tail_band())
    return jnp.transpose(found, (0, 2, 1, 3))


def on_device(stack, range_filter, scatter_mask):
    def move(tiles):
        return lax.all_to_all(tiles, "dr", split_axis=0, concat_axis=0, tiled=True)

    tiles, kept = filter_lines(stack, range_filter, scatter_mask, FIRST, 4)
    own = move(tiles)
    tiles = filter_lines(stack, range_filter, scatter_mask, SECOND, 8, kept)
    rest = move(tiles)
    count = lax.axis_size("az")
    down = [(i, i + 1) for i in range(count - 1)]
    up = [(i + 1, i) for i in range(count - 1)]
    above = lax.ppermute(own[:, 6:13], "az", down)
    below = lax.ppermute(own[:, 0:7], "az", up)
    early = own_rows(early_kernel, 2, own)
    inner = own_rows(inner_kernel, 3, rest)
    return link_windows(own, rest, above, below, early, inner)


def solution(mesh):
    in_specs = (P(None, "dr", "az", None), P("dr", None), P("az", None))
    out_specs = P(None, None, "az", "dr")
    return jax.shard_map(
        on_device, mesh=mesh, in_specs=in_specs, out_specs=out_specs, check_vma=False
    )
```

```python
import math

import jax
import jax.numpy as jnp
import numpy as np
from jax import lax
from jax.experimental import pallas as pl
from jax.experimental.pallas import tpu as pltpu
from jax.sharding import PartitionSpec as P


ITERS = 4
BETA_LOAD = 1.0
PROJ_LOAD = 1.0

DATES = 32
RG = 4096
TILES = 8
HALO = 6
PLANES = 32
HERE = 4
FIRST, SECOND = (0, 16), (8,)
KEPT = (6, 7, 16, 17)
SHIFTS = 17
PAIRS = (SHIFTS + 1) * DATES
WRAP = 48


def slot_of(line):
    if 6 <= line < 18:
        return line - 6
    return line if line < 6 else line - 11


EARLY_TAIL, LATE_TAIL, SLOTS = 6, 12, 13


def tables():
    lane = np.arange(128)
    freq = 4 * (lane % 32) + lane // 32
    turn = 2.0 * np.pi / 128 * (np.outer(lane, freq) % 128)
    forward = np.block([[np.cos(turn), -np.sin(turn)], [np.sin(turn), np.cos(turn)]])
    turn = 2.0 * np.pi / 128 * (np.outer(freq, lane - HALO) % 128)
    inverse = np.block([[np.cos(turn), np.sin(turn)], [-np.sin(turn), np.cos(turn)]]) / RG
    plane = np.arange(PLANES)
    angle = 2.0 * np.pi / RG * np.outer(plane, lane)
    back = 2.0 * np.pi / RG * np.outer(plane, lane - HALO)
    parts = [forward[:, :128], forward[:, 128:], inverse[:, :128], inverse[:, 128:]]
    parts += [np.cos(angle), np.sin(angle), np.cos(back), np.sin(back)]
    return np.concatenate(parts, axis=0).astype(np.float32)


def cmul(value, cos, sin):
    re, im = value
    if abs(sin) < 1e-12:
        return (re, im) if cos > 0 else (-re, -im)
    if abs(cos) < 1e-12:
        return (-im, re) if sin > 0 else (im, -re)
    if abs(abs(cos) - abs(sin)) < 1e-12:
        size = abs(cos)
        if cos > 0 and sin > 0:
            return ((re - im) * size, (re + im) * size)
        if cos > 0:
            return ((re + im) * size, (im - re) * size)
        if sin > 0:
            return ((-re - im) * size, (re - im) * size)
        return ((im - re) * size, (-re - im) * size)
    return (re * cos - im * sin, im * cos + re * sin)


def small_dft(values, sign):
    count = len(values)
    if count == 1:
        return values
    even = small_dft(values[0::2], sign)
    odd = small_dft(values[1::2], sign)
    half = count // 2
    low, high = [], []
    for k in range(half):
        angle = sign * 2.0 * math.pi * k / count
        re, im = cmul(odd[k], math.cos(angle), math.sin(angle))
        low.append((even[k][0] + re, even[k][1] + im))
        high.append((even[k][0] - re, even[k][1] - im))
    return low + high


def dft_planes(load, hold, store, sign):
    for m in range(8):
        parts = small_dft([load(8 * i + m) for i in range(4)], sign)
        for s in range(4):
            angle = sign * 2.0 * math.pi * m * s / 32
            re, im = cmul(parts[s], math.cos(angle), math.sin(angle))
            hold[0, s * 8 + m] = re
            hold[1, s * 8 + m] = im
    for s in range(4):
        parts = small_dft([(hold[0, s * 8 + m], hold[1, s * 8 + m]) for m in range(8)], sign)
        for u in range(8):
            store(s + 4 * u, *parts[u])


def split(values):
    high = values.astype(jnp.bfloat16)
    return high, (values - high.astype(jnp.float32)).astype(jnp.bfloat16)


def dot3(values, table):
    high, low = split(values)
    return jnp.dot(
        jnp.concatenate([high, low, high], axis=1), table, preferred_element_type=jnp.float32
    )


def filter_kernel(
    blocks, group, stack, gains, mask, table, kept, out,
    raw, gains_in, mask_in, table_in, sem,
    spec, first, hold, held, gain, weights, lines_out, forward, inverse, place,
):
    count = len(blocks)
    lines_here = 8 * count
    rows_here = HERE * lines_here
    pitch = lines_here + 1
    early = blocks == FIRST
    stack_copies = []
    for d in range(HERE):
        for i, block in enumerate(blocks):
            for c in range(2):
                stack_copies.append(
                    pltpu.make_async_copy(
                        stack.at[c, d, pl.ds(block, 8)],
                        raw.at[c, d * count + i],
                        sem.at[c * HERE * count + d * count + i],
                    )
                )
    copies = {}
    for i, (name, source, target) in enumerate(
        (("table", table, table_in), ("gains", gains, gains_in))
    ):
        copies[name] = pltpu.make_async_copy(source, target, sem.at[9 * count + i])
    for i, block in enumerate(blocks):
        copies["mask", i] = pltpu.make_async_copy(
            mask.at[pl.ds(block, 8)], mask_in.at[pl.ds(8 * i, 8)], sem.at[8 * count + i]
        )
    for copy in stack_copies + list(copies.values()):
        copy.start()
    lanes = lax.broadcasted_iota(jnp.int32, (8, 128), 1)

    def ahead(block, carry):
        rows = pl.ds(pl.multiple_of(block * 8, 8), 8)

        def store(q, re, im):
            spec[0, q, rows] = re
            spec[1, q, rows] = im

        for c in range(2):
            pltpu.make_async_copy(
                stack.at[0, 0, pl.ds(0, 8)], raw.at[c, block], sem.at[c * HERE * count + block]
            ).wait()

        def load(n):
            lanes = slice(n * 128, (n + 1) * 128)
            return (
                raw[0, block, :, lanes].astype(jnp.float32),
                raw[1, block, :, lanes].astype(jnp.float32),
            )

        dft_planes(load, hold, store, -1)
        return carry

    lax.fori_loop(0, rows_here // 8, ahead, 0)
    copies["gains"].wait()
    for n in range(PLANES):
        four = gains_in[:, n * 128 : (n + 1) * 128]
        for d in range(HERE):
            gain[d, n : n + 1] = four[d : d + 1]
    for d in range(HERE):
        turned = jnp.transpose(gain[d])
        gain[d] = jnp.concatenate([turned[32 * w : 32 * w + 32] for w in range(4)], axis=1)
    steps = PLANES // group
    copies["table"].wait()
    for i, target in enumerate((forward, inverse)):
        for half in range(2):
            begin = 256 * (2 * i + half)
            high, low = split(table_in[begin : begin + 256])
            for j, part in enumerate((high, high, low)):
                target[256 * j : 256 * j + 256, 128 * half : 128 * half + 128] = part
    row = lax.broadcasted_iota(jnp.int32, (512, 128), 0)
    column = lax.broadcasted_iota(jnp.int32, (512, 128), 1)
    for p in range(4):
        place[:, 128 * p : 128 * p + 128] = jnp.where(row == 4 * column + p, 1.0, 0.0).astype(
            jnp.bfloat16
        )

    def middle(step, carry):
        now = jnp.minimum(step, steps - 1) * group
        past = jnp.maximum(step - 1, 0) * group
        parts = []
        for i in range(group):
            tc = table_in[pl.ds(1024 + now + i, 1), :]
            ts = table_in[pl.ds(1056 + now + i, 1), :]
            re, im = spec[0, now + i], spec[1, now + i]
            parts.append(jnp.concatenate([re * tc + im * ts, im * tc - re * ts], axis=1))
        back = dot3(held[lax.rem(step + 1, 2)], inverse[...])
        found = dot3(jnp.concatenate(parts, axis=0), forward[...])
        for i in range(group):
            for d in range(HERE):
                row = gain[d, pl.ds(now + i, 1), :]
                begin = i * rows_here + d * lines_here
                held[lax.rem(step, 2), begin : begin + lines_here] = found[
                    begin : begin + lines_here
                ] * jnp.concatenate([row, row], axis=1)
        for i in range(group):
            tc = table_in[pl.ds(1088 + past + i, 1), :]
            ts = table_in[pl.ds(1120 + past + i, 1), :]
            re = back[i * rows_here : (i + 1) * rows_here, :128]
            im = back[i * rows_here : (i + 1) * rows_here, 128:]
            first[0, past + i] = re * tc - im * ts
            first[1, past + i] = im * tc + re * ts
        return carry

    lax.fori_loop(0, steps + 1, middle, 0)

    for i in range(count):
        copies["mask", i].wait()
        rows = slice(8 * i, 8 * i + 8)
        before = pltpu.roll(mask_in[rows, RG - 128 :].astype(jnp.float32), HALO, 1)
        for n in range(PLANES):
            now = pltpu.roll(mask_in[rows, n * 128 : (n + 1) * 128].astype(jnp.float32), HALO, 1)
            joined = jnp.where(lanes < HALO, before, now)
            if n == 0:
                weights[PLANES, rows] = jnp.where(lanes < HALO, joined, 0.0)
                joined = jnp.where(lanes < HALO, 0.0, joined)
            weights[n, rows] = joined
            before = now

    def behind(block, carry):
        rows = pl.ds(pl.multiple_of(block * 8, 8), 8)
        begin = (block // count) * pitch + lax.rem(block, count) * 8
        to_re = pl.ds(begin, 8)
        to_im = pl.ds(begin + HERE * pitch, 8)
        lines = pl.ds(pl.multiple_of(lax.rem(block, count) * 8, 8), 8)

        def store(n, re, im):
            weight = weights[n, lines]
            lines_out[n, to_re] = re * weight
            lines_out[n, to_im] = im * weight
            if n == 0:
                weight = weights[PLANES, lines]
                lines_out[PLANES, to_re] = re * weight
                lines_out[PLANES, to_im] = im * weight

        dft_planes(lambda q: (first[0, q, rows], first[1, q, rows]), hold, store, 1)
        return carry

    lax.fori_loop(0, rows_here // 8, behind, 0)

    def gather(plane):
        return jnp.concatenate(
            [lines_out[plane, pl.ds(line, 8, stride=pitch), :] for line in range(lines_here)],
            axis=0,
        )

    def put_tail(slot, found):
        tails = []
        for p in range(4):
            tail = jnp.zeros((8, 128), jnp.float32)
            for line in range(lines_here):
                part = found[line * 8 : line * 8 + 8, p * 128 : p * 128 + 128]
                if line:
                    part = pltpu.roll(part, 3 * line, 1)
                tail = jnp.where(lanes >= 3 * line, part, tail)
            tails.append(jnp.where(lanes < 3 * lines_here, tail, 0.0))
        out[slot, EARLY_TAIL if early else LATE_TAIL] = jnp.concatenate(tails, axis=0).astype(
            jnp.bfloat16
        )

    def one_tile(t):
        left = jnp.concatenate([gather(4 * t + v) for v in range(4)], axis=1).astype(jnp.bfloat16)
        found = jnp.dot(left, place[...], preferred_element_type=jnp.float32)
        for index in range(lines_here):
            line = blocks[index // 8] + index % 8
            value = jnp.concatenate(
                [found[index * 8 : index * 8 + 8, p * 128 : p * 128 + 128] for p in range(4)],
                axis=0,
            ).astype(jnp.bfloat16)
            if early and line in KEPT:
                kept[t, KEPT.index(line)] = value
            else:
                out[t, slot_of(line)] = value
        if not early:
            for index, line in enumerate(KEPT):
                out[t, slot_of(line)] = kept[t, index]
        put_tail(lax.rem(t + TILES - 1, TILES), found)

    def tile(step, carry):
        one_tile(2 * step)
        one_tile(2 * step + 1)
        return carry

    lax.fori_loop(0, TILES // 2, tile, 0)
    found = jnp.dot(
        gather(PLANES).astype(jnp.bfloat16), place[:128], preferred_element_type=jnp.float32
    )
    put_tail(TILES - 1, found)


def filter_lines(stack, gains, mask, blocks, group, kept=None):
    count = len(blocks)
    tiles = jax.ShapeDtypeStruct((TILES, SLOTS, 32, 128), jnp.bfloat16)
    rest = jax.ShapeDtypeStruct((TILES, len(KEPT), 32, 128), jnp.bfloat16)
    hbm = pl.BlockSpec(memory_space=pltpu.MemorySpace.HBM)
    vmem = pl.BlockSpec(memory_space=pltpu.MemorySpace.VMEM)

    def kernel(*refs):
        if blocks == FIRST:
            refs = refs[:4] + (refs[5], refs[4]) + refs[6:]
        filter_kernel(blocks, group, *refs)

    rows = HERE * 8 * count
    return pl.pallas_call(
        kernel,
        out_shape=(tiles, rest) if blocks == FIRST else tiles,
        in_specs=[hbm] * 4 + ([] if blocks == FIRST else [vmem]),
        scratch_shapes=[
            pltpu.VMEM((2, HERE * count, 8, RG), jnp.bfloat16),
            pltpu.VMEM((HERE, RG), jnp.float32),
            pltpu.VMEM((8 * count, RG), jnp.int32),
            pltpu.VMEM((1152, 128), jnp.float32),
            pltpu.SemaphoreType.DMA((9 * count + 2,)),
            pltpu.VMEM((2, PLANES, rows, 128), jnp.float32),
            pltpu.VMEM((2, PLANES, rows, 128), jnp.float32),
            pltpu.VMEM((2, PLANES, 8, 128), jnp.float32),
            pltpu.VMEM((2, group * rows, 256), jnp.float32),
            pltpu.VMEM((HERE, PLANES, 128), jnp.float32),
            pltpu.VMEM((PLANES + 1, 8 * count, 128), jnp.float32),
            pltpu.VMEM((PLANES + 1, 2 * rows + 2 * HERE, 128), jnp.float32),
            pltpu.VMEM((768, 256), jnp.bfloat16),
            pltpu.VMEM((768, 256), jnp.bfloat16),
            pltpu.VMEM((512, 512), jnp.bfloat16),
        ],
        compiler_params=pltpu.CompilerParams(vmem_limit_bytes=65_700_000),
        cost_estimate=pl.CostEstimate(
            flops=2_000_000_000 * count, bytes_accessed=2_000_000, transcendentals=0
        ),
    )(stack, gains, mask, tables(), *(() if kept is None else (kept,)))


def unpacker(fields):
    z_re, z_im, z_sum, z_dif = fields
    rows = lax.broadcasted_iota(jnp.int32, (8, 128), 0)
    low = rows < 4

    def put(plane, group, first, second):
        re = jnp.where(low, first, pltpu.roll(second, 4, 0))
        im = jnp.where(low, pltpu.roll(first, 4, 0), second)
        total, change = re + im, im - re
        z_im[plane, 8 * group : 8 * group + 8] = im
        for begin in [8 * group] + ([32 + 8 * group] if group < 2 else []):
            z_re[plane, begin : begin + 8] = re
            z_sum[plane, begin : begin + 8] = total
            z_dif[plane, begin : begin + 8] = change

    def run(ref, slot, line, count):
        def step(i, carry):
            for group in range(4):
                first = ref[2 * group, slot + i].astype(jnp.float32)
                second = ref[2 * group + 1, slot + i].astype(jnp.float32)
                for p in range(4):
                    cut = slice(8 * p, 8 * p + 8)
                    put((line + i) * 4 + p, group, first[cut], second[cut])
            return carry

        lax.fori_loop(0, count, step, 0)

    return put, run


WIDTH = 8


def gram(fields, base, count, store):
    z_re, z_im, z_sum, z_dif = fields

    def block(index, carry):
        group = index // 2
        own = pl.ds(pl.multiple_of(group * 8, 8), 8)
        begin = pl.multiple_of(group * 8 + lax.rem(index, 2) * 8, 8)
        unit = min(8, count)

        def some(chunk, totals):
            totals = [list(totals[3 * i : 3 * i + 3]) for i in range(WIDTH)]
            for step in range(unit):
                plane = base + chunk * unit + step
                mine = (z_sum[plane, own], z_re[plane, own], z_im[plane, own])
                for i in range(WIDTH):
                    other = pl.ds(begin + 1 + i, 8)
                    others = (z_re[plane, other], z_sum[plane, other], z_dif[plane, other])
                    for k in range(3):
                        totals[i][k] = totals[i][k] + others[k] * mine[k]
            return tuple(t for total in totals for t in total)

        zero = jnp.zeros((8, 128), jnp.float32)
        totals = lax.fori_loop(0, count // unit, some, (zero,) * (3 * WIDTH))
        totals = [totals[3 * i : 3 * i + 3] for i in range(WIDTH)]
        for i in range(WIDTH):
            one, two, three = totals[i]
            spot = (lax.rem(index, 2) * 8 + 1 + i) * DATES + group * 8
            spot = pl.ds(pl.multiple_of(spot, 8), 8)
            store(0, spot, one + three)
            store(1, spot, one - two)
        return carry

    lax.fori_loop(0, 8, block, 0)
    for group in range(4):
        own = slice(8 * group, 8 * group + 8)
        total = None
        for step in range(count):
            re, im = z_re[base + step, own], z_im[base + step, own]
            term = re * re + im * im
            total = term if total is None else total + term
        store(0, own, total)


def gram_rows(fields, sums, count, first_plane, first_row):
    def one_row(r, carry):
        def store(c, spot, value):
            sums[first_row + r, c, spot] = value

        gram(fields, first_plane + r * 16, 16, store)
        return carry

    lax.fori_loop(0, count, one_row, 0)


def send_rows(fields, held, target, sem, count):
    def copy(r):
        return pltpu.make_async_copy(held.at[r], target.at[r], sem.at[r])

    def one_row(r, carry):
        def store(c, spot, value):
            held[r, c, spot] = value

        gram(fields, r * 16, 16, store)

        @pl.when(r > 0)
        def _():
            copy(r - 1).start()

        return carry

    lax.fori_loop(0, count, one_row, 0)
    copy(count - 1).start()
    for r in range(count):
        copy(r).wait()


def early_kernel(own, target, held, sem, *fields):
    _, run = unpacker(fields)
    run(own, 2, 0, 4)
    run(own, 7, 4, 4)
    send_rows(fields, held, target, sem, 2)


def halo_kernel(own, above, below, target, held, sem, *fields):
    _, run = unpacker(fields)
    run(above, 1, 0, 6)
    run(own, 0, 6, 2)
    run(own, 11, 8, 2)
    run(below, 0, 10, 6)
    send_rows(fields, held, target, sem, 4)


def some_rows(kernel, count, *chunks):
    field = pltpu.VMEM((count * 16, WRAP, 128), jnp.float32)
    return pl.pallas_call(
        kernel,
        out_shape=jax.ShapeDtypeStruct((count, 2, PAIRS, 128), jnp.float32),
        out_specs=pl.BlockSpec(memory_space=pltpu.MemorySpace.HBM),
        scratch_shapes=[
            pltpu.VMEM((count, 2, PAIRS, 128), jnp.float32),
            pltpu.SemaphoreType.DMA((count,)),
        ]
        + [field] * 4,
        compiler_params=pltpu.CompilerParams(vmem_limit_bytes=64_200_000),
        cost_estimate=pl.CostEstimate(
            flops=3_000_000_000 * count, bytes_accessed=2_000_000, transcendentals=0
        ),
    )(*chunks)


def link_kernel(
    own, rest, above, below, early_sums, halo_sums, near, band, out,
    z_re, z_im, z_sum, z_dif, sums, early, edges, sem, tails, extra, cov, vec,
):
    copies = [
        pltpu.make_async_copy(early_sums, early, sem.at[0]),
        pltpu.make_async_copy(halo_sums, edges, sem.at[1]),
    ]
    for copy in copies:
        copy.start()
    fields = (z_re, z_im, z_sum, z_dif)
    lanes = lax.broadcasted_iota(jnp.int32, (8, 128), 1)
    put, run = unpacker(fields)
    run(rest, 0, 0, 12)
    for group in range(4):
        pieces = []
        for source in (2 * group, 2 * group + 1):
            mine = own[source, EARLY_TAIL].astype(jnp.float32)
            others = rest[source, LATE_TAIL].astype(jnp.float32)
            up = above[source, 0].astype(jnp.float32)
            down = below[source, 6].astype(jnp.float32)
            piece = []
            for p in range(4):
                cut = slice(8 * p, 8 * p + 8)
                value = jnp.zeros((8, 128), jnp.float32)
                for part, turn, begin in (
                    (up, 128 - 30, 0),
                    (mine, 18, 18),
                    (others, 42, 42),
                    (mine, 42, 66),
                    (down, 90, 90),
                ):
                    value = jnp.where(lanes >= begin, pltpu.roll(part[cut], turn, 1), value)
                piece.append(jnp.where(lanes < 108, value, 0.0))
            pieces.append(piece)
        for p in range(4):
            put(48 + p, group, pieces[0][p], pieces[1][p])

    def store_tail(c, spot, value):
        tails[c, spot] = value

    gram(fields, 48, 4, store_tail)
    tails[1, 0:DATES] = jnp.zeros((DATES, 128), jnp.float32)
    gram_rows(fields, sums, 3, 0, 0)
    for c in range(2):
        high, low = split(tails[c])
        extra[c] = jnp.dot(
            jnp.concatenate([high, low], axis=1), band[...], preferred_element_type=jnp.float32
        )

    for copy in copies:
        copy.wait()

    def windows(step, carry):
        size = 2 * DATES
        begin = pl.multiple_of(step * size, size)
        spot = pl.ds(begin, size)
        twice = pl.multiple_of(step * 2 * size, 2 * size)
        for c in range(2):
            rowsum = [edges[r, c, spot] for r in (0, 1)]
            rowsum += [early[0, c, spot]] + [sums[r, c, spot] for r in range(3)]
            rowsum += [early[1, c, spot]]
            rowsum += [edges[r, c, spot] for r in (2, 3)]
            pairs = [rowsum[r] + rowsum[r + 1] for r in range(8)]
            value = jnp.concatenate([pairs[a] + pairs[a + 2] for a in range(6)], axis=0)
            high, low = split(value)
            found = jnp.dot(
                jnp.concatenate([high, low], axis=1), near[...], preferred_element_type=jnp.float32
            )
            for a in range(6):
                full = found[a * size : (a + 1) * size] + extra[c, spot, a * 128 : a * 128 + 128]
                for i in range(2):
                    half = full[i * DATES : (i + 1) * DATES]
                    cov[a, c, pl.ds(twice + 2 * i * DATES, DATES)] = half
                    cov[a, c, pl.ds(twice + (2 * i + 1) * DATES, DATES)] = half
        return carry

    lax.fori_loop(0, (SHIFTS + 1) // 2, windows, 0)

    def put_vec(c, group, value):
        for copy in range(3):
            vec[c, copy * DATES + group * 8 : copy * DATES + group * 8 + 8] = value

    def window_row(a, carry):
        weights = []
        for group in range(4):
            power = cov[a, 0, 8 * group : 8 * group + 8]
            weights.append(1.0 / jnp.sqrt(power + BETA_LOAD))
            put_vec(0, group, weights[group])

        def iterate(real, last):
            found = []
            for group in range(4):
                row = 8 * group
                re_parts, im_parts = [], []
                for s in range(SHIFTS):
                    terms = [(2 * s * DATES + row, DATES + row + s, 1)]
                    if 0 < s < SHIFTS - 1:
                        terms.append((2 * s * DATES + DATES + row - s, DATES + row - s, -1))
                    for place, other, sign in terms:
                        cov_re = cov[a, 0, place : place + 8]
                        x_re = vec[0, other : other + 8]
                        x_im = None if real else vec[1, other : other + 8]
                        if s == 0:
                            re = cov_re * x_re
                            im = None if real else cov_re * x_im
                        else:
                            cov_im = cov[a, 1, place : place + 8]
                            re = cov_re * x_re
                            im = cov_im * x_re
                            if sign < 0:
                                im = -im if real else cov_re * x_im - im
                                re = re if real else re + cov_im * x_im
                            elif not real:
                                re = re - cov_im * x_im
                                im = im + cov_re * x_im
                        re_parts.append(re)
                        if im is not None:
                            im_parts.append(im)
                found.append((sum_two(re_parts), sum_two(im_parts)))
            for group in range(4):
                u_re = found[group][0] * weights[group]
                u_im = found[group][1] * weights[group]
                length = 1.0 / jnp.sqrt(u_re * u_re + u_im * u_im + PROJ_LOAD)
                x_re, x_im = u_re * length, u_im * length
                if last:
                    out[0, a, 8 * group : 8 * group + 8] = x_re
                    out[1, a, 8 * group : 8 * group + 8] = x_im
                else:
                    put_vec(0, group, x_re * weights[group])
                    put_vec(1, group, x_im * weights[group])

        iterate(True, False)
        lax.fori_loop(0, ITERS - 2, lambda i, carry: (iterate(False, False), carry)[1], 0)
        iterate(False, True)
        return carry

    lax.fori_loop(0, 6, window_row, 0)


def sum_two(parts):
    sums = parts[:2]
    for i, part in enumerate(parts[2:]):
        sums[i % 2] = sums[i % 2] + part
    return sums[0] + sums[1]


def tail_band():
    near = np.zeros((128, 128), np.float32)
    for block in range(128):
        near[block, max(block - 3, 0) : block + 1] = 1.0
    band = np.zeros((6, 128, 128), np.float32)
    for row in range(6):
        for line in range(4 * row, 4 * row + 16):
            for block in range(3):
                band[row, line * 3 + block, 125 + block :] = 1.0
    both = np.concatenate(list(band), axis=1)
    both = np.concatenate([both, both], axis=0).astype(jnp.bfloat16)
    return np.concatenate([near, near], axis=0).astype(jnp.bfloat16), both


def link_windows(own, rest, above, below, early, edges):
    field = pltpu.VMEM((52, WRAP, 128), jnp.float32)
    vmem = pl.BlockSpec(memory_space=pltpu.MemorySpace.VMEM)
    hbm = pl.BlockSpec(memory_space=pltpu.MemorySpace.HBM)
    found = pl.pallas_call(
        link_kernel,
        out_shape=jax.ShapeDtypeStruct((2, 6, DATES, 128), jnp.float32),
        in_specs=[vmem] * 4 + [hbm] * 2 + [vmem] * 2,
        scratch_shapes=[field] * 4
        + [
            pltpu.VMEM((3, 2, PAIRS, 128), jnp.float32),
            pltpu.VMEM((2, 2, PAIRS, 128), jnp.float32),
            pltpu.VMEM((4, 2, PAIRS, 128), jnp.float32),
            pltpu.SemaphoreType.DMA((2,)),
            pltpu.VMEM((2, PAIRS, 128), jnp.float32),
            pltpu.VMEM((2, PAIRS, 6 * 128), jnp.float32),
            pltpu.VMEM((6, 2, 2 * PAIRS, 128), jnp.float32),
            pltpu.VMEM((2, 3 * DATES, 128), jnp.float32),
        ],
        compiler_params=pltpu.CompilerParams(vmem_limit_bytes=64_200_000),
        cost_estimate=pl.CostEstimate(
            flops=20_000_000_000, bytes_accessed=8_000_000, transcendentals=0
        ),
        name="link_windows",
    )(own, rest, above, below, early, edges, *tail_band())
    return jnp.transpose(found, (0, 2, 1, 3))


def on_device(stack, range_filter, scatter_mask):
    def move(tiles):
        return lax.all_to_all(tiles, "dr", split_axis=0, concat_axis=0, tiled=True)

    tiles, kept = filter_lines(stack, range_filter, scatter_mask, FIRST, 4)
    own = move(tiles)
    tiles = filter_lines(stack, range_filter, scatter_mask, SECOND, 8, kept)
    rest = move(tiles)
    count = lax.axis_size("az")
    down = [(i, i + 1) for i in range(count - 1)]
    up = [(i + 1, i) for i in range(count - 1)]
    above = lax.ppermute(own[:, 6:13], "az", down)
    below = lax.ppermute(own[:, 0:7], "az", up)
    early = some_rows(early_kernel, 2, own)
    edges = some_rows(halo_kernel, 4, own, above, below)
    return link_windows(own, rest, above, below, early, edges)


def solution(mesh):
    in_specs = (P(None, "dr", "az", None), P("dr", None), P("az", None))
    out_specs = P(None, None, "az", "dr")
    return jax.shard_map(
        on_device, mesh=mesh, in_specs=in_specs, out_specs=out_specs, check_vma=False
    )
```

```python
import math

import jax
import jax.numpy as jnp
import numpy as np
from jax import lax
from jax.experimental import pallas as pl
from jax.experimental.pallas import tpu as pltpu
from jax.sharding import PartitionSpec as P


ITERS = 4
BETA_LOAD = 1.0
PROJ_LOAD = 1.0

DATES = 32
RG = 4096
TILES = 8
HALO = 6
PLANES = 32
HERE = 4
FIRST, SECOND = (0, 16), (8,)
KEPT = (6, 7, 16, 17)
GROUP_FIRST, GROUP_SECOND = 8, 16
SHIFTS = 17
PAIRS = (SHIFTS + 1) * DATES
WRAP = 48


def slot_of(line):
    if 6 <= line < 18:
        return line - 6
    return line if line < 6 else line - 11


EARLY_TAIL, LATE_TAIL, SLOTS = 6, 12, 13


def tables():
    lane = np.arange(128)
    freq = 4 * (lane % 32) + lane // 32
    turn = 2.0 * np.pi / 128 * (np.outer(lane, freq) % 128)
    forward = np.block([[np.cos(turn), -np.sin(turn)], [np.sin(turn), np.cos(turn)]])
    turn = 2.0 * np.pi / 128 * (np.outer(freq, lane - HALO) % 128)
    inverse = np.block([[np.cos(turn), np.sin(turn)], [-np.sin(turn), np.cos(turn)]]) / RG
    plane = np.arange(PLANES)
    angle = 2.0 * np.pi / RG * np.outer(plane, lane)
    back = 2.0 * np.pi / RG * np.outer(plane, lane - HALO)
    parts = [forward[:, :128], forward[:, 128:], inverse[:, :128], inverse[:, 128:]]
    parts += [np.cos(angle), np.sin(angle), np.cos(back), np.sin(back)]
    return np.concatenate(parts, axis=0).astype(np.float32)


def cmul(value, cos, sin):
    re, im = value
    if abs(sin) < 1e-12:
        return (re, im) if cos > 0 else (-re, -im)
    if abs(cos) < 1e-12:
        return (-im, re) if sin > 0 else (im, -re)
    if abs(abs(cos) - abs(sin)) < 1e-12:
        size = abs(cos)
        if cos > 0 and sin > 0:
            return ((re - im) * size, (re + im) * size)
        if cos > 0:
            return ((re + im) * size, (im - re) * size)
        if sin > 0:
            return ((-re - im) * size, (re - im) * size)
        return ((im - re) * size, (-re - im) * size)
    return (re * cos - im * sin, im * cos + re * sin)


def small_dft(values, sign):
    count = len(values)
    if count == 1:
        return values
    even = small_dft(values[0::2], sign)
    odd = small_dft(values[1::2], sign)
    half = count // 2
    low, high = [], []
    for k in range(half):
        angle = sign * 2.0 * math.pi * k / count
        re, im = cmul(odd[k], math.cos(angle), math.sin(angle))
        low.append((even[k][0] + re, even[k][1] + im))
        high.append((even[k][0] - re, even[k][1] - im))
    return low + high


def dft_planes(load, hold, store, sign):
    for m in range(8):
        parts = small_dft([load(8 * i + m) for i in range(4)], sign)
        for s in range(4):
            angle = sign * 2.0 * math.pi * m * s / 32
            re, im = cmul(parts[s], math.cos(angle), math.sin(angle))
            hold[0, s * 8 + m] = re
            hold[1, s * 8 + m] = im
    for s in range(4):
        parts = small_dft([(hold[0, s * 8 + m], hold[1, s * 8 + m]) for m in range(8)], sign)
        for u in range(8):
            store(s + 4 * u, *parts[u])


def split(values):
    high = values.astype(jnp.bfloat16)
    return high, (values - high.astype(jnp.float32)).astype(jnp.bfloat16)


def dot3(values, table):
    high, low = split(values)
    return jnp.dot(
        jnp.concatenate([high, low, high], axis=1), table, preferred_element_type=jnp.float32
    )


def filter_kernel(
    blocks, group, stack, gains, mask, table, kept, out,
    raw, gains_in, mask_in, table_in, sem,
    spec, first, hold, held, gain, weights, lines_out, forward, inverse, place,
):
    count = len(blocks)
    lines_here = 8 * count
    rows_here = HERE * lines_here
    pitch = lines_here + 1
    early = blocks == FIRST
    stack_copies = []
    for d in range(HERE):
        for i, block in enumerate(blocks):
            for c in range(2):
                stack_copies.append(
                    pltpu.make_async_copy(
                        stack.at[c, d, pl.ds(block, 8)],
                        raw.at[c, d * count + i],
                        sem.at[c * HERE * count + d * count + i],
                    )
                )
    copies = {}
    for i, (name, source, target) in enumerate(
        (("table", table, table_in), ("gains", gains, gains_in))
    ):
        copies[name] = pltpu.make_async_copy(source, target, sem.at[9 * count + i])
    for i, block in enumerate(blocks):
        copies["mask", i] = pltpu.make_async_copy(
            mask.at[pl.ds(block, 8)], mask_in.at[pl.ds(8 * i, 8)], sem.at[8 * count + i]
        )
    first_copies = [copies["gains"], copies["table"]]
    last_copies = [copies["mask", i] for i in range(count)]
    for copy in first_copies + stack_copies + last_copies:
        copy.start()
    lanes = lax.broadcasted_iota(jnp.int32, (8, 128), 1)
    row = lax.broadcasted_iota(jnp.int32, (512, 128), 0)
    column = lax.broadcasted_iota(jnp.int32, (512, 128), 1)
    for p in range(4):
        place[:, 128 * p : 128 * p + 128] = jnp.where(row == 4 * column + p, 1.0, 0.0).astype(
            jnp.bfloat16
        )

    copies["gains"].wait()
    for n in range(PLANES):
        four = gains_in[:, n * 128 : (n + 1) * 128]
        for d in range(HERE):
            gain[d, n : n + 1] = four[d : d + 1]
    for d in range(HERE):
        turned = jnp.transpose(gain[d])
        gain[d] = jnp.concatenate([turned[32 * w : 32 * w + 32] for w in range(4)], axis=1)
    copies["table"].wait()
    for i, target in enumerate((forward, inverse)):
        for half in range(2):
            begin = 256 * (2 * i + half)
            high, low = split(table_in[begin : begin + 256])
            for j, part in enumerate((high, high, low)):
                target[256 * j : 256 * j + 256, 128 * half : 128 * half + 128] = part

    def ahead(block, carry):
        rows = pl.ds(pl.multiple_of(block * 8, 8), 8)

        def store(q, re, im):
            spec[0, q, rows] = re
            spec[1, q, rows] = im

        for c in range(2):
            pltpu.make_async_copy(
                stack.at[0, 0, pl.ds(0, 8)], raw.at[c, block], sem.at[c * HERE * count + block]
            ).wait()

        def load(n):
            lanes = slice(n * 128, (n + 1) * 128)
            return (
                raw[0, block, :, lanes].astype(jnp.float32),
                raw[1, block, :, lanes].astype(jnp.float32),
            )

        dft_planes(load, hold, store, -1)
        return carry

    lax.fori_loop(0, rows_here // 8, ahead, 0)
    steps = PLANES // group

    def ahead_part(step):
        now = step * group
        parts = []
        for i in range(group):
            tc = table_in[pl.ds(1024 + now + i, 1), :]
            ts = table_in[pl.ds(1056 + now + i, 1), :]
            re, im = spec[0, now + i], spec[1, now + i]
            parts.append(jnp.concatenate([re * tc + im * ts, im * tc - re * ts], axis=1))
        found = dot3(jnp.concatenate(parts, axis=0), forward[...])
        slot = step % 2 if isinstance(step, int) else lax.rem(step, 2)
        for i in range(group):
            for d in range(HERE):
                row = gain[d, pl.ds(now + i, 1), :]
                begin = i * rows_here + d * lines_here
                held[slot, begin : begin + lines_here] = found[
                    begin : begin + lines_here
                ] * jnp.concatenate([row, row], axis=1)

    def back_part(step):
        past = step * group
        slot = step % 2 if isinstance(step, int) else lax.rem(step, 2)
        back = dot3(held[slot], inverse[...])
        for i in range(group):
            tc = table_in[pl.ds(1088 + past + i, 1), :]
            ts = table_in[pl.ds(1120 + past + i, 1), :]
            re = back[i * rows_here : (i + 1) * rows_here, :128]
            im = back[i * rows_here : (i + 1) * rows_here, 128:]
            first[0, past + i] = re * tc - im * ts
            first[1, past + i] = im * tc + re * ts

    def middle(step, carry):
        back_part(step - 1)
        ahead_part(step)
        return carry

    ahead_part(0)
    lax.fori_loop(1, steps, middle, 0)
    back_part(steps - 1)

    for i in range(count):
        copies["mask", i].wait()
        rows = slice(8 * i, 8 * i + 8)
        before = pltpu.roll(mask_in[rows, RG - 128 :].astype(jnp.float32), HALO, 1)
        for n in range(PLANES):
            now = pltpu.roll(mask_in[rows, n * 128 : (n + 1) * 128].astype(jnp.float32), HALO, 1)
            joined = jnp.where(lanes < HALO, before, now)
            if n == 0:
                weights[PLANES, rows] = jnp.where(lanes < HALO, joined, 0.0)
                joined = jnp.where(lanes < HALO, 0.0, joined)
            weights[n, rows] = joined
            before = now

    def behind(block, carry):
        rows = pl.ds(pl.multiple_of(block * 8, 8), 8)
        begin = (block // count) * pitch + lax.rem(block, count) * 8
        to_re = pl.ds(begin, 8)
        to_im = pl.ds(begin + HERE * pitch, 8)
        lines = pl.ds(pl.multiple_of(lax.rem(block, count) * 8, 8), 8)

        def store(n, re, im):
            weight = weights[n, lines]
            lines_out[n, to_re] = re * weight
            lines_out[n, to_im] = im * weight
            if n == 0:
                weight = weights[PLANES, lines]
                lines_out[PLANES, to_re] = re * weight
                lines_out[PLANES, to_im] = im * weight

        dft_planes(lambda q: (first[0, q, rows], first[1, q, rows]), hold, store, 1)
        return carry

    lax.fori_loop(0, rows_here // 8, behind, 0)

    def gather(plane):
        return jnp.concatenate(
            [lines_out[plane, pl.ds(line, 8, stride=pitch), :] for line in range(lines_here)],
            axis=0,
        )

    def put_tail(slot, found):
        tails = []
        for p in range(4):
            tail = jnp.zeros((8, 128), jnp.float32)
            for line in range(lines_here):
                part = found[line * 8 : line * 8 + 8, p * 128 : p * 128 + 128]
                if line:
                    part = pltpu.roll(part, 3 * line, 1)
                tail = jnp.where(lanes >= 3 * line, part, tail)
            tails.append(jnp.where(lanes < 3 * lines_here, tail, 0.0))
        out[slot, EARLY_TAIL if early else LATE_TAIL] = jnp.concatenate(tails, axis=0).astype(
            jnp.bfloat16
        )

    def one_tile(t, found):
        for index in range(lines_here):
            line = blocks[index // 8] + index % 8
            value = jnp.concatenate(
                [found[index * 8 : index * 8 + 8, p * 128 : p * 128 + 128] for p in range(4)],
                axis=0,
            ).astype(jnp.bfloat16)
            if early and line in KEPT:
                kept[t, KEPT.index(line)] = value
            else:
                out[t, slot_of(line)] = value
        if not early:
            for index, line in enumerate(KEPT):
                out[t, slot_of(line)] = kept[t, index]
        put_tail(lax.rem(t + TILES - 1, TILES), found)

    def tile(step, carry):
        left = [
            jnp.concatenate([gather(8 * step + 4 * i + v) for v in range(4)], axis=1)
            for i in range(2)
        ]
        found = jnp.dot(
            jnp.concatenate(left, axis=0).astype(jnp.bfloat16),
            place[...],
            preferred_element_type=jnp.float32,
        )
        for i in range(2):
            one_tile(2 * step + i, found[8 * lines_here * i : 8 * lines_here * (i + 1)])
        return carry

    lax.fori_loop(0, TILES // 2, tile, 0)
    found = jnp.dot(
        gather(PLANES).astype(jnp.bfloat16), place[:128], preferred_element_type=jnp.float32
    )
    put_tail(TILES - 1, found)


def filter_lines(stack, gains, mask, blocks, group, kept=None):
    count = len(blocks)
    tiles = jax.ShapeDtypeStruct((TILES, SLOTS, 32, 128), jnp.bfloat16)
    rest = jax.ShapeDtypeStruct((TILES, len(KEPT), 32, 128), jnp.bfloat16)
    hbm = pl.BlockSpec(memory_space=pltpu.MemorySpace.HBM)
    vmem = pl.BlockSpec(memory_space=pltpu.MemorySpace.VMEM)

    def kernel(*refs):
        if blocks == FIRST:
            refs = refs[:4] + (refs[5], refs[4]) + refs[6:]
        filter_kernel(blocks, group, *refs)

    rows = HERE * 8 * count
    return pl.pallas_call(
        kernel,
        out_shape=(tiles, rest) if blocks == FIRST else tiles,
        in_specs=[hbm] * 4 + ([] if blocks == FIRST else [vmem]),
        scratch_shapes=[
            pltpu.VMEM((2, HERE * count, 8, RG), jnp.bfloat16),
            pltpu.VMEM((HERE, RG), jnp.float32),
            pltpu.VMEM((8 * count, RG), jnp.int32),
            pltpu.VMEM((1152, 128), jnp.float32),
            pltpu.SemaphoreType.DMA((9 * count + 2,)),
            pltpu.VMEM((2, PLANES, rows, 128), jnp.float32),
            pltpu.VMEM((2, PLANES, rows, 128), jnp.float32),
            pltpu.VMEM((2, PLANES, 8, 128), jnp.float32),
            pltpu.VMEM((2, group * rows, 256), jnp.float32),
            pltpu.VMEM((HERE, PLANES, 128), jnp.float32),
            pltpu.VMEM((PLANES + 1, 8 * count, 128), jnp.float32),
            pltpu.VMEM((PLANES + 1, 2 * rows + 2 * HERE, 128), jnp.float32),
            pltpu.VMEM((768, 256), jnp.bfloat16),
            pltpu.VMEM((768, 256), jnp.bfloat16),
            pltpu.VMEM((512, 512), jnp.bfloat16),
        ],
        compiler_params=pltpu.CompilerParams(vmem_limit_bytes=65_700_000),
        cost_estimate=pl.CostEstimate(
            flops=2_000_000_000 * count, bytes_accessed=2_000_000, transcendentals=0
        ),
    )(stack, gains, mask, tables(), *(() if kept is None else (kept,)))


def unpacker(fields):
    z_re, z_im, z_sum, z_dif = fields
    rows = lax.broadcasted_iota(jnp.int32, (8, 128), 0)
    low = rows < 4

    def put(plane, group, first, second):
        re = jnp.where(low, first, pltpu.roll(second, 4, 0))
        im = jnp.where(low, pltpu.roll(first, 4, 0), second)
        total, change = re + im, im - re
        z_im[plane, 8 * group : 8 * group + 8] = im
        for begin in [8 * group] + ([32 + 8 * group] if group < 2 else []):
            z_re[plane, begin : begin + 8] = re
            z_sum[plane, begin : begin + 8] = total
            z_dif[plane, begin : begin + 8] = change

    def run(ref, slot, line, count):
        def step(i, carry):
            for group in range(4):
                first = ref[2 * group, slot + i].astype(jnp.float32)
                second = ref[2 * group + 1, slot + i].astype(jnp.float32)
                for p in range(4):
                    cut = slice(8 * p, 8 * p + 8)
                    put((line + i) * 4 + p, group, first[cut], second[cut])
            return carry

        lax.fori_loop(0, count, step, 0)

    return put, run


WIDTH = 8


def gram(fields, base, count, store):
    z_re, z_im, z_sum, z_dif = fields

    def block(index, carry):
        group = index // 2
        own = pl.ds(pl.multiple_of(group * 8, 8), 8)
        begin = pl.multiple_of(group * 8 + lax.rem(index, 2) * 8, 8)
        unit = min(8, count)

        def some(chunk, totals):
            totals = [list(totals[3 * i : 3 * i + 3]) for i in range(WIDTH)]
            for step in range(unit):
                plane = base + chunk * unit + step
                mine = (z_sum[plane, own], z_re[plane, own], z_im[plane, own])
                for i in range(WIDTH):
                    other = pl.ds(begin + 1 + i, 8)
                    others = (z_re[plane, other], z_sum[plane, other], z_dif[plane, other])
                    for k in range(3):
                        totals[i][k] = totals[i][k] + others[k] * mine[k]
            return tuple(t for total in totals for t in total)

        zero = jnp.zeros((8, 128), jnp.float32)
        totals = lax.fori_loop(0, count // unit, some, (zero,) * (3 * WIDTH))
        totals = [totals[3 * i : 3 * i + 3] for i in range(WIDTH)]
        for i in range(WIDTH):
            one, two, three = totals[i]
            spot = (lax.rem(index, 2) * 8 + 1 + i) * DATES + group * 8
            spot = pl.ds(pl.multiple_of(spot, 8), 8)
            store(0, spot, one + three)
            store(1, spot, one - two)
        return carry

    lax.fori_loop(0, 8, block, 0)
    for group in range(4):
        own = slice(8 * group, 8 * group + 8)
        total = None
        for step in range(count):
            re, im = z_re[base + step, own], z_im[base + step, own]
            term = re * re + im * im
            total = term if total is None else total + term
        store(0, own, total)


def gram_rows(fields, sums, count, first_plane, first_row):
    def one_row(r, carry):
        def store(c, spot, value):
            sums[first_row + r, c, spot] = value

        gram(fields, first_plane + r * 16, 16, store)
        return carry

    lax.fori_loop(0, count, one_row, 0)


def early_kernel(own, sums, *fields):
    _, run = unpacker(fields)
    run(own, 2, 0, 4)
    run(own, 7, 4, 4)
    gram_rows(fields, sums, 2, 0, 0)


def inner_kernel(rest, sums, *fields):
    _, run = unpacker(fields)
    run(rest, 0, 0, 12)
    gram_rows(fields, sums, 3, 0, 0)


def own_rows(kernel, count, *chunks):
    field = pltpu.VMEM((count * 16, WRAP, 128), jnp.float32)
    return pl.pallas_call(
        kernel,
        out_shape=jax.ShapeDtypeStruct((count, 2, PAIRS, 128), jnp.float32),
        scratch_shapes=[field] * 4,
        compiler_params=pltpu.CompilerParams(vmem_limit_bytes=(4 + 3 * count) << 20),
        cost_estimate=pl.CostEstimate(
            flops=3_000_000_000 * count, bytes_accessed=2_000_000, transcendentals=0
        ),
    )(*chunks)


def link_kernel(
    own, rest, above, below, early, inner, near, band, out,
    z_re, z_im, z_sum, z_dif, sums, tails, extra, cov, vec,
):
    fields = (z_re, z_im, z_sum, z_dif)
    lanes = lax.broadcasted_iota(jnp.int32, (8, 128), 1)
    put, run = unpacker(fields)
    run(above, 1, 0, 6)
    run(own, 0, 6, 2)
    run(own, 11, 8, 2)
    run(below, 0, 10, 6)
    for group in range(4):
        pieces = []
        for source in (2 * group, 2 * group + 1):
            mine = own[source, EARLY_TAIL].astype(jnp.float32)
            others = rest[source, LATE_TAIL].astype(jnp.float32)
            up = above[source, 0].astype(jnp.float32)
            down = below[source, 6].astype(jnp.float32)
            piece = []
            for p in range(4):
                cut = slice(8 * p, 8 * p + 8)
                value = jnp.zeros((8, 128), jnp.float32)
                for part, turn, begin in (
                    (up, 128 - 30, 0),
                    (mine, 18, 18),
                    (others, 42, 42),
                    (mine, 42, 66),
                    (down, 90, 90),
                ):
                    value = jnp.where(lanes >= begin, pltpu.roll(part[cut], turn, 1), value)
                piece.append(jnp.where(lanes < 108, value, 0.0))
            pieces.append(piece)
        for p in range(4):
            put(64 + p, group, pieces[0][p], pieces[1][p])

    def store_tail(c, spot, value):
        tails[c, spot] = value

    gram(fields, 64, 4, store_tail)
    tails[1, 0:DATES] = jnp.zeros((DATES, 128), jnp.float32)
    gram_rows(fields, sums, 4, 0, 0)
    for c in range(2):
        high, low = split(tails[c])
        extra[c] = jnp.dot(
            jnp.concatenate([high, low], axis=1), band[...], preferred_element_type=jnp.float32
        )

    def windows(step, carry):
        size = 2 * DATES
        begin = pl.multiple_of(step * size, size)
        spot = pl.ds(begin, size)
        twice = pl.multiple_of(step * 2 * size, 2 * size)
        for c in range(2):
            rowsum = [sums[r, c, spot] for r in (0, 1)]
            rowsum += [early[0, c, spot]] + [inner[r, c, spot] for r in range(3)]
            rowsum += [early[1, c, spot]]
            rowsum += [sums[r, c, spot] for r in (2, 3)]
            pairs = [rowsum[r] + rowsum[r + 1] for r in range(8)]
            value = jnp.concatenate([pairs[a] + pairs[a + 2] for a in range(6)], axis=0)
            high, low = split(value)
            found = jnp.dot(
                jnp.concatenate([high, low], axis=1), near[...], preferred_element_type=jnp.float32
            )
            for a in range(6):
                full = found[a * size : (a + 1) * size] + extra[c, spot, a * 128 : a * 128 + 128]
                for i in range(2):
                    half = full[i * DATES : (i + 1) * DATES]
                    cov[a, c, pl.ds(twice + 2 * i * DATES, DATES)] = half
                    cov[a, c, pl.ds(twice + (2 * i + 1) * DATES, DATES)] = half
        return carry

    lax.fori_loop(0, (SHIFTS + 1) // 2, windows, 0)

    def put_vec(c, group, value):
        for copy in range(3):
            vec[c, copy * DATES + group * 8 : copy * DATES + group * 8 + 8] = value

    def window_row(a, carry):
        weights = []
        for group in range(4):
            power = cov[a, 0, 8 * group : 8 * group + 8]
            weights.append(1.0 / jnp.sqrt(power + BETA_LOAD))
            put_vec(0, group, weights[group])

        def iterate(real, last):
            found = []
            for group in range(4):
                row = 8 * group
                re_parts, im_parts = [], []
                for s in range(SHIFTS):
                    terms = [(2 * s * DATES + row, DATES + row + s, 1)]
                    if 0 < s < SHIFTS - 1:
                        terms.append((2 * s * DATES + DATES + row - s, DATES + row - s, -1))
                    for place, other, sign in terms:
                        cov_re = cov[a, 0, place : place + 8]
                        x_re = vec[0, other : other + 8]
                        x_im = None if real else vec[1, other : other + 8]
                        if s == 0:
                            re = cov_re * x_re
                            im = None if real else cov_re * x_im
                        else:
                            cov_im = cov[a, 1, place : place + 8]
                            re = cov_re * x_re
                            im = cov_im * x_re
                            if sign < 0:
                                im = -im if real else cov_re * x_im - im
                                re = re if real else re + cov_im * x_im
                            elif not real:
                                re = re - cov_im * x_im
                                im = im + cov_re * x_im
                        re_parts.append(re)
                        if im is not None:
                            im_parts.append(im)
                found.append((sum_two(re_parts), sum_two(im_parts)))
            for group in range(4):
                u_re = found[group][0] * weights[group]
                u_im = found[group][1] * weights[group]
                length = 1.0 / jnp.sqrt(u_re * u_re + u_im * u_im + PROJ_LOAD)
                x_re, x_im = u_re * length, u_im * length
                if last:
                    out[0, a, 8 * group : 8 * group + 8] = x_re
                    out[1, a, 8 * group : 8 * group + 8] = x_im
                else:
                    put_vec(0, group, x_re * weights[group])
                    put_vec(1, group, x_im * weights[group])

        iterate(True, False)
        lax.fori_loop(0, ITERS - 2, lambda i, carry: (iterate(False, False), carry)[1], 0)
        iterate(False, True)
        return carry

    lax.fori_loop(0, 6, window_row, 0)


def sum_two(parts):
    sums = parts[:2]
    for i, part in enumerate(parts[2:]):
        sums[i % 2] = sums[i % 2] + part
    return sums[0] + sums[1]


def tail_band():
    near = np.zeros((128, 128), np.float32)
    for block in range(128):
        near[block, max(block - 3, 0) : block + 1] = 1.0
    band = np.zeros((6, 128, 128), np.float32)
    for row in range(6):
        for line in range(4 * row, 4 * row + 16):
            for block in range(3):
                band[row, line * 3 + block, 125 + block :] = 1.0
    both = np.concatenate(list(band), axis=1)
    both = np.concatenate([both, both], axis=0).astype(jnp.bfloat16)
    return np.concatenate([near, near], axis=0).astype(jnp.bfloat16), both


def link_windows(own, rest, above, below, early, inner):
    field = pltpu.VMEM((68, WRAP, 128), jnp.float32)
    found = pl.pallas_call(
        link_kernel,
        out_shape=jax.ShapeDtypeStruct((2, 6, DATES, 128), jnp.float32),
        scratch_shapes=[field] * 4
        + [
            pltpu.VMEM((4, 2, PAIRS, 128), jnp.float32),
            pltpu.VMEM((2, PAIRS, 128), jnp.float32),
            pltpu.VMEM((2, PAIRS, 6 * 128), jnp.float32),
            pltpu.VMEM((6, 2, 2 * PAIRS, 128), jnp.float32),
            pltpu.VMEM((2, 3 * DATES, 128), jnp.float32),
        ],
        compiler_params=pltpu.CompilerParams(vmem_limit_bytes=28 << 20),
        cost_estimate=pl.CostEstimate(
            flops=20_000_000_000, bytes_accessed=8_000_000, transcendentals=0
        ),
        name="link_windows",
    )(own, rest, above, below, early, inner, *tail_band())
    return jnp.transpose(found, (0, 2, 1, 3))


def on_device(stack, range_filter, scatter_mask):
    def move(tiles):
        return lax.all_to_all(tiles, "dr", split_axis=0, concat_axis=0, tiled=True)

    tiles, kept = filter_lines(stack, range_filter, scatter_mask, FIRST, GROUP_FIRST)
    own = move(tiles)
    tiles = filter_lines(stack, range_filter, scatter_mask, SECOND, GROUP_SECOND, kept)
    rest = move(tiles)
    count = lax.axis_size("az")
    down = [(i, i + 1) for i in range(count - 1)]
    up = [(i + 1, i) for i in range(count - 1)]
    above = lax.ppermute(own[:, 6:13], "az", down)
    below = lax.ppermute(own[:, 0:7], "az", up)
    early = own_rows(early_kernel, 2, own)
    inner = own_rows(inner_kernel, 3, rest)
    return link_windows(own, rest, above, below, early, inner)


def solution(mesh):
    in_specs = (P(None, "dr", "az", None), P("dr", None), P("az", None))
    out_specs = P(None, None, "az", "dr")
    return jax.shard_map(
        on_device, mesh=mesh, in_specs=in_specs, out_specs=out_specs, check_vma=False
    )
```

```python
import math

import jax
import jax.numpy as jnp
import numpy as np
from jax import lax
from jax.experimental import pallas as pl
from jax.experimental.pallas import tpu as pltpu
from jax.sharding import PartitionSpec as P


ITERS = 4
BETA_LOAD = 1.0
PROJ_LOAD = 1.0

DATES = 32
RG = 4096
TILES = 8
HALO = 6
PLANES = 32
HERE = 4
FIRST, SECOND = (0, 16), (8,)
KEPT = (6, 7, 16, 17)
GROUP_FIRST, GROUP_SECOND = 8, 16
SHIFTS = 17
PAIRS = (SHIFTS + 1) * DATES
WRAP = 48


def slot_of(line):
    if 6 <= line < 18:
        return line - 6
    return line if line < 6 else line - 11


EARLY_TAIL, LATE_TAIL, SLOTS = 6, 12, 13


def tables():
    lane = np.arange(128)
    freq = 4 * (lane % 32) + lane // 32
    turn = 2.0 * np.pi / 128 * (np.outer(lane, freq) % 128)
    forward = np.block([[np.cos(turn), -np.sin(turn)], [np.sin(turn), np.cos(turn)]])
    turn = 2.0 * np.pi / 128 * (np.outer(freq, lane - HALO) % 128)
    inverse = np.block([[np.cos(turn), np.sin(turn)], [-np.sin(turn), np.cos(turn)]]) / RG
    plane = np.arange(PLANES)
    angle = 2.0 * np.pi / RG * np.outer(plane, lane)
    back = 2.0 * np.pi / RG * np.outer(plane, lane - HALO)
    parts = [forward[:, :128], forward[:, 128:], inverse[:, :128], inverse[:, 128:]]
    parts += [np.cos(angle), np.sin(angle), np.cos(back), np.sin(back)]
    return np.concatenate(parts, axis=0).astype(np.float32)


def cmul(value, cos, sin):
    re, im = value
    if abs(sin) < 1e-12:
        return (re, im) if cos > 0 else (-re, -im)
    if abs(cos) < 1e-12:
        return (-im, re) if sin > 0 else (im, -re)
    if abs(abs(cos) - abs(sin)) < 1e-12:
        size = abs(cos)
        if cos > 0 and sin > 0:
            return ((re - im) * size, (re + im) * size)
        if cos > 0:
            return ((re + im) * size, (im - re) * size)
        if sin > 0:
            return ((-re - im) * size, (re - im) * size)
        return ((im - re) * size, (-re - im) * size)
    return (re * cos - im * sin, im * cos + re * sin)


def small_dft(values, sign):
    count = len(values)
    if count == 1:
        return values
    even = small_dft(values[0::2], sign)
    odd = small_dft(values[1::2], sign)
    half = count // 2
    low, high = [], []
    for k in range(half):
        angle = sign * 2.0 * math.pi * k / count
        re, im = cmul(odd[k], math.cos(angle), math.sin(angle))
        low.append((even[k][0] + re, even[k][1] + im))
        high.append((even[k][0] - re, even[k][1] - im))
    return low + high


def dft_planes(load, hold, store, sign):
    for m in range(8):
        parts = small_dft([load(8 * i + m) for i in range(4)], sign)
        for s in range(4):
            angle = sign * 2.0 * math.pi * m * s / 32
            re, im = cmul(parts[s], math.cos(angle), math.sin(angle))
            hold[0, s * 8 + m] = re
            hold[1, s * 8 + m] = im
    for s in range(4):
        parts = small_dft([(hold[0, s * 8 + m], hold[1, s * 8 + m]) for m in range(8)], sign)
        for u in range(8):
            store(s + 4 * u, *parts[u])


def split(values):
    high = values.astype(jnp.bfloat16)
    return high, (values - high.astype(jnp.float32)).astype(jnp.bfloat16)


def dot3(values, table):
    high, low = split(values)
    return jnp.dot(
        jnp.concatenate([high, low, high], axis=1), table, preferred_element_type=jnp.float32
    )


def filter_kernel(
    blocks, group, stack, gains, mask, table, kept, out,
    raw, gains_in, mask_in, table_in, sem,
    spec, first, hold, held, gain, weights, lines_out, forward, inverse, place,
):
    count = len(blocks)
    lines_here = 8 * count
    rows_here = HERE * lines_here
    pitch = lines_here + 1
    early = blocks == FIRST
    stack_copies = []
    for d in range(HERE):
        for i, block in enumerate(blocks):
            for c in range(2):
                stack_copies.append(
                    pltpu.make_async_copy(
                        stack.at[c, d, pl.ds(block, 8)],
                        raw.at[c, d * count + i],
                        sem.at[c * HERE * count + d * count + i],
                    )
                )
    copies = {}
    for i, (name, source, target) in enumerate(
        (("table", table, table_in), ("gains", gains, gains_in))
    ):
        copies[name] = pltpu.make_async_copy(source, target, sem.at[9 * count + i])
    for i, block in enumerate(blocks):
        copies["mask", i] = pltpu.make_async_copy(
            mask.at[pl.ds(block, 8)], mask_in.at[pl.ds(8 * i, 8)], sem.at[8 * count + i]
        )
    first_copies = [copies["gains"], copies["table"]]
    last_copies = [copies["mask", i] for i in range(count)]
    for copy in first_copies + stack_copies + last_copies:
        copy.start()
    lanes = lax.broadcasted_iota(jnp.int32, (8, 128), 1)
    row = lax.broadcasted_iota(jnp.int32, (512, 128), 0)
    column = lax.broadcasted_iota(jnp.int32, (512, 128), 1)
    for p in range(4):
        place[:, 128 * p : 128 * p + 128] = jnp.where(row == 4 * column + p, 1.0, 0.0).astype(
            jnp.bfloat16
        )

    copies["gains"].wait()
    for n in range(PLANES):
        four = gains_in[:, n * 128 : (n + 1) * 128]
        for d in range(HERE):
            gain[d, n : n + 1] = four[d : d + 1]
    for d in range(HERE):
        turned = jnp.transpose(gain[d])
        gain[d] = jnp.concatenate([turned[32 * w : 32 * w + 32] for w in range(4)], axis=1)
    copies["table"].wait()
    for i, target in enumerate((forward, inverse)):
        for half in range(2):
            begin = 256 * (2 * i + half)
            high, low = split(table_in[begin : begin + 256])
            for j, part in enumerate((high, high, low)):
                target[256 * j : 256 * j + 256, 128 * half : 128 * half + 128] = part

    def ahead(block, carry):
        rows = pl.ds(pl.multiple_of(block * 8, 8), 8)

        def store(q, re, im):
            spec[0, q, rows] = re
            spec[1, q, rows] = im

        for c in range(2):
            pltpu.make_async_copy(
                stack.at[0, 0, pl.ds(0, 8)], raw.at[c, block], sem.at[c * HERE * count + block]
            ).wait()

        def load(n):
            lanes = slice(n * 128, (n + 1) * 128)
            return (
                raw[0, block, :, lanes].astype(jnp.float32),
                raw[1, block, :, lanes].astype(jnp.float32),
            )

        dft_planes(load, hold, store, -1)
        return carry

    lax.fori_loop(0, rows_here // 8, ahead, 0)
    steps = PLANES // group

    def ahead_part(step):
        now = step * group
        parts = []
        for i in range(group):
            tc = table_in[pl.ds(1024 + now + i, 1), :]
            ts = table_in[pl.ds(1056 + now + i, 1), :]
            re, im = spec[0, now + i], spec[1, now + i]
            parts.append(jnp.concatenate([re * tc + im * ts, im * tc - re * ts], axis=1))
        found = dot3(jnp.concatenate(parts, axis=0), forward[...])
        slot = step % 2 if isinstance(step, int) else lax.rem(step, 2)
        for i in range(group):
            for d in range(HERE):
                row = gain[d, pl.ds(now + i, 1), :]
                begin = i * rows_here + d * lines_here
                held[slot, begin : begin + lines_here] = found[
                    begin : begin + lines_here
                ] * jnp.concatenate([row, row], axis=1)

    def back_part(step):
        past = step * group
        slot = step % 2 if isinstance(step, int) else lax.rem(step, 2)
        back = dot3(held[slot], inverse[...])
        for i in range(group):
            tc = table_in[pl.ds(1088 + past + i, 1), :]
            ts = table_in[pl.ds(1120 + past + i, 1), :]
            re = back[i * rows_here : (i + 1) * rows_here, :128]
            im = back[i * rows_here : (i + 1) * rows_here, 128:]
            first[0, past + i] = re * tc - im * ts
            first[1, past + i] = im * tc + re * ts

    def middle(step, carry):
        back_part(step - 1)
        ahead_part(step)
        return carry

    ahead_part(0)
    lax.fori_loop(1, steps, middle, 0)
    back_part(steps - 1)

    for i in range(count):
        copies["mask", i].wait()
        rows = slice(8 * i, 8 * i + 8)
        before = pltpu.roll(mask_in[rows, RG - 128 :].astype(jnp.float32), HALO, 1)
        for n in range(PLANES):
            now = pltpu.roll(mask_in[rows, n * 128 : (n + 1) * 128].astype(jnp.float32), HALO, 1)
            joined = jnp.where(lanes < HALO, before, now)
            if n == 0:
                weights[PLANES, rows] = jnp.where(lanes < HALO, joined, 0.0)
                joined = jnp.where(lanes < HALO, 0.0, joined)
            weights[n, rows] = joined
            before = now

    def behind(block, carry):
        rows = pl.ds(pl.multiple_of(block * 8, 8), 8)
        begin = (block // count) * pitch + lax.rem(block, count) * 8
        to_re = pl.ds(begin, 8)
        to_im = pl.ds(begin + HERE * pitch, 8)
        lines = pl.ds(pl.multiple_of(lax.rem(block, count) * 8, 8), 8)

        def store(n, re, im):
            weight = weights[n, lines]
            lines_out[n, to_re] = re * weight
            lines_out[n, to_im] = im * weight
            if n == 0:
                weight = weights[PLANES, lines]
                lines_out[PLANES, to_re] = re * weight
                lines_out[PLANES, to_im] = im * weight

        dft_planes(lambda q: (first[0, q, rows], first[1, q, rows]), hold, store, 1)
        return carry

    lax.fori_loop(0, rows_here // 8, behind, 0)

    def gather(plane):
        return jnp.concatenate(
            [lines_out[plane, pl.ds(line, 8, stride=pitch), :] for line in range(lines_here)],
            axis=0,
        )

    def put_tail(slot, found):
        tails = []
        for p in range(4):
            tail = jnp.zeros((8, 128), jnp.float32)
            for line in range(lines_here):
                part = found[line * 8 : line * 8 + 8, p * 128 : p * 128 + 128]
                if line:
                    part = pltpu.roll(part, 3 * line, 1)
                tail = jnp.where(lanes >= 3 * line, part, tail)
            tails.append(jnp.where(lanes < 3 * lines_here, tail, 0.0))
        out[slot, EARLY_TAIL if early else LATE_TAIL] = jnp.concatenate(tails, axis=0).astype(
            jnp.bfloat16
        )

    def one_tile(t, found):
        for index in range(lines_here):
            line = blocks[index // 8] + index % 8
            value = jnp.concatenate(
                [found[index * 8 : index * 8 + 8, p * 128 : p * 128 + 128] for p in range(4)],
                axis=0,
            ).astype(jnp.bfloat16)
            if early and line in KEPT:
                kept[t, KEPT.index(line)] = value
            else:
                out[t, slot_of(line)] = value
        if not early:
            for index, line in enumerate(KEPT):
                out[t, slot_of(line)] = kept[t, index]
        put_tail(lax.rem(t + TILES - 1, TILES), found)

    def tile(step, carry):
        left = [
            jnp.concatenate([gather(8 * step + 4 * i + v) for v in range(4)], axis=1)
            for i in range(2)
        ]
        found = jnp.dot(
            jnp.concatenate(left, axis=0).astype(jnp.bfloat16),
            place[...],
            preferred_element_type=jnp.float32,
        )
        for i in range(2):
            one_tile(2 * step + i, found[8 * lines_here * i : 8 * lines_here * (i + 1)])
        return carry

    lax.fori_loop(0, TILES // 2, tile, 0)
    found = jnp.dot(
        gather(PLANES).astype(jnp.bfloat16), place[:128], preferred_element_type=jnp.float32
    )
    put_tail(TILES - 1, found)


def filter_lines(stack, gains, mask, blocks, group, kept=None):
    count = len(blocks)
    tiles = jax.ShapeDtypeStruct((TILES, SLOTS, 32, 128), jnp.bfloat16)
    rest = jax.ShapeDtypeStruct((TILES, len(KEPT), 32, 128), jnp.bfloat16)
    hbm = pl.BlockSpec(memory_space=pltpu.MemorySpace.HBM)
    vmem = pl.BlockSpec(memory_space=pltpu.MemorySpace.VMEM)

    def kernel(*refs):
        if blocks == FIRST:
            refs = refs[:4] + (refs[5], refs[4]) + refs[6:]
        filter_kernel(blocks, group, *refs)

    rows = HERE * 8 * count
    return pl.pallas_call(
        kernel,
        out_shape=(tiles, rest) if blocks == FIRST else tiles,
        in_specs=[hbm] * 4 + ([] if blocks == FIRST else [vmem]),
        scratch_shapes=[
            pltpu.VMEM((2, HERE * count, 8, RG), jnp.bfloat16),
            pltpu.VMEM((HERE, RG), jnp.float32),
            pltpu.VMEM((8 * count, RG), jnp.int32),
            pltpu.VMEM((1152, 128), jnp.float32),
            pltpu.SemaphoreType.DMA((9 * count + 2,)),
            pltpu.VMEM((2, PLANES, rows, 128), jnp.float32),
            pltpu.VMEM((2, PLANES, rows, 128), jnp.float32),
            pltpu.VMEM((2, PLANES, 8, 128), jnp.float32),
            pltpu.VMEM((2, group * rows, 256), jnp.float32),
            pltpu.VMEM((HERE, PLANES, 128), jnp.float32),
            pltpu.VMEM((PLANES + 1, 8 * count, 128), jnp.float32),
            pltpu.VMEM((PLANES + 1, 2 * rows + 2 * HERE, 128), jnp.float32),
            pltpu.VMEM((768, 256), jnp.bfloat16),
            pltpu.VMEM((768, 256), jnp.bfloat16),
            pltpu.VMEM((512, 512), jnp.bfloat16),
        ],
        compiler_params=pltpu.CompilerParams(vmem_limit_bytes=65_700_000),
        cost_estimate=pl.CostEstimate(
            flops=2_000_000_000 * count, bytes_accessed=2_000_000, transcendentals=0
        ),
    )(stack, gains, mask, tables(), *(() if kept is None else (kept,)))


def unpacker(fields):
    z_re, z_im, z_sum, z_dif = fields
    rows = lax.broadcasted_iota(jnp.int32, (8, 128), 0)
    low = rows < 4

    def put(plane, group, first, second):
        re = jnp.where(low, first, pltpu.roll(second, 4, 0))
        im = jnp.where(low, pltpu.roll(first, 4, 0), second)
        total, change = re + im, im - re
        z_im[plane, 8 * group : 8 * group + 8] = im
        for begin in [8 * group] + ([32 + 8 * group] if group < 2 else []):
            z_re[plane, begin : begin + 8] = re
            z_sum[plane, begin : begin + 8] = total
            z_dif[plane, begin : begin + 8] = change

    def run(ref, slot, line, count):
        def step(i, carry):
            for group in range(4):
                first = ref[2 * group, slot + i].astype(jnp.float32)
                second = ref[2 * group + 1, slot + i].astype(jnp.float32)
                for p in range(4):
                    cut = slice(8 * p, 8 * p + 8)
                    put((line + i) * 4 + p, group, first[cut], second[cut])
            return carry

        lax.fori_loop(0, count, step, 0)

    return put, run


WIDTH = 8


def gram(fields, base, count, store):
    z_re, z_im, z_sum, z_dif = fields

    def block(index, carry):
        group = index // 2
        own = pl.ds(pl.multiple_of(group * 8, 8), 8)
        begin = pl.multiple_of(group * 8 + lax.rem(index, 2) * 8, 8)
        unit = min(8, count)

        def some(chunk, totals):
            totals = [list(totals[3 * i : 3 * i + 3]) for i in range(WIDTH)]
            for step in range(0, unit, 2):
                pair = [base + chunk * unit + step + q for q in range(2)]
                mine = [(z_sum[p, own], z_re[p, own], z_im[p, own]) for p in pair]
                for i in range(WIDTH):
                    other = pl.ds(begin + 1 + i, 8)
                    for k, ref in enumerate((z_re, z_sum, z_dif)):
                        terms = [ref[p, other] * part[k] for p, part in zip(pair, mine)]
                        totals[i][k] = totals[i][k] + (terms[0] + terms[1])
            return tuple(t for total in totals for t in total)

        zero = jnp.zeros((8, 128), jnp.float32)
        totals = lax.fori_loop(0, count // unit, some, (zero,) * (3 * WIDTH))
        totals = [totals[3 * i : 3 * i + 3] for i in range(WIDTH)]
        for i in range(WIDTH):
            one, two, three = totals[i]
            spot = (lax.rem(index, 2) * 8 + 1 + i) * DATES + group * 8
            spot = pl.ds(pl.multiple_of(spot, 8), 8)
            store(0, spot, one + three)
            store(1, spot, one - two)
        return carry

    lax.fori_loop(0, 8, block, 0)
    for group in range(4):
        own = slice(8 * group, 8 * group + 8)
        total = None
        for step in range(count):
            re, im = z_re[base + step, own], z_im[base + step, own]
            term = re * re + im * im
            total = term if total is None else total + term
        store(0, own, total)


def gram_rows(fields, sums, count, first_plane, first_row):
    def one_row(r, carry):
        def store(c, spot, value):
            sums[first_row + r, c, spot] = value

        gram(fields, first_plane + r * 16, 16, store)
        return carry

    lax.fori_loop(0, count, one_row, 0)


def early_kernel(own, sums, *fields):
    _, run = unpacker(fields)
    run(own, 2, 0, 4)
    run(own, 7, 4, 4)
    gram_rows(fields, sums, 2, 0, 0)


def inner_kernel(rest, sums, *fields):
    _, run = unpacker(fields)
    run(rest, 0, 0, 12)
    gram_rows(fields, sums, 3, 0, 0)


def own_rows(kernel, count, *chunks):
    field = pltpu.VMEM((count * 16, WRAP, 128), jnp.float32)
    return pl.pallas_call(
        kernel,
        out_shape=jax.ShapeDtypeStruct((count, 2, PAIRS, 128), jnp.float32),
        scratch_shapes=[field] * 4,
        compiler_params=pltpu.CompilerParams(vmem_limit_bytes=(4 + 3 * count) << 20),
        cost_estimate=pl.CostEstimate(
            flops=3_000_000_000 * count, bytes_accessed=2_000_000, transcendentals=0
        ),
    )(*chunks)


def link_kernel(
    own, rest, above, below, early, inner, near, band, out,
    z_re, z_im, z_sum, z_dif, sums, tails, extra, cov, vec,
):
    fields = (z_re, z_im, z_sum, z_dif)
    lanes = lax.broadcasted_iota(jnp.int32, (8, 128), 1)
    put, run = unpacker(fields)
    run(above, 1, 0, 6)
    run(own, 0, 6, 2)
    run(own, 11, 8, 2)
    run(below, 0, 10, 6)
    for group in range(4):
        pieces = []
        for source in (2 * group, 2 * group + 1):
            mine = own[source, EARLY_TAIL].astype(jnp.float32)
            others = rest[source, LATE_TAIL].astype(jnp.float32)
            up = above[source, 0].astype(jnp.float32)
            down = below[source, 6].astype(jnp.float32)
            piece = []
            for p in range(4):
                cut = slice(8 * p, 8 * p + 8)
                value = jnp.zeros((8, 128), jnp.float32)
                for part, turn, begin in (
                    (up, 128 - 30, 0),
                    (mine, 18, 18),
                    (others, 42, 42),
                    (mine, 42, 66),
                    (down, 90, 90),
                ):
                    value = jnp.where(lanes >= begin, pltpu.roll(part[cut], turn, 1), value)
                piece.append(jnp.where(lanes < 108, value, 0.0))
            pieces.append(piece)
        for p in range(4):
            put(64 + p, group, pieces[0][p], pieces[1][p])

    def store_tail(c, spot, value):
        tails[c, spot] = value

    gram(fields, 64, 4, store_tail)
    tails[1, 0:DATES] = jnp.zeros((DATES, 128), jnp.float32)
    gram_rows(fields, sums, 4, 0, 0)
    for c in range(2):
        high, low = split(tails[c])
        extra[c] = jnp.dot(
            jnp.concatenate([high, low], axis=1), band[...], preferred_element_type=jnp.float32
        )

    def windows(step, carry):
        size = 2 * DATES
        begin = pl.multiple_of(step * size, size)
        spot = pl.ds(begin, size)
        twice = pl.multiple_of(step * 2 * size, 2 * size)
        for c in range(2):
            rowsum = [sums[r, c, spot] for r in (0, 1)]
            rowsum += [early[0, c, spot]] + [inner[r, c, spot] for r in range(3)]
            rowsum += [early[1, c, spot]]
            rowsum += [sums[r, c, spot] for r in (2, 3)]
            pairs = [rowsum[r] + rowsum[r + 1] for r in range(8)]
            value = jnp.concatenate([pairs[a] + pairs[a + 2] for a in range(6)], axis=0)
            high, low = split(value)
            found = jnp.dot(
                jnp.concatenate([high, low], axis=1), near[...], preferred_element_type=jnp.float32
            )
            for a in range(6):
                full = found[a * size : (a + 1) * size] + extra[c, spot, a * 128 : a * 128 + 128]
                for i in range(2):
                    half = full[i * DATES : (i + 1) * DATES]
                    cov[a, c, pl.ds(twice + 2 * i * DATES, DATES)] = half
                    cov[a, c, pl.ds(twice + (2 * i + 1) * DATES, DATES)] = half
        return carry

    lax.fori_loop(0, (SHIFTS + 1) // 2, windows, 0)

    def put_vec(c, group, value):
        for copy in range(3):
            vec[c, copy * DATES + group * 8 : copy * DATES + group * 8 + 8] = value

    def window_row(a, carry):
        weights = []
        for group in range(4):
            power = cov[a, 0, 8 * group : 8 * group + 8]
            weights.append(1.0 / jnp.sqrt(power + BETA_LOAD))
            put_vec(0, group, weights[group])

        def iterate(real, last):
            sums = [[None, None] for _ in range(4)]
            for s in range(SHIFTS):
                for group in range(4):
                    row = 8 * group
                    re_parts, im_parts = [], []
                    terms = [(2 * s * DATES + row, DATES + row + s, 1)]
                    if 0 < s < SHIFTS - 1:
                        terms.append((2 * s * DATES + DATES + row - s, DATES + row - s, -1))
                    for place, other, sign in terms:
                        cov_re = cov[a, 0, place : place + 8]
                        x_re = vec[0, other : other + 8]
                        x_im = None if real else vec[1, other : other + 8]
                        if s == 0:
                            re = cov_re * x_re
                            im = None if real else cov_re * x_im
                        else:
                            cov_im = cov[a, 1, place : place + 8]
                            re = cov_re * x_re
                            im = cov_im * x_re
                            if sign < 0:
                                im = -im if real else cov_re * x_im - im
                                re = re if real else re + cov_im * x_im
                            elif not real:
                                re = re - cov_im * x_im
                                im = im + cov_re * x_im
                        re_parts.append(re)
                        if im is not None:
                            im_parts.append(im)
                    for k, parts in enumerate((re_parts, im_parts)):
                        if parts:
                            part = parts[0] if len(parts) == 1 else parts[0] + parts[1]
                            sums[group][k] = part if sums[group][k] is None else sums[group][k] + part
            found = sums
            for group in range(4):
                u_re = found[group][0] * weights[group]
                u_im = found[group][1] * weights[group]
                length = 1.0 / jnp.sqrt(u_re * u_re + u_im * u_im + PROJ_LOAD)
                x_re, x_im = u_re * length, u_im * length
                if last:
                    out[0, a, 8 * group : 8 * group + 8] = x_re
                    out[1, a, 8 * group : 8 * group + 8] = x_im
                else:
                    put_vec(0, group, x_re * weights[group])
                    put_vec(1, group, x_im * weights[group])

        iterate(True, False)
        for _ in range(ITERS - 2):
            iterate(False, False)
        iterate(False, True)
        return carry

    lax.fori_loop(0, 6, window_row, 0)


def tail_band():
    near = np.zeros((128, 128), np.float32)
    for block in range(128):
        near[block, max(block - 3, 0) : block + 1] = 1.0
    band = np.zeros((6, 128, 128), np.float32)
    for row in range(6):
        for line in range(4 * row, 4 * row + 16):
            for block in range(3):
                band[row, line * 3 + block, 125 + block :] = 1.0
    both = np.concatenate(list(band), axis=1)
    both = np.concatenate([both, both], axis=0).astype(jnp.bfloat16)
    return np.concatenate([near, near], axis=0).astype(jnp.bfloat16), both


def link_windows(own, rest, above, below, early, inner):
    field = pltpu.VMEM((68, WRAP, 128), jnp.float32)
    found = pl.pallas_call(
        link_kernel,
        out_shape=jax.ShapeDtypeStruct((2, 6, DATES, 128), jnp.float32),
        scratch_shapes=[field] * 4
        + [
            pltpu.VMEM((4, 2, PAIRS, 128), jnp.float32),
            pltpu.VMEM((2, PAIRS, 128), jnp.float32),
            pltpu.VMEM((2, PAIRS, 6 * 128), jnp.float32),
            pltpu.VMEM((6, 2, 2 * PAIRS, 128), jnp.float32),
            pltpu.VMEM((2, 3 * DATES, 128), jnp.float32),
        ],
        compiler_params=pltpu.CompilerParams(vmem_limit_bytes=28 << 20),
        cost_estimate=pl.CostEstimate(
            flops=20_000_000_000, bytes_accessed=8_000_000, transcendentals=0
        ),
        name="link_windows",
    )(own, rest, above, below, early, inner, *tail_band())
    return jnp.transpose(found, (0, 2, 1, 3))


def on_device(stack, range_filter, scatter_mask):
    def move(tiles):
        return lax.all_to_all(tiles, "dr", split_axis=0, concat_axis=0, tiled=True)

    tiles, kept = filter_lines(stack, range_filter, scatter_mask, FIRST, GROUP_FIRST)
    own = move(tiles)
    tiles = filter_lines(stack, range_filter, scatter_mask, SECOND, GROUP_SECOND, kept)
    rest = move(tiles)
    count = lax.axis_size("az")
    down = [(i, i + 1) for i in range(count - 1)]
    up = [(i + 1, i) for i in range(count - 1)]
    above = lax.ppermute(own[:, 6:13], "az", down)
    below = lax.ppermute(own[:, 0:7], "az", up)
    early = own_rows(early_kernel, 2, own)
    inner = own_rows(inner_kernel, 3, rest)
    return link_windows(own, rest, above, below, early, inner)


def solution(mesh):
    in_specs = (P(None, "dr", "az", None), P("dr", None), P("az", None))
    out_specs = P(None, None, "az", "dr")
    return jax.shard_map(
        on_device, mesh=mesh, in_specs=in_specs, out_specs=out_specs, check_vma=False
    )
```

```python
import math

import jax
import jax.numpy as jnp
import numpy as np
from jax import lax
from jax.experimental import pallas as pl
from jax.experimental.pallas import tpu as pltpu
from jax.sharding import PartitionSpec as P


ITERS = 4
BETA_LOAD = 1.0
PROJ_LOAD = 1.0

DATES = 32
RG = 4096
TILES = 8
HALO = 6
PLANES = 32
HERE = 4
FIRST, SECOND = (0, 16), (8,)
KEPT = (6, 7, 16, 17)
GROUP_FIRST, GROUP_SECOND = 8, 16
SHIFTS = 17
PAIRS = (SHIFTS + 1) * DATES
WRAP = 48


def slot_of(line):
    if 6 <= line < 18:
        return line - 6
    return line if line < 6 else line - 11


EARLY_TAIL, LATE_TAIL, SLOTS = 6, 12, 13


def tables():
    lane = np.arange(128)
    freq = 4 * (lane % 32) + lane // 32
    turn = 2.0 * np.pi / 128 * (np.outer(lane, freq) % 128)
    forward = np.block([[np.cos(turn), -np.sin(turn)], [np.sin(turn), np.cos(turn)]])
    turn = 2.0 * np.pi / 128 * (np.outer(freq, lane - HALO) % 128)
    inverse = np.block([[np.cos(turn), np.sin(turn)], [-np.sin(turn), np.cos(turn)]]) / RG
    plane = np.arange(PLANES)
    angle = 2.0 * np.pi / RG * np.outer(plane, lane)
    back = 2.0 * np.pi / RG * np.outer(plane, lane - HALO)
    parts = [forward[:, :128], forward[:, 128:], inverse[:, :128], inverse[:, 128:]]
    parts += [np.cos(angle), np.sin(angle), np.cos(back), np.sin(back)]
    return np.concatenate(parts, axis=0).astype(np.float32)


def cmul(value, cos, sin):
    re, im = value
    if abs(sin) < 1e-12:
        return (re, im) if cos > 0 else (-re, -im)
    if abs(cos) < 1e-12:
        return (-im, re) if sin > 0 else (im, -re)
    if abs(abs(cos) - abs(sin)) < 1e-12:
        size = abs(cos)
        if cos > 0 and sin > 0:
            return ((re - im) * size, (re + im) * size)
        if cos > 0:
            return ((re + im) * size, (im - re) * size)
        if sin > 0:
            return ((-re - im) * size, (re - im) * size)
        return ((im - re) * size, (-re - im) * size)
    return (re * cos - im * sin, im * cos + re * sin)


def small_dft(values, sign):
    count = len(values)
    if count == 1:
        return values
    even = small_dft(values[0::2], sign)
    odd = small_dft(values[1::2], sign)
    half = count // 2
    low, high = [], []
    for k in range(half):
        angle = sign * 2.0 * math.pi * k / count
        re, im = cmul(odd[k], math.cos(angle), math.sin(angle))
        low.append((even[k][0] + re, even[k][1] + im))
        high.append((even[k][0] - re, even[k][1] - im))
    return low + high


def dft_planes(load, hold, store, sign):
    for m in range(8):
        parts = small_dft([load(8 * i + m) for i in range(4)], sign)
        for s in range(4):
            angle = sign * 2.0 * math.pi * m * s / 32
            re, im = cmul(parts[s], math.cos(angle), math.sin(angle))
            hold[0, s * 8 + m] = re
            hold[1, s * 8 + m] = im
    for s in range(4):
        parts = small_dft([(hold[0, s * 8 + m], hold[1, s * 8 + m]) for m in range(8)], sign)
        for u in range(8):
            store(s + 4 * u, *parts[u])


def split(values):
    high = values.astype(jnp.bfloat16)
    return high, (values - high.astype(jnp.float32)).astype(jnp.bfloat16)


def dot3(values, table):
    high, low = split(values)
    return jnp.dot(
        jnp.concatenate([high, low, high], axis=1), table, preferred_element_type=jnp.float32
    )


def filter_kernel(
    blocks, group, stack, gains, mask, table, kept, out,
    raw, gains_in, mask_in, table_in, sem,
    spec, first, hold, held, gain, weights, lines_out, forward, inverse, place,
):
    count = len(blocks)
    lines_here = 8 * count
    rows_here = HERE * lines_here
    pitch = lines_here + 1
    early = blocks == FIRST
    stack_copies = []
    for d in range(HERE):
        for i, block in enumerate(blocks):
            for c in range(2):
                stack_copies.append(
                    pltpu.make_async_copy(
                        stack.at[c, d, pl.ds(block, 8)],
                        raw.at[c, d * count + i],
                        sem.at[c * HERE * count + d * count + i],
                    )
                )
    copies = {}
    for i, (name, source, target) in enumerate(
        (("table", table, table_in), ("gains", gains, gains_in))
    ):
        copies[name] = pltpu.make_async_copy(source, target, sem.at[9 * count + i])
    for i, block in enumerate(blocks):
        copies["mask", i] = pltpu.make_async_copy(
            mask.at[pl.ds(block, 8)], mask_in.at[pl.ds(8 * i, 8)], sem.at[8 * count + i]
        )
    first_copies = [copies["gains"], copies["table"]]
    last_copies = [copies["mask", i] for i in range(count)]
    for copy in first_copies + stack_copies + last_copies:
        copy.start()
    lanes = lax.broadcasted_iota(jnp.int32, (8, 128), 1)
    row = lax.broadcasted_iota(jnp.int32, (512, 128), 0)
    column = lax.broadcasted_iota(jnp.int32, (512, 128), 1)
    for p in range(4):
        place[:, 128 * p : 128 * p + 128] = jnp.where(row == 4 * column + p, 1.0, 0.0).astype(
            jnp.bfloat16
        )

    copies["gains"].wait()
    for n in range(PLANES):
        four = gains_in[:, n * 128 : (n + 1) * 128]
        for d in range(HERE):
            gain[d, n : n + 1] = four[d : d + 1]
    for d in range(HERE):
        turned = jnp.transpose(gain[d])
        gain[d] = jnp.concatenate([turned[32 * w : 32 * w + 32] for w in range(4)], axis=1)
    copies["table"].wait()
    for i, target in enumerate((forward, inverse)):
        for half in range(2):
            begin = 256 * (2 * i + half)
            high, low = split(table_in[begin : begin + 256])
            for j, part in enumerate((high, high, low)):
                target[256 * j : 256 * j + 256, 128 * half : 128 * half + 128] = part

    def ahead(block, carry):
        rows = pl.ds(pl.multiple_of(block * 8, 8), 8)

        def store(q, re, im):
            spec[0, q, rows] = re
            spec[1, q, rows] = im

        for c in range(2):
            pltpu.make_async_copy(
                stack.at[0, 0, pl.ds(0, 8)], raw.at[c, block], sem.at[c * HERE * count + block]
            ).wait()

        def load(n):
            lanes = slice(n * 128, (n + 1) * 128)
            return (
                raw[0, block, :, lanes].astype(jnp.float32),
                raw[1, block, :, lanes].astype(jnp.float32),
            )

        dft_planes(load, hold, store, -1)
        return carry

    lax.fori_loop(0, rows_here // 8, ahead, 0)
    steps = PLANES // group

    def ahead_part(step):
        now = step * group
        parts = []
        for i in range(group):
            tc = table_in[pl.ds(1024 + now + i, 1), :]
            ts = table_in[pl.ds(1056 + now + i, 1), :]
            re, im = spec[0, now + i], spec[1, now + i]
            parts.append(jnp.concatenate([re * tc + im * ts, im * tc - re * ts], axis=1))
        found = dot3(jnp.concatenate(parts, axis=0), forward[...])
        slot = step % 2 if isinstance(step, int) else lax.rem(step, 2)
        for i in range(group):
            for d in range(HERE):
                row = gain[d, pl.ds(now + i, 1), :]
                begin = i * rows_here + d * lines_here
                held[slot, begin : begin + lines_here] = found[
                    begin : begin + lines_here
                ] * jnp.concatenate([row, row], axis=1)

    def back_part(step):
        past = step * group
        slot = step % 2 if isinstance(step, int) else lax.rem(step, 2)
        back = dot3(held[slot], inverse[...])
        for i in range(group):
            tc = table_in[pl.ds(1088 + past + i, 1), :]
            ts = table_in[pl.ds(1120 + past + i, 1), :]
            re = back[i * rows_here : (i + 1) * rows_here, :128]
            im = back[i * rows_here : (i + 1) * rows_here, 128:]
            first[0, past + i] = re * tc - im * ts
            first[1, past + i] = im * tc + re * ts

    def middle(step, carry):
        back_part(step - 1)
        ahead_part(step)
        return carry

    ahead_part(0)
    lax.fori_loop(1, steps, middle, 0)
    back_part(steps - 1)

    for i in range(count):
        copies["mask", i].wait()
        rows = slice(8 * i, 8 * i + 8)
        before = pltpu.roll(mask_in[rows, RG - 128 :].astype(jnp.float32), HALO, 1)
        for n in range(PLANES):
            now = pltpu.roll(mask_in[rows, n * 128 : (n + 1) * 128].astype(jnp.float32), HALO, 1)
            joined = jnp.where(lanes < HALO, before, now)
            if n == 0:
                weights[PLANES, rows] = jnp.where(lanes < HALO, joined, 0.0)
                joined = jnp.where(lanes < HALO, 0.0, joined)
            weights[n, rows] = joined
            before = now

    def behind(block, carry):
        rows = pl.ds(pl.multiple_of(block * 8, 8), 8)
        begin = (block // count) * pitch + lax.rem(block, count) * 8
        to_re = pl.ds(begin, 8)
        to_im = pl.ds(begin + HERE * pitch, 8)
        lines = pl.ds(pl.multiple_of(lax.rem(block, count) * 8, 8), 8)

        def store(n, re, im):
            weight = weights[n, lines]
            lines_out[n, to_re] = re * weight
            lines_out[n, to_im] = im * weight
            if n == 0:
                weight = weights[PLANES, lines]
                lines_out[PLANES, to_re] = re * weight
                lines_out[PLANES, to_im] = im * weight

        dft_planes(lambda q: (first[0, q, rows], first[1, q, rows]), hold, store, 1)
        return carry

    lax.fori_loop(0, rows_here // 8, behind, 0)

    def gather(plane):
        return jnp.concatenate(
            [lines_out[plane, pl.ds(line, 8, stride=pitch), :] for line in range(lines_here)],
            axis=0,
        )

    def put_tail(slot, found):
        tails = []
        for p in range(4):
            tail = jnp.zeros((8, 128), jnp.float32)
            for line in range(lines_here):
                part = found[line * 8 : line * 8 + 8, p * 128 : p * 128 + 128]
                if line:
                    part = pltpu.roll(part, 3 * line, 1)
                tail = jnp.where(lanes >= 3 * line, part, tail)
            tails.append(jnp.where(lanes < 3 * lines_here, tail, 0.0))
        out[slot, EARLY_TAIL if early else LATE_TAIL] = jnp.concatenate(tails, axis=0).astype(
            jnp.bfloat16
        )

    def one_tile(t, found):
        for index in range(lines_here):
            line = blocks[index // 8] + index % 8
            value = jnp.concatenate(
                [found[index * 8 : index * 8 + 8, p * 128 : p * 128 + 128] for p in range(4)],
                axis=0,
            ).astype(jnp.bfloat16)
            if early and line in KEPT:
                kept[t, KEPT.index(line)] = value
            else:
                out[t, slot_of(line)] = value
        if not early:
            for index, line in enumerate(KEPT):
                out[t, slot_of(line)] = kept[t, index]
        put_tail(lax.rem(t + TILES - 1, TILES), found)

    def tile(step, carry):
        left = [
            jnp.concatenate([gather(8 * step + 4 * i + v) for v in range(4)], axis=1)
            for i in range(2)
        ]
        found = jnp.dot(
            jnp.concatenate(left, axis=0).astype(jnp.bfloat16),
            place[...],
            preferred_element_type=jnp.float32,
        )
        for i in range(2):
            one_tile(2 * step + i, found[8 * lines_here * i : 8 * lines_here * (i + 1)])
        return carry

    lax.fori_loop(0, TILES // 2, tile, 0)
    found = jnp.dot(
        gather(PLANES).astype(jnp.bfloat16), place[:128], preferred_element_type=jnp.float32
    )
    put_tail(TILES - 1, found)


def filter_lines(stack, gains, mask, blocks, group, kept=None):
    count = len(blocks)
    tiles = jax.ShapeDtypeStruct((TILES, SLOTS, 32, 128), jnp.bfloat16)
    rest = jax.ShapeDtypeStruct((TILES, len(KEPT), 32, 128), jnp.bfloat16)
    hbm = pl.BlockSpec(memory_space=pltpu.MemorySpace.HBM)
    vmem = pl.BlockSpec(memory_space=pltpu.MemorySpace.VMEM)

    def kernel(*refs):
        if blocks == FIRST:
            refs = refs[:4] + (refs[5], refs[4]) + refs[6:]
        filter_kernel(blocks, group, *refs)

    rows = HERE * 8 * count
    return pl.pallas_call(
        kernel,
        out_shape=(tiles, rest) if blocks == FIRST else tiles,
        in_specs=[hbm] * 4 + ([] if blocks == FIRST else [vmem]),
        scratch_shapes=[
            pltpu.VMEM((2, HERE * count, 8, RG), jnp.bfloat16),
            pltpu.VMEM((HERE, RG), jnp.float32),
            pltpu.VMEM((8 * count, RG), jnp.int32),
            pltpu.VMEM((1152, 128), jnp.float32),
            pltpu.SemaphoreType.DMA((9 * count + 2,)),
            pltpu.VMEM((2, PLANES, rows, 128), jnp.float32),
            pltpu.VMEM((2, PLANES, rows, 128), jnp.float32),
            pltpu.VMEM((2, PLANES, 8, 128), jnp.float32),
            pltpu.VMEM((2, group * rows, 256), jnp.float32),
            pltpu.VMEM((HERE, PLANES, 128), jnp.float32),
            pltpu.VMEM((PLANES + 1, 8 * count, 128), jnp.float32),
            pltpu.VMEM((PLANES + 1, 2 * rows + 2 * HERE, 128), jnp.float32),
            pltpu.VMEM((768, 256), jnp.bfloat16),
            pltpu.VMEM((768, 256), jnp.bfloat16),
            pltpu.VMEM((512, 512), jnp.bfloat16),
        ],
        compiler_params=pltpu.CompilerParams(vmem_limit_bytes=65_700_000),
        cost_estimate=pl.CostEstimate(
            flops=2_000_000_000 * count, bytes_accessed=2_000_000, transcendentals=0
        ),
    )(stack, gains, mask, tables(), *(() if kept is None else (kept,)))


def unpacker(fields):
    z_re, z_im, z_sum, z_dif = fields
    rows = lax.broadcasted_iota(jnp.int32, (8, 128), 0)
    low = rows < 4

    def put(plane, group, first, second):
        re = jnp.where(low, first, pltpu.roll(second, 4, 0))
        im = jnp.where(low, pltpu.roll(first, 4, 0), second)
        total, change = re + im, im - re
        z_im[plane, 8 * group : 8 * group + 8] = im
        for begin in [8 * group] + ([32 + 8 * group] if group < 2 else []):
            z_re[plane, begin : begin + 8] = re
            z_sum[plane, begin : begin + 8] = total
            z_dif[plane, begin : begin + 8] = change

    def run(ref, slot, line, count):
        def step(i, carry):
            for group in range(4):
                first = ref[2 * group, slot + i].astype(jnp.float32)
                second = ref[2 * group + 1, slot + i].astype(jnp.float32)
                for p in range(4):
                    cut = slice(8 * p, 8 * p + 8)
                    put((line + i) * 4 + p, group, first[cut], second[cut])
            return carry

        lax.fori_loop(0, count, step, 0)

    return put, run


WIDTH = 8


def gram(fields, base, count, store):
    z_re, z_im, z_sum, z_dif = fields

    def block(index, carry):
        group = index // 2
        own = pl.ds(pl.multiple_of(group * 8, 8), 8)
        begin = pl.multiple_of(group * 8 + lax.rem(index, 2) * 8, 8)
        unit = min(8, count)

        def some(chunk, totals):
            totals = [list(totals[3 * i : 3 * i + 3]) for i in range(WIDTH)]
            for step in range(0, unit, 2):
                pair = [base + chunk * unit + step + q for q in range(2)]
                mine = [(z_sum[p, own], z_re[p, own], z_im[p, own]) for p in pair]
                for i in range(WIDTH):
                    other = pl.ds(begin + 1 + i, 8)
                    for k, ref in enumerate((z_re, z_sum, z_dif)):
                        terms = [ref[p, other] * part[k] for p, part in zip(pair, mine)]
                        totals[i][k] = totals[i][k] + (terms[0] + terms[1])
            return tuple(t for total in totals for t in total)

        zero = jnp.zeros((8, 128), jnp.float32)
        totals = lax.fori_loop(0, count // unit, some, (zero,) * (3 * WIDTH))
        totals = [totals[3 * i : 3 * i + 3] for i in range(WIDTH)]
        for i in range(WIDTH):
            one, two, three = totals[i]
            spot = (lax.rem(index, 2) * 8 + 1 + i) * DATES + group * 8
            spot = pl.ds(pl.multiple_of(spot, 8), 8)
            store(0, spot, one + three)
            store(1, spot, one - two)
        return carry

    lax.fori_loop(0, 8, block, 0)
    for group in range(4):
        own = slice(8 * group, 8 * group + 8)
        total = None
        for step in range(count):
            re, im = z_re[base + step, own], z_im[base + step, own]
            term = re * re + im * im
            total = term if total is None else total + term
        store(0, own, total)


def gram_rows(fields, sums, count, first_plane, first_row):
    def one_row(r, carry):
        def store(c, spot, value):
            sums[first_row + r, c, spot] = value

        gram(fields, first_plane + r * 16, 16, store)
        return carry

    lax.fori_loop(0, count, one_row, 0)


def early_kernel(own, sums, *fields):
    _, run = unpacker(fields)
    run(own, 2, 0, 4)
    run(own, 7, 4, 4)
    gram_rows(fields, sums, 2, 0, 0)


def inner_kernel(rest, sums, *fields):
    _, run = unpacker(fields)
    run(rest, 0, 0, 12)
    gram_rows(fields, sums, 3, 0, 0)


def upper_kernel(own, above, sums, *fields):
    _, run = unpacker(fields)
    run(above, 1, 0, 6)
    run(own, 0, 6, 2)
    gram_rows(fields, sums, 2, 0, 0)


def own_rows(kernel, count, *chunks):
    field = pltpu.VMEM((count * 16, WRAP, 128), jnp.float32)
    return pl.pallas_call(
        kernel,
        out_shape=jax.ShapeDtypeStruct((count, 2, PAIRS, 128), jnp.float32),
        scratch_shapes=[field] * 4,
        compiler_params=pltpu.CompilerParams(vmem_limit_bytes=(4 + 3 * count) << 20),
        cost_estimate=pl.CostEstimate(
            flops=3_000_000_000 * count, bytes_accessed=2_000_000, transcendentals=0
        ),
    )(*chunks)


def link_kernel(
    own, rest, above, below, upper, early, inner, near, band, out,
    z_re, z_im, z_sum, z_dif, sums, tails, extra, cov, vec,
):
    fields = (z_re, z_im, z_sum, z_dif)
    lanes = lax.broadcasted_iota(jnp.int32, (8, 128), 1)
    put, run = unpacker(fields)
    run(own, 11, 0, 2)
    run(below, 0, 2, 6)
    for group in range(4):
        pieces = []
        for source in (2 * group, 2 * group + 1):
            mine = own[source, EARLY_TAIL].astype(jnp.float32)
            others = rest[source, LATE_TAIL].astype(jnp.float32)
            up = above[source, 0].astype(jnp.float32)
            down = below[source, 6].astype(jnp.float32)
            piece = []
            for p in range(4):
                cut = slice(8 * p, 8 * p + 8)
                value = jnp.zeros((8, 128), jnp.float32)
                for part, turn, begin in (
                    (up, 128 - 30, 0),
                    (mine, 18, 18),
                    (others, 42, 42),
                    (mine, 42, 66),
                    (down, 90, 90),
                ):
                    value = jnp.where(lanes >= begin, pltpu.roll(part[cut], turn, 1), value)
                piece.append(jnp.where(lanes < 108, value, 0.0))
            pieces.append(piece)
        for p in range(4):
            put(32 + p, group, pieces[0][p], pieces[1][p])

    def store_tail(c, spot, value):
        tails[c, spot] = value

    gram(fields, 32, 4, store_tail)
    tails[1, 0:DATES] = jnp.zeros((DATES, 128), jnp.float32)
    gram_rows(fields, sums, 2, 0, 0)
    for c in range(2):
        high, low = split(tails[c])
        extra[c] = jnp.dot(
            jnp.concatenate([high, low], axis=1), band[...], preferred_element_type=jnp.float32
        )

    def windows(step, carry):
        size = 2 * DATES
        begin = pl.multiple_of(step * size, size)
        spot = pl.ds(begin, size)
        twice = pl.multiple_of(step * 2 * size, 2 * size)
        for c in range(2):
            rowsum = [upper[r, c, spot] for r in (0, 1)]
            rowsum += [early[0, c, spot]] + [inner[r, c, spot] for r in range(3)]
            rowsum += [early[1, c, spot]]
            rowsum += [sums[r, c, spot] for r in (0, 1)]
            pairs = [rowsum[r] + rowsum[r + 1] for r in range(8)]
            value = jnp.concatenate([pairs[a] + pairs[a + 2] for a in range(6)], axis=0)
            high, low = split(value)
            found = jnp.dot(
                jnp.concatenate([high, low], axis=1), near[...], preferred_element_type=jnp.float32
            )
            for a in range(6):
                full = found[a * size : (a + 1) * size] + extra[c, spot, a * 128 : a * 128 + 128]
                for i in range(2):
                    half = full[i * DATES : (i + 1) * DATES]
                    cov[a, c, pl.ds(twice + 2 * i * DATES, DATES)] = half
                    cov[a, c, pl.ds(twice + (2 * i + 1) * DATES, DATES)] = half
        return carry

    lax.fori_loop(0, (SHIFTS + 1) // 2, windows, 0)

    def put_vec(c, group, value):
        for copy in range(3):
            vec[c, copy * DATES + group * 8 : copy * DATES + group * 8 + 8] = value

    def window_row(a, carry):
        weights = []
        for group in range(4):
            power = cov[a, 0, 8 * group : 8 * group + 8]
            weights.append(1.0 / jnp.sqrt(power + BETA_LOAD))
            put_vec(0, group, weights[group])

        def iterate(real, last):
            sums = [[None, None] for _ in range(4)]
            for s in range(SHIFTS):
                for group in range(4):
                    row = 8 * group
                    re_parts, im_parts = [], []
                    terms = [(2 * s * DATES + row, DATES + row + s, 1)]
                    if 0 < s < SHIFTS - 1:
                        terms.append((2 * s * DATES + DATES + row - s, DATES + row - s, -1))
                    for place, other, sign in terms:
                        cov_re = cov[a, 0, place : place + 8]
                        x_re = vec[0, other : other + 8]
                        x_im = None if real else vec[1, other : other + 8]
                        if s == 0:
                            re = cov_re * x_re
                            im = None if real else cov_re * x_im
                        else:
                            cov_im = cov[a, 1, place : place + 8]
                            re = cov_re * x_re
                            im = cov_im * x_re
                            if sign < 0:
                                im = -im if real else cov_re * x_im - im
                                re = re if real else re + cov_im * x_im
                            elif not real:
                                re = re - cov_im * x_im
                                im = im + cov_re * x_im
                        re_parts.append(re)
                        if im is not None:
                            im_parts.append(im)
                    for k, parts in enumerate((re_parts, im_parts)):
                        if parts:
                            part = parts[0] if len(parts) == 1 else parts[0] + parts[1]
                            sums[group][k] = part if sums[group][k] is None else sums[group][k] + part
            found = sums
            for group in range(4):
                u_re = found[group][0] * weights[group]
                u_im = found[group][1] * weights[group]
                length = 1.0 / jnp.sqrt(u_re * u_re + u_im * u_im + PROJ_LOAD)
                x_re, x_im = u_re * length, u_im * length
                if last:
                    out[0, a, 8 * group : 8 * group + 8] = x_re
                    out[1, a, 8 * group : 8 * group + 8] = x_im
                else:
                    put_vec(0, group, x_re * weights[group])
                    put_vec(1, group, x_im * weights[group])

        iterate(True, False)
        for _ in range(ITERS - 2):
            iterate(False, False)
        iterate(False, True)
        return carry

    lax.fori_loop(0, 6, window_row, 0)


def tail_band():
    near = np.zeros((128, 128), np.float32)
    for block in range(128):
        near[block, max(block - 3, 0) : block + 1] = 1.0
    band = np.zeros((6, 128, 128), np.float32)
    for row in range(6):
        for line in range(4 * row, 4 * row + 16):
            for block in range(3):
                band[row, line * 3 + block, 125 + block :] = 1.0
    both = np.concatenate(list(band), axis=1)
    both = np.concatenate([both, both], axis=0).astype(jnp.bfloat16)
    return np.concatenate([near, near], axis=0).astype(jnp.bfloat16), both


def link_windows(own, rest, above, below, upper, early, inner):
    field = pltpu.VMEM((36, WRAP, 128), jnp.float32)
    found = pl.pallas_call(
        link_kernel,
        out_shape=jax.ShapeDtypeStruct((2, 6, DATES, 128), jnp.float32),
        scratch_shapes=[field] * 4
        + [
            pltpu.VMEM((2, 2, PAIRS, 128), jnp.float32),
            pltpu.VMEM((2, PAIRS, 128), jnp.float32),
            pltpu.VMEM((2, PAIRS, 6 * 128), jnp.float32),
            pltpu.VMEM((6, 2, 2 * PAIRS, 128), jnp.float32),
            pltpu.VMEM((2, 3 * DATES, 128), jnp.float32),
        ],
        compiler_params=pltpu.CompilerParams(vmem_limit_bytes=28 << 20),
        cost_estimate=pl.CostEstimate(
            flops=20_000_000_000, bytes_accessed=8_000_000, transcendentals=0
        ),
        name="link_windows",
    )(own, rest, above, below, upper, early, inner, *tail_band())
    return jnp.transpose(found, (0, 2, 1, 3))


def on_device(stack, range_filter, scatter_mask):
    def move(tiles):
        return lax.all_to_all(tiles, "dr", split_axis=0, concat_axis=0, tiled=True)

    tiles, kept = filter_lines(stack, range_filter, scatter_mask, FIRST, GROUP_FIRST)
    own = move(tiles)
    tiles = filter_lines(stack, range_filter, scatter_mask, SECOND, GROUP_SECOND, kept)
    rest = move(tiles)
    count = lax.axis_size("az")
    down = [(i, i + 1) for i in range(count - 1)]
    up = [(i + 1, i) for i in range(count - 1)]
    above = lax.ppermute(own[:, 6:13], "az", down)
    below = lax.ppermute(own[:, 0:7], "az", up)
    early = own_rows(early_kernel, 2, own)
    inner = own_rows(inner_kernel, 3, rest)
    upper = own_rows(upper_kernel, 2, own, above)
    return link_windows(own, rest, above, below, upper, early, inner)


def solution(mesh):
    in_specs = (P(None, "dr", "az", None), P("dr", None), P("az", None))
    out_specs = P(None, None, "az", "dr")
    return jax.shard_map(
        on_device, mesh=mesh, in_specs=in_specs, out_specs=out_specs, check_vma=False
    )
```

```python
import math

import jax
import jax.numpy as jnp
import numpy as np
from jax import lax
from jax.experimental import pallas as pl
from jax.experimental.pallas import tpu as pltpu
from jax.sharding import PartitionSpec as P


ITERS = 4
BETA_LOAD = 1.0
PROJ_LOAD = 1.0

DATES = 32
RG = 4096
TILES = 8
HALO = 6
PLANES = 32
HERE = 4
FIRST, SECOND = (0, 16), (8,)
KEPT = (6, 7, 16, 17)
GROUP_FIRST, GROUP_SECOND = 8, 16
SHIFTS = 17
PAIRS = (SHIFTS + 1) * DATES
WRAP = 48


def slot_of(line):
    if 6 <= line < 18:
        return line - 6
    return line if line < 6 else line - 11


EARLY_TAIL, LATE_TAIL, SLOTS = 6, 12, 13


def tables():
    lane = np.arange(128)
    freq = 4 * (lane % 32) + lane // 32
    turn = 2.0 * np.pi / 128 * (np.outer(lane, freq) % 128)
    forward = np.block([[np.cos(turn), -np.sin(turn)], [np.sin(turn), np.cos(turn)]])
    turn = 2.0 * np.pi / 128 * (np.outer(freq, lane - HALO) % 128)
    inverse = np.block([[np.cos(turn), np.sin(turn)], [-np.sin(turn), np.cos(turn)]]) / RG
    plane = np.arange(PLANES)
    angle = 2.0 * np.pi / RG * np.outer(plane, lane)
    back = 2.0 * np.pi / RG * np.outer(plane, lane - HALO)
    parts = [forward[:, :128], forward[:, 128:], inverse[:, :128], inverse[:, 128:]]
    parts += [np.cos(angle), np.sin(angle), np.cos(back), np.sin(back)]
    return np.concatenate(parts, axis=0).astype(np.float32)


def cmul(value, cos, sin):
    re, im = value
    if abs(sin) < 1e-12:
        return (re, im) if cos > 0 else (-re, -im)
    if abs(cos) < 1e-12:
        return (-im, re) if sin > 0 else (im, -re)
    if abs(abs(cos) - abs(sin)) < 1e-12:
        size = abs(cos)
        if cos > 0 and sin > 0:
            return ((re - im) * size, (re + im) * size)
        if cos > 0:
            return ((re + im) * size, (im - re) * size)
        if sin > 0:
            return ((-re - im) * size, (re - im) * size)
        return ((im - re) * size, (-re - im) * size)
    return (re * cos - im * sin, im * cos + re * sin)


def small_dft(values, sign):
    count = len(values)
    if count == 1:
        return values
    even = small_dft(values[0::2], sign)
    odd = small_dft(values[1::2], sign)
    half = count // 2
    low, high = [], []
    for k in range(half):
        angle = sign * 2.0 * math.pi * k / count
        re, im = cmul(odd[k], math.cos(angle), math.sin(angle))
        low.append((even[k][0] + re, even[k][1] + im))
        high.append((even[k][0] - re, even[k][1] - im))
    return low + high


def dft_planes(load, hold, store, sign):
    for m in range(8):
        parts = small_dft([load(8 * i + m) for i in range(4)], sign)
        for s in range(4):
            angle = sign * 2.0 * math.pi * m * s / 32
            re, im = cmul(parts[s], math.cos(angle), math.sin(angle))
            hold[0, s * 8 + m] = re
            hold[1, s * 8 + m] = im
    for s in range(4):
        parts = small_dft([(hold[0, s * 8 + m], hold[1, s * 8 + m]) for m in range(8)], sign)
        for u in range(8):
            store(s + 4 * u, *parts[u])


def split(values):
    high = values.astype(jnp.bfloat16)
    return high, (values - high.astype(jnp.float32)).astype(jnp.bfloat16)


def dot3(values, table):
    high, low = split(values)
    return jnp.dot(
        jnp.concatenate([high, low, high], axis=1), table, preferred_element_type=jnp.float32
    )


def filter_kernel(
    blocks, group, stack, gains, mask, table, kept, out,
    raw, gains_in, mask_in, table_in, sem,
    spec, first, hold, held, gain, weights, lines_out, forward, inverse, place,
):
    count = len(blocks)
    lines_here = 8 * count
    rows_here = HERE * lines_here
    pitch = lines_here + 1
    early = blocks == FIRST
    stack_copies = []
    for d in range(HERE):
        for i, block in enumerate(blocks):
            for c in range(2):
                stack_copies.append(
                    pltpu.make_async_copy(
                        stack.at[c, d, pl.ds(block, 8)],
                        raw.at[c, d * count + i],
                        sem.at[c * HERE * count + d * count + i],
                    )
                )
    copies = {}
    for i, (name, source, target) in enumerate(
        (("table", table, table_in), ("gains", gains, gains_in))
    ):
        copies[name] = pltpu.make_async_copy(source, target, sem.at[9 * count + i])
    for i, block in enumerate(blocks):
        copies["mask", i] = pltpu.make_async_copy(
            mask.at[pl.ds(block, 8)], mask_in.at[pl.ds(8 * i, 8)], sem.at[8 * count + i]
        )
    first_copies = [copies["gains"], copies["table"]]
    last_copies = [copies["mask", i] for i in range(count)]
    for copy in first_copies + stack_copies + last_copies:
        copy.start()
    lanes = lax.broadcasted_iota(jnp.int32, (8, 128), 1)
    row = lax.broadcasted_iota(jnp.int32, (512, 128), 0)
    column = lax.broadcasted_iota(jnp.int32, (512, 128), 1)
    for p in range(4):
        place[:, 128 * p : 128 * p + 128] = jnp.where(row == 4 * column + p, 1.0, 0.0).astype(
            jnp.bfloat16
        )

    copies["gains"].wait()
    for n in range(PLANES):
        four = gains_in[:, n * 128 : (n + 1) * 128]
        for d in range(HERE):
            gain[d, n : n + 1] = four[d : d + 1]
    for d in range(HERE):
        turned = jnp.transpose(gain[d])
        gain[d] = jnp.concatenate([turned[32 * w : 32 * w + 32] for w in range(4)], axis=1)
    copies["table"].wait()
    for i, target in enumerate((forward, inverse)):
        for half in range(2):
            begin = 256 * (2 * i + half)
            high, low = split(table_in[begin : begin + 256])
            for j, part in enumerate((high, high, low)):
                target[256 * j : 256 * j + 256, 128 * half : 128 * half + 128] = part

    def ahead(block, carry):
        rows = pl.ds(pl.multiple_of(block * 8, 8), 8)

        def store(q, re, im):
            spec[0, q, rows] = re
            spec[1, q, rows] = im

        for c in range(2):
            pltpu.make_async_copy(
                stack.at[0, 0, pl.ds(0, 8)], raw.at[c, block], sem.at[c * HERE * count + block]
            ).wait()

        def load(n):
            lanes = slice(n * 128, (n + 1) * 128)
            return (
                raw[0, block, :, lanes].astype(jnp.float32),
                raw[1, block, :, lanes].astype(jnp.float32),
            )

        dft_planes(load, hold, store, -1)
        return carry

    lax.fori_loop(0, rows_here // 8, ahead, 0)
    steps = PLANES // group

    def ahead_part(step):
        now = step * group
        parts = []
        for i in range(group):
            tc = table_in[pl.ds(1024 + now + i, 1), :]
            ts = table_in[pl.ds(1056 + now + i, 1), :]
            re, im = spec[0, now + i], spec[1, now + i]
            parts.append(jnp.concatenate([re * tc + im * ts, im * tc - re * ts], axis=1))
        found = dot3(jnp.concatenate(parts, axis=0), forward[...])
        slot = step % 2 if isinstance(step, int) else lax.rem(step, 2)
        for i in range(group):
            for d in range(HERE):
                row = gain[d, pl.ds(now + i, 1), :]
                begin = i * rows_here + d * lines_here
                held[slot, begin : begin + lines_here] = found[
                    begin : begin + lines_here
                ] * jnp.concatenate([row, row], axis=1)

    def back_part(step):
        past = step * group
        slot = step % 2 if isinstance(step, int) else lax.rem(step, 2)
        back = dot3(held[slot], inverse[...])
        for i in range(group):
            tc = table_in[pl.ds(1088 + past + i, 1), :]
            ts = table_in[pl.ds(1120 + past + i, 1), :]
            re = back[i * rows_here : (i + 1) * rows_here, :128]
            im = back[i * rows_here : (i + 1) * rows_here, 128:]
            first[0, past + i] = re * tc - im * ts
            first[1, past + i] = im * tc + re * ts

    def middle(step, carry):
        back_part(step - 1)
        ahead_part(step)
        return carry

    ahead_part(0)
    lax.fori_loop(1, steps, middle, 0)
    back_part(steps - 1)

    for i in range(count):
        copies["mask", i].wait()
        rows = slice(8 * i, 8 * i + 8)
        before = pltpu.roll(mask_in[rows, RG - 128 :].astype(jnp.float32), HALO, 1)
        for n in range(PLANES):
            now = pltpu.roll(mask_in[rows, n * 128 : (n + 1) * 128].astype(jnp.float32), HALO, 1)
            joined = jnp.where(lanes < HALO, before, now)
            if n == 0:
                weights[PLANES, rows] = jnp.where(lanes < HALO, joined, 0.0)
                joined = jnp.where(lanes < HALO, 0.0, joined)
            weights[n, rows] = joined
            before = now

    def behind(block, carry):
        rows = pl.ds(pl.multiple_of(block * 8, 8), 8)
        begin = (block // count) * pitch + lax.rem(block, count) * 8
        to_re = pl.ds(begin, 8)
        to_im = pl.ds(begin + HERE * pitch, 8)
        lines = pl.ds(pl.multiple_of(lax.rem(block, count) * 8, 8), 8)

        def store(n, re, im):
            weight = weights[n, lines]
            lines_out[n, to_re] = re * weight
            lines_out[n, to_im] = im * weight
            if n == 0:
                weight = weights[PLANES, lines]
                lines_out[PLANES, to_re] = re * weight
                lines_out[PLANES, to_im] = im * weight

        dft_planes(lambda q: (first[0, q, rows], first[1, q, rows]), hold, store, 1)
        return carry

    lax.fori_loop(0, rows_here // 8, behind, 0)

    def gather(plane):
        return jnp.concatenate(
            [lines_out[plane, pl.ds(line, 8, stride=pitch), :] for line in range(lines_here)],
            axis=0,
        )

    def put_tail(slot, found):
        tails = []
        for p in range(4):
            tail = jnp.zeros((8, 128), jnp.float32)
            for line in range(lines_here):
                part = found[line * 8 : line * 8 + 8, p * 128 : p * 128 + 128]
                if line:
                    part = pltpu.roll(part, 3 * line, 1)
                tail = jnp.where(lanes >= 3 * line, part, tail)
            tails.append(jnp.where(lanes < 3 * lines_here, tail, 0.0))
        out[slot, EARLY_TAIL if early else LATE_TAIL] = jnp.concatenate(tails, axis=0).astype(
            jnp.bfloat16
        )

    def one_tile(t, found):
        for index in range(lines_here):
            line = blocks[index // 8] + index % 8
            value = jnp.concatenate(
                [found[index * 8 : index * 8 + 8, p * 128 : p * 128 + 128] for p in range(4)],
                axis=0,
            ).astype(jnp.bfloat16)
            if early and line in KEPT:
                kept[t, KEPT.index(line)] = value
            else:
                out[t, slot_of(line)] = value
        if not early:
            for index, line in enumerate(KEPT):
                out[t, slot_of(line)] = kept[t, index]
        put_tail(lax.rem(t + TILES - 1, TILES), found)

    def tile(step, carry):
        left = [
            jnp.concatenate([gather(8 * step + 4 * i + v) for v in range(4)], axis=1)
            for i in range(2)
        ]
        found = jnp.dot(
            jnp.concatenate(left, axis=0).astype(jnp.bfloat16),
            place[...],
            preferred_element_type=jnp.float32,
        )
        for i in range(2):
            one_tile(2 * step + i, found[8 * lines_here * i : 8 * lines_here * (i + 1)])
        return carry

    lax.fori_loop(0, TILES // 2, tile, 0)
    found = jnp.dot(
        gather(PLANES).astype(jnp.bfloat16), place[:128], preferred_element_type=jnp.float32
    )
    put_tail(TILES - 1, found)


def filter_lines(stack, gains, mask, blocks, group, kept=None):
    count = len(blocks)
    tiles = jax.ShapeDtypeStruct((TILES, SLOTS, 32, 128), jnp.bfloat16)
    rest = jax.ShapeDtypeStruct((TILES, len(KEPT), 32, 128), jnp.bfloat16)
    hbm = pl.BlockSpec(memory_space=pltpu.MemorySpace.HBM)
    vmem = pl.BlockSpec(memory_space=pltpu.MemorySpace.VMEM)

    def kernel(*refs):
        if blocks == FIRST:
            refs = refs[:4] + (refs[5], refs[4]) + refs[6:]
        filter_kernel(blocks, group, *refs)

    rows = HERE * 8 * count
    return pl.pallas_call(
        kernel,
        out_shape=(tiles, rest) if blocks == FIRST else tiles,
        in_specs=[hbm] * 4 + ([] if blocks == FIRST else [vmem]),
        scratch_shapes=[
            pltpu.VMEM((2, HERE * count, 8, RG), jnp.bfloat16),
            pltpu.VMEM((HERE, RG), jnp.float32),
            pltpu.VMEM((8 * count, RG), jnp.int32),
            pltpu.VMEM((1152, 128), jnp.float32),
            pltpu.SemaphoreType.DMA((9 * count + 2,)),
            pltpu.VMEM((2, PLANES, rows, 128), jnp.float32),
            pltpu.VMEM((2, PLANES, rows, 128), jnp.float32),
            pltpu.VMEM((2, PLANES, 8, 128), jnp.float32),
            pltpu.VMEM((2, group * rows, 256), jnp.float32),
            pltpu.VMEM((HERE, PLANES, 128), jnp.float32),
            pltpu.VMEM((PLANES + 1, 8 * count, 128), jnp.float32),
            pltpu.VMEM((PLANES + 1, 2 * rows + 2 * HERE, 128), jnp.float32),
            pltpu.VMEM((768, 256), jnp.bfloat16),
            pltpu.VMEM((768, 256), jnp.bfloat16),
            pltpu.VMEM((512, 512), jnp.bfloat16),
        ],
        compiler_params=pltpu.CompilerParams(vmem_limit_bytes=65_700_000),
        cost_estimate=pl.CostEstimate(
            flops=2_000_000_000 * count, bytes_accessed=2_000_000, transcendentals=0
        ),
    )(stack, gains, mask, tables(), *(() if kept is None else (kept,)))


def unpacker(fields):
    z_re, z_im, z_sum, z_dif = fields
    rows = lax.broadcasted_iota(jnp.int32, (8, 128), 0)
    low = rows < 4

    def put(plane, group, first, second):
        re = jnp.where(low, first, pltpu.roll(second, 4, 0))
        im = jnp.where(low, pltpu.roll(first, 4, 0), second)
        total, change = re + im, im - re
        z_im[plane, 8 * group : 8 * group + 8] = im
        for begin in [8 * group] + ([32 + 8 * group] if group < 2 else []):
            z_re[plane, begin : begin + 8] = re
            z_sum[plane, begin : begin + 8] = total
            z_dif[plane, begin : begin + 8] = change

    def run(ref, slot, line, count):
        def step(i, carry):
            for group in range(4):
                first = ref[2 * group, slot + i].astype(jnp.float32)
                second = ref[2 * group + 1, slot + i].astype(jnp.float32)
                for p in range(4):
                    cut = slice(8 * p, 8 * p + 8)
                    put((line + i) * 4 + p, group, first[cut], second[cut])
            return carry

        lax.fori_loop(0, count, step, 0)

    return put, run


WIDTH = 8


def gram(fields, base, count, store):
    z_re, z_im, z_sum, z_dif = fields

    def block(index, carry):
        group = index // 2
        own = pl.ds(pl.multiple_of(group * 8, 8), 8)
        begin = pl.multiple_of(group * 8 + lax.rem(index, 2) * 8, 8)
        unit = min(8, count)

        def some(chunk, totals):
            totals = [list(totals[3 * i : 3 * i + 3]) for i in range(WIDTH)]
            for step in range(0, unit, 2):
                pair = [base + chunk * unit + step + q for q in range(2)]
                mine = [(z_sum[p, own], z_re[p, own], z_im[p, own]) for p in pair]
                for i in range(WIDTH):
                    other = pl.ds(begin + 1 + i, 8)
                    for k, ref in enumerate((z_re, z_sum, z_dif)):
                        terms = [ref[p, other] * part[k] for p, part in zip(pair, mine)]
                        totals[i][k] = totals[i][k] + (terms[0] + terms[1])
            return tuple(t for total in totals for t in total)

        zero = jnp.zeros((8, 128), jnp.float32)
        totals = lax.fori_loop(0, count // unit, some, (zero,) * (3 * WIDTH))
        totals = [totals[3 * i : 3 * i + 3] for i in range(WIDTH)]
        for i in range(WIDTH):
            one, two, three = totals[i]
            spot = (lax.rem(index, 2) * 8 + 1 + i) * DATES + group * 8
            spot = pl.ds(pl.multiple_of(spot, 8), 8)
            store(0, spot, one + three)
            store(1, spot, one - two)
        return carry

    lax.fori_loop(0, 8, block, 0)
    for group in range(4):
        own = slice(8 * group, 8 * group + 8)
        total = None
        for step in range(count):
            re, im = z_re[base + step, own], z_im[base + step, own]
            term = re * re + im * im
            total = term if total is None else total + term
        store(0, own, total)


def gram_rows(fields, sums, count, first_plane, first_row):
    def one_row(r, carry):
        def store(c, spot, value):
            sums[first_row + r, c, spot] = value

        gram(fields, first_plane + r * 16, 16, store)
        return carry

    lax.fori_loop(0, count, one_row, 0)


def early_kernel(own, sums, *fields):
    _, run = unpacker(fields)
    run(own, 2, 0, 4)
    run(own, 7, 4, 4)
    gram_rows(fields, sums, 2, 0, 0)


def inner_kernel(rest, sums, *fields):
    _, run = unpacker(fields)
    run(rest, 0, 0, 12)
    gram_rows(fields, sums, 3, 0, 0)


def upper_kernel(own, above, sums, *fields):
    _, run = unpacker(fields)
    run(above, 1, 0, 6)
    run(own, 0, 6, 2)
    gram_rows(fields, sums, 2, 0, 0)


def own_rows(kernel, count, *chunks):
    field = pltpu.VMEM((count * 16, WRAP, 128), jnp.float32)
    return pl.pallas_call(
        kernel,
        out_shape=jax.ShapeDtypeStruct((count, 2, PAIRS, 128), jnp.float32),
        scratch_shapes=[field] * 4,
        compiler_params=pltpu.CompilerParams(vmem_limit_bytes=(4 + 3 * count) << 20),
        cost_estimate=pl.CostEstimate(
            flops=3_000_000_000 * count, bytes_accessed=2_000_000, transcendentals=0
        ),
    )(*chunks)


def link_kernel(
    own, rest, above, below, upper, early, inner, near, band, out,
    z_re, z_im, z_sum, z_dif, sums, tails, extra, cov, vec,
):
    fields = (z_re, z_im, z_sum, z_dif)
    lanes = lax.broadcasted_iota(jnp.int32, (8, 128), 1)
    put, run = unpacker(fields)
    run(own, 11, 0, 2)
    run(below, 0, 2, 6)
    for group in range(4):
        pieces = []
        for source in (2 * group, 2 * group + 1):
            mine = own[source, EARLY_TAIL].astype(jnp.float32)
            others = rest[source, LATE_TAIL].astype(jnp.float32)
            up = above[source, 0].astype(jnp.float32)
            down = below[source, 6].astype(jnp.float32)
            piece = []
            for p in range(4):
                cut = slice(8 * p, 8 * p + 8)
                value = jnp.zeros((8, 128), jnp.float32)
                for part, turn, begin in (
                    (up, 128 - 30, 0),
                    (mine, 18, 18),
                    (others, 42, 42),
                    (mine, 42, 66),
                    (down, 90, 90),
                ):
                    value = jnp.where(lanes >= begin, pltpu.roll(part[cut], turn, 1), value)
                piece.append(jnp.where(lanes < 108, value, 0.0))
            pieces.append(piece)
        for p in range(4):
            put(32 + p, group, pieces[0][p], pieces[1][p])

    def store_tail(c, spot, value):
        tails[c, spot] = value

    gram(fields, 32, 4, store_tail)
    tails[1, 0:DATES] = jnp.zeros((DATES, 128), jnp.float32)
    gram_rows(fields, sums, 2, 0, 0)
    for c in range(2):
        high, low = split(tails[c])
        extra[c] = jnp.dot(
            jnp.concatenate([high, low], axis=1), band[...], preferred_element_type=jnp.float32
        )

    def windows(step, carry):
        size = 2 * DATES
        begin = pl.multiple_of(step * size, size)
        spot = pl.ds(begin, size)
        twice = pl.multiple_of(step * 2 * size, 2 * size)
        for c in range(2):
            rowsum = [upper[r, c, spot] for r in (0, 1)]
            rowsum += [early[0, c, spot]] + [inner[r, c, spot] for r in range(3)]
            rowsum += [early[1, c, spot]]
            rowsum += [sums[r, c, spot] for r in (0, 1)]
            pairs = [rowsum[r] + rowsum[r + 1] for r in range(8)]
            value = jnp.concatenate([pairs[a] + pairs[a + 2] for a in range(6)], axis=0)
            found = jnp.dot(
                value.astype(jnp.bfloat16), near[...], preferred_element_type=jnp.float32
            )
            for a in range(6):
                full = found[a * size : (a + 1) * size] + extra[c, spot, a * 128 : a * 128 + 128]
                for i in range(2):
                    half = full[i * DATES : (i + 1) * DATES]
                    cov[a, c, pl.ds(twice + 2 * i * DATES, DATES)] = half
                    cov[a, c, pl.ds(twice + (2 * i + 1) * DATES, DATES)] = half
        return carry

    lax.fori_loop(0, (SHIFTS + 1) // 2, windows, 0)

    def put_vec(c, group, value):
        for copy in range(3):
            vec[c, copy * DATES + group * 8 : copy * DATES + group * 8 + 8] = value

    def window_row(a, carry):
        weights = []
        for group in range(4):
            power = cov[a, 0, 8 * group : 8 * group + 8]
            weights.append(1.0 / jnp.sqrt(power + BETA_LOAD))
            put_vec(0, group, weights[group])

        def iterate(real, last):
            sums = [[None, None] for _ in range(4)]
            for s in range(SHIFTS):
                for group in range(4):
                    row = 8 * group
                    re_parts, im_parts = [], []
                    terms = [(2 * s * DATES + row, DATES + row + s, 1)]
                    if 0 < s < SHIFTS - 1:
                        terms.append((2 * s * DATES + DATES + row - s, DATES + row - s, -1))
                    for place, other, sign in terms:
                        cov_re = cov[a, 0, place : place + 8]
                        x_re = vec[0, other : other + 8]
                        x_im = None if real else vec[1, other : other + 8]
                        if s == 0:
                            re = cov_re * x_re
                            im = None if real else cov_re * x_im
                        else:
                            cov_im = cov[a, 1, place : place + 8]
                            re = cov_re * x_re
                            im = cov_im * x_re
                            if sign < 0:
                                im = -im if real else cov_re * x_im - im
                                re = re if real else re + cov_im * x_im
                            elif not real:
                                re = re - cov_im * x_im
                                im = im + cov_re * x_im
                        re_parts.append(re)
                        if im is not None:
                            im_parts.append(im)
                    for k, parts in enumerate((re_parts, im_parts)):
                        if parts:
                            part = parts[0] if len(parts) == 1 else parts[0] + parts[1]
                            sums[group][k] = part if sums[group][k] is None else sums[group][k] + part
            found = sums
            for group in range(4):
                u_re = found[group][0] * weights[group]
                u_im = found[group][1] * weights[group]
                length = 1.0 / jnp.sqrt(u_re * u_re + u_im * u_im + PROJ_LOAD)
                x_re, x_im = u_re * length, u_im * length
                if last:
                    out[0, a, 8 * group : 8 * group + 8] = x_re
                    out[1, a, 8 * group : 8 * group + 8] = x_im
                else:
                    put_vec(0, group, x_re * weights[group])
                    put_vec(1, group, x_im * weights[group])

        iterate(True, False)
        for _ in range(ITERS - 2):
            iterate(False, False)
        iterate(False, True)
        return carry

    lax.fori_loop(0, 6, window_row, 0)


def tail_band():
    near = np.zeros((128, 128), np.float32)
    for block in range(128):
        near[block, max(block - 3, 0) : block + 1] = 1.0
    band = np.zeros((6, 128, 128), np.float32)
    for row in range(6):
        for line in range(4 * row, 4 * row + 16):
            for block in range(3):
                band[row, line * 3 + block, 125 + block :] = 1.0
    both = np.concatenate(list(band), axis=1)
    both = np.concatenate([both, both], axis=0).astype(jnp.bfloat16)
    return near.astype(jnp.bfloat16), both


def link_windows(own, rest, above, below, upper, early, inner):
    field = pltpu.VMEM((36, WRAP, 128), jnp.float32)
    found = pl.pallas_call(
        link_kernel,
        out_shape=jax.ShapeDtypeStruct((2, 6, DATES, 128), jnp.float32),
        scratch_shapes=[field] * 4
        + [
            pltpu.VMEM((2, 2, PAIRS, 128), jnp.float32),
            pltpu.VMEM((2, PAIRS, 128), jnp.float32),
            pltpu.VMEM((2, PAIRS, 6 * 128), jnp.float32),
            pltpu.VMEM((6, 2, 2 * PAIRS, 128), jnp.float32),
            pltpu.VMEM((2, 3 * DATES, 128), jnp.float32),
        ],
        compiler_params=pltpu.CompilerParams(vmem_limit_bytes=28 << 20),
        cost_estimate=pl.CostEstimate(
            flops=20_000_000_000, bytes_accessed=8_000_000, transcendentals=0
        ),
        name="link_windows",
    )(own, rest, above, below, upper, early, inner, *tail_band())
    return jnp.transpose(found, (0, 2, 1, 3))


def on_device(stack, range_filter, scatter_mask):
    def move(tiles):
        return lax.all_to_all(tiles, "dr", split_axis=0, concat_axis=0, tiled=True)

    tiles, kept = filter_lines(stack, range_filter, scatter_mask, FIRST, GROUP_FIRST)
    own = move(tiles)
    tiles = filter_lines(stack, range_filter, scatter_mask, SECOND, GROUP_SECOND, kept)
    rest = move(tiles)
    count = lax.axis_size("az")
    down = [(i, i + 1) for i in range(count - 1)]
    up = [(i + 1, i) for i in range(count - 1)]
    above = lax.ppermute(own[:, 6:13], "az", down)
    below = lax.ppermute(own[:, 0:7], "az", up)
    early = own_rows(early_kernel, 2, own)
    inner = own_rows(inner_kernel, 3, rest)
    upper = own_rows(upper_kernel, 2, own, above)
    return link_windows(own, rest, above, below, upper, early, inner)


def solution(mesh):
    in_specs = (P(None, "dr", "az", None), P("dr", None), P("az", None))
    out_specs = P(None, None, "az", "dr")
    return jax.shard_map(
        on_device, mesh=mesh, in_specs=in_specs, out_specs=out_specs, check_vma=False
    )
```
